32 devices in a mesh: node: 16 (over z, y, x), head: 2 (over core).
Axes of the slice: x: 2, y: 2, z: 4, core: 2. Of those that a mesh axis runs over, the one named last changes fastest.
Arguments:
- inputs: bfloat16 [8192, 8192], P('node', 'head'), may hold values from -6 to 6
- b_matrix: bfloat16 [8192, 128], P('node'), may hold values from -0.5390625 to 0.5390625
- c_matrix: bfloat16 [8192, 128], P('node'), may hold values from -0.5390625 to 0.5390625
- step_size: float32 [128, 8192], P('head', 'node'), may hold values from 0 to 4, as said below
- decay_rate: float32 [128], P('head'), may hold values from 0 to 1, as said below
- parents: int32 [16], replicated, may hold values from -1 to 15, as said below
- cotangent: bfloat16 [8192, 8192], P('node', 'head'), may hold values from -0.59765625 to 0.59765625
Outputs:
- outputs: bfloat16 [8192, 8192], P('node', 'head')
- grad_inputs: bfloat16 [8192, 8192], P('node', 'head')
- grad_b: float32 [8192, 128], P(('node', 'head'))
- grad_c: float32 [8192, 128], P(('node', 'head'))
The draws below stay inside these ranges and needn't reach their ends.
Inputs may be any that keep to these rules, and one draw needn't show every extreme that they name: parents[n] is -1 for a root or the index of another node; following parents from any node reaches a root within 3 steps, and some node is exactly 3 steps from its root. `step_size`: positive. `decay_rate`: positive.
All inputs are finite; a program needn't handle non-finite values.
Results may differ from the reference program's by a relative error of at most 0.019.
Values may be sent and summed in bfloat16 or wider, within the bound.
No kernel may reach another device: no remote copies, remote signals or barrier semaphores. Data moves between devices by JAX's collectives and lax.ppermute only.
A program may use at most 128 MiB of HBM per device.

```python
import math
import jax
import jax.numpy as jnp
from jax import lax

HEADS = 128
HEAD_DIM = 64
STATE = 128
LEN = 512
LEVELS = 3
NODES = 16
TOKENS = 8192


def draw_parents(key, part):
    shuffled = jax.random.permutation(jax.random.fold_in(key, 101), NODES)
    bound_one = max(1, NODES // 8)
    bound_two = bound_one + NODES // 4
    bound_three = bound_two + NODES // 4
    positions = jnp.arange(NODES)
    depth_level = (positions >= bound_one).astype(jnp.int32) + (positions >= bound_two).astype(jnp.int32) + (positions >= bound_three).astype(jnp.int32)
    low_bounds = jnp.array([0, 0, bound_one, bound_two], jnp.int32)
    high_bounds = jnp.array([1, bound_one, bound_two, bound_three], jnp.int32)
    picked = jax.random.randint(jax.random.fold_in(key, 102), (NODES,), low_bounds[depth_level], high_bounds[depth_level])
    parent_node = jnp.where(depth_level > 0, shuffled[picked], -1).astype(jnp.int32)
    return jnp.zeros((NODES,), jnp.int32).at[shuffled].set(parent_node)


def draw_step_size(key, part):
    base_key = jax.random.fold_in(key, 201)
    node_key = jax.random.fold_in(key, 202)
    base_values = jnp.exp(jax.random.uniform(base_key, (HEADS, TOKENS), jnp.float32, math.log(0.5), math.log(2.0)))
    node_scale = jnp.exp(jax.random.uniform(node_key, (1, NODES, 1), jnp.float32, math.log(0.5), math.log(2.0)))
    return (base_values.reshape(HEADS, NODES, LEN) * node_scale).reshape(HEADS, TOKENS)


def draw_decay_rate(key, part):
    slow_share = 0.5
    slow_flag = jax.random.uniform(jax.random.fold_in(key, 301), (HEADS,), jnp.float32) < slow_share
    slow_rate = jnp.exp(jax.random.uniform(jax.random.fold_in(key, 302), (HEADS,), jnp.float32, math.log(0.05), math.log(0.3))) / LEN
    fast_rate = jnp.exp(jax.random.uniform(jax.random.fold_in(key, 303), (HEADS,), jnp.float32, math.log(0.02), math.log(0.1)))
    return jnp.where(slow_flag, slow_rate, fast_rate)


def levels(stream_key, extent, cuts, least, largest):
    def one(axis_at, blocks):
        steps = jax.random.uniform(jax.random.fold_in(jax.random.fold_in(stream_key, 6), axis_at), (blocks,), jnp.float32, least / len(cuts), largest / len(cuts))
        return jnp.repeat(jnp.exp(steps), extent[axis_at] // blocks).reshape((-1,) + (1,) * (len(extent) - axis_at - 1))

    loudness = one(*cuts[0])
    for cut in cuts[1:]:
        loudness = loudness * one(*cut)
    return loudness


def gaussian(own_key, extent, width, bound, cuts=(), dtype=jnp.bfloat16):
    values = width * jax.random.normal(own_key, extent, jnp.float32)
    if cuts:
        values = values * levels(own_key, extent, cuts, -0.22, 0.18)
    return jnp.clip(values, -bound, bound).astype(dtype)


def setup_inputs(seed: int = 0) -> dict:
    streams_of = jax.random.split(jax.random.key(seed), 8)
    return {
        "inputs": gaussian(streams_of[0], (TOKENS, HEADS * HEAD_DIM), 1.0, 6.0, ((0, 16), (1, 2))),
        "b_matrix": gaussian(streams_of[1], (TOKENS, STATE), 0.09, 0.5390625, ((0, 16),)),
        "c_matrix": gaussian(streams_of[2], (TOKENS, STATE), 0.09, 0.5390625, ((0, 16),)),
        "step_size": draw_step_size(jax.random.fold_in(streams_of[7], 71), 0),
        "decay_rate": draw_decay_rate(jax.random.fold_in(streams_of[7], 71), 0),
        "parents": draw_parents(jax.random.fold_in(streams_of[7], 71), 0),
        "cotangent": gaussian(streams_of[6], (TOKENS, HEADS * HEAD_DIM), 0.1, 0.59765625, ((0, 16), (1, 2))),
    }


highest = lax.Precision.HIGHEST


def local_terms(inputs, b_matrix, c_matrix, step_size, decay_rate, cotangent):
    length = b_matrix.shape[0]
    x_heads = inputs.reshape(length, HEADS, HEAD_DIM)
    cot_heads = cotangent.reshape(length, HEADS, HEAD_DIM)
    cumulative = jnp.cumsum(-step_size * decay_rate[:, None], axis=1)
    last_value = cumulative[:, -1]
    growth = jnp.exp(cumulative)
    tail_decay = jnp.exp(last_value[:, None] - cumulative)
    scaled = (step_size.T[:, :, None] * x_heads.astype(jnp.float32)).astype(jnp.bfloat16)
    tailed = (tail_decay.T[:, :, None] * scaled.astype(jnp.float32)).astype(jnp.bfloat16)
    emitted = (growth.T[:, :, None] * cot_heads.astype(jnp.float32)).astype(jnp.bfloat16)
    gram_matrix = jnp.dot(c_matrix, b_matrix.T, preferred_element_type=jnp.float32)
    positions = jnp.arange(length)
    causal = positions[:, None] >= positions[None, :]
    differ = cumulative[:, :, None] - cumulative[:, None, :]
    decay_mask = jnp.where(causal[None], jnp.exp(jnp.where(causal[None], differ, 0.0)), 0.0)
    weights = (decay_mask * gram_matrix[None]).astype(jnp.bfloat16)
    decay_total = jnp.exp(last_value)
    return cot_heads, growth, tail_decay, scaled, tailed, emitted, decay_mask, weights, decay_total


def reference(inputs, b_matrix, c_matrix, step_size, decay_rate, parents, cotangent):
    node_inputs = inputs.reshape(NODES, LEN, HEADS * HEAD_DIM)
    node_b = b_matrix.reshape(NODES, LEN, STATE)
    node_c = c_matrix.reshape(NODES, LEN, STATE)
    node_steps = step_size.reshape(HEADS, NODES, LEN).transpose(1, 0, 2)
    node_cot = cotangent.reshape(NODES, LEN, HEADS * HEAD_DIM)

    def first_pass(pieces):
        x_node, b_node, c_node, s_node, cot_node = pieces
        found = local_terms(x_node, b_node, c_node, s_node, decay_rate, cot_node)
        tailed = found[4]
        emitted = found[5]
        state_local = jnp.einsum("shp,sn->hpn", tailed.astype(jnp.float32), b_node.astype(jnp.float32))
        seed_grad = jnp.einsum("thp,tn->hpn", emitted.astype(jnp.float32), c_node.astype(jnp.float32))
        return state_local, seed_grad, found[8]

    states, seeds, decays = lax.map(first_pass, (node_inputs, node_b, node_c, node_steps, node_cot))
    linked = (parents[:, None] == jnp.arange(NODES)[None, :]).astype(jnp.float32)
    flat_state = states.reshape(NODES, HEADS, HEAD_DIM * STATE)
    flat_seed = seeds.reshape(NODES, HEADS, HEAD_DIM * STATE)
    node_decay = decays[:, :, None]
    start_state = jnp.zeros((NODES, HEADS, HEAD_DIM * STATE), jnp.float32)
    back_state = jnp.zeros((NODES, HEADS, HEAD_DIM * STATE), jnp.float32)
    for turn_index in range(LEVELS):
        final_state = node_decay * start_state + flat_state
        start_state = jnp.einsum("nm,mhk->nhk", linked, final_state, precision=highest)
        grad_state = flat_seed + node_decay * back_state
        back_state = jnp.einsum("mn,mhk->nhk", linked, grad_state, precision=highest)
    start_low = start_state.reshape(NODES, HEADS, HEAD_DIM, STATE).astype(jnp.bfloat16)
    back_low = back_state.reshape(NODES, HEADS, HEAD_DIM, STATE).astype(jnp.bfloat16)

    def second_pass(pieces):
        x_node, b_node, c_node, s_node, cot_node, start_node, back_node = pieces
        found = local_terms(x_node, b_node, c_node, s_node, decay_rate, cot_node)
        cot_heads, growth, tail_decay, scaled, tailed, emitted, decay_mask, weights, decay_total = found
        b_wide = b_node.astype(jnp.float32)
        c_wide = c_node.astype(jnp.float32)
        start_wide = start_node.astype(jnp.float32)
        back_wide = back_node.astype(jnp.float32)
        intra_part = jnp.einsum("hts,shp->thp", weights.astype(jnp.float32), scaled.astype(jnp.float32))
        carried = jnp.einsum("tn,hpn->thp", c_wide, start_wide)
        outputs = (intra_part + growth.T[:, :, None] * carried).astype(jnp.bfloat16)
        grad_scores = jnp.einsum("thp,shp->hts", cot_heads.astype(jnp.float32), scaled.astype(jnp.float32))
        mixed_scores = (decay_mask * grad_scores).astype(jnp.bfloat16).astype(jnp.float32)
        grad_scaled = jnp.einsum("hts,thp->shp", weights.astype(jnp.float32), cot_heads.astype(jnp.float32))
        grad_scaled = grad_scaled + tail_decay.T[:, :, None] * jnp.einsum("sn,hpn->shp", b_wide, back_wide)
        grad_inputs = (s_node.T[:, :, None] * grad_scaled).astype(jnp.bfloat16)
        grad_c = jnp.einsum("hts,sn->tn", mixed_scores, b_wide) + jnp.einsum("thp,hpn->tn", emitted.astype(jnp.float32), start_wide)
        grad_b = jnp.einsum("hts,tn->sn", mixed_scores, c_wide) + jnp.einsum("shp,hpn->sn", tailed.astype(jnp.float32), back_wide)
        return outputs.reshape(LEN, HEADS * HEAD_DIM), grad_inputs.reshape(LEN, HEADS * HEAD_DIM), grad_b, grad_c

    outputs, grad_inputs, grad_b, grad_c = lax.map(second_pass, (node_inputs, node_b, node_c, node_steps, node_cot, start_low, back_low))
    return (outputs.reshape(TOKENS, HEADS * HEAD_DIM), grad_inputs.reshape(TOKENS, HEADS * HEAD_DIM), grad_b.reshape(TOKENS, STATE), grad_c.reshape(TOKENS, STATE))
```

```python
import functools
import math

import jax
import jax.numpy as jnp
from jax import lax
from jax.experimental import pallas as pl
from jax.experimental.pallas import tpu as pltpu
from jax.sharding import PartitionSpec as P

LEVELS = 3
LANES = 128
CHUNKS = 2

f32 = jnp.float32
bf16 = jnp.bfloat16
NN = (((1,), (0,)), ((), ()))
NT = (((1,), (1,)), ((), ()))


def mm(a, b, dims=NN):
    return lax.dot_general(a, b, dims, preferred_element_type=f32)


def split_two(v):
    high = v.astype(bf16)
    return high, (v - high.astype(f32)).astype(bf16)


def spread_matrix(rows, heads, width, head_width, offset):
    row = lax.broadcasted_iota(jnp.int32, (rows, width), 0) % heads
    lane = (lax.broadcasted_iota(jnp.int32, (rows, width), 1) + offset) // head_width
    return (row == lane).astype(bf16)


def states_kernel(
    heads,
    head_width,
    x_ref,
    cot_ref,
    b_ref,
    c_ref,
    step_ref,
    rate_ref,
    send_ref,
    low_ref,
    src_ref,
    grow_ref,
    tail_ref,
    bt_ref,
    ct_ref,
):
    block = x_ref.shape[1]
    length = step_ref.shape[1]
    index = pl.program_id(0)
    width = heads * head_width

    @pl.when(index == 0)
    def _():
        step = step_ref[...]
        terms = -step * rate_ref[...]
        row = lax.broadcasted_iota(jnp.int32, (length, length), 0)
        col = lax.broadcasted_iota(jnp.int32, (length, length), 1)
        upper = (row <= col).astype(bf16)
        first = terms.astype(bf16)
        rest = terms - first.astype(f32)
        second, third = split_two(rest)
        cumulative = mm(third, upper) + mm(second, upper) + mm(first, upper)
        last = cumulative[:, length - 1 :]
        low_ref[...] = cumulative
        src_ref[...] = cumulative - jnp.log(step)
        growth = jnp.exp(cumulative)
        tail = jnp.exp(last - cumulative) * step
        grow_ref[...] = jnp.concatenate(split_two(growth.T), axis=1)
        tail_ref[...] = jnp.concatenate(split_two(tail.T), axis=1)
        bt_ref[...] = b_ref[...].T
        ct_ref[...] = c_ref[...].T
        total = jnp.exp(jnp.broadcast_to(last, (heads, send_ref.shape[0])))
        pad = jnp.zeros((LANES - heads, send_ref.shape[0]), f32)
        totals = jnp.concatenate([total, pad], axis=0).T
        send_ref[:, 2 * width :] = totals.astype(bf16)

    spread = spread_matrix(2 * heads, heads, block, head_width, index * block)
    tail_wide = mm(tail_ref[...], spread)
    grow_wide = mm(grow_ref[...], spread)
    tailed = (tail_wide * x_ref[...].astype(f32)).astype(bf16)
    emitted = (grow_wide * cot_ref[...].astype(f32)).astype(bf16)
    at = pl.multiple_of(index * block, block)
    send_ref[:, pl.ds(at, block)] = mm(bt_ref[...], tailed).astype(bf16)
    send_ref[:, pl.ds(at + width, block)] = mm(ct_ref[...], emitted).astype(bf16)


def node_states(x, cot, b, c, step, rate, chunk, heads, head_width):
    length, state = b.shape
    width = heads * head_width
    block = min(width, 4 * LANES)
    count = width // block
    whole = lambda i: (0, 0)
    return pl.pallas_call(
        functools.partial(states_kernel, heads, head_width),
        grid=(count,),
        in_specs=[
            pl.BlockSpec((length, block), lambda i: (0, chunk * count + i)),
            pl.BlockSpec((length, block), lambda i: (0, chunk * count + i)),
            pl.BlockSpec((length, state), whole),
            pl.BlockSpec((length, state), whole),
            pl.BlockSpec((heads, length), lambda i: (chunk, 0)),
            pl.BlockSpec((heads, 1), lambda i: (chunk, 0)),
        ],
        out_specs=[
            pl.BlockSpec((state, 2 * width + LANES), whole),
            pl.BlockSpec((heads, length), whole),
            pl.BlockSpec((heads, length), whole),
            pl.BlockSpec((length, 2 * heads), whole),
            pl.BlockSpec((length, 2 * heads), whole),
        ],
        out_shape=[
            jax.ShapeDtypeStruct((state, 2 * width + LANES), bf16),
            jax.ShapeDtypeStruct((heads, length), f32),
            jax.ShapeDtypeStruct((heads, length), f32),
            jax.ShapeDtypeStruct((length, 2 * heads), bf16),
            jax.ShapeDtypeStruct((length, 2 * heads), bf16),
        ],
        scratch_shapes=[pltpu.VMEM((state, length), bf16), pltpu.VMEM((state, length), bf16)],
        name="node_states",
        cost_estimate=pl.CostEstimate(
            flops=4 * length * state * width,
            bytes_accessed=4 * length * width + 4 * state * width,
            transcendentals=0,
        ),
    )(x, cot, b, c, step, rate)


def inner_kernel(
    heads,
    head_width,
    x_ref,
    cot_ref,
    b_ref,
    c_ref,
    low_ref,
    src_ref,
    out_ref,
    grad_ref,
    gc_ref,
    gb_ref,
    gram_ref,
    mixed_ref,
    wa_ref,
    wb_ref,
):
    length = x_ref.shape[0]
    index = pl.program_id(0)
    pack = LANES // head_width
    blocks = length // LANES
    half = length // 2
    weights = (wa_ref, wb_ref)

    @pl.when(index == 0)
    def _():
        gram_ref[...] = mm(c_ref[...], b_ref[...], NT)
        mixed_ref[...] = jnp.zeros_like(mixed_ref)
        for ref in weights:
            ref[...] = jnp.zeros_like(ref)

    lane = lax.broadcasted_iota(jnp.int32, (1, LANES), 1) // head_width
    causal = lax.broadcasted_iota(jnp.int32, (LANES, LANES), 0) >= lax.broadcasted_iota(
        jnp.int32, (LANES, LANES), 1
    )
    x = x_ref[...]
    cot = cot_ref[...]
    cots = [jnp.where(lane == a, cot, jnp.zeros_like(cot)) for a in range(pack)]
    columns = [
        jnp.broadcast_to(low_ref[pl.ds(index * pack + a, 1), :], (LANES, length)).T
        for a in range(pack)
    ]
    sources = [src_ref[pl.ds(index * pack + a, 1), :] for a in range(pack)]
    for i in range(blocks):
        rows = slice(i * LANES, (i + 1) * LANES)
        until = (i + 1) * LANES
        scores = [mm(cots[a][rows], x[:until], NT) for a in range(pack)]
        for j in range(i + 1):
            cols = slice(j * LANES, (j + 1) * LANES)
            gram = gram_ref[rows, cols]
            mixed = mixed_ref[rows, cols]
            for a in range(pack):
                differ = columns[a][rows] - sources[a][:, cols]
                if i == j:
                    differ = jnp.where(causal, differ, -jnp.inf)
                decay = jnp.exp(differ)
                weights[a][rows, cols] = (decay * gram).astype(bf16)
                mixed = mixed + decay * scores[a][:, cols]
            mixed_ref[rows, cols] = mixed
    cot_turned = cot.T
    turned = []
    for a in range(pack):
        w = weights[a]
        top = mm(w[:half, :half], x[:half])
        bottom = mm(w[half:, :], x)
        both = jnp.concatenate([top, bottom], axis=0)
        out = both if a == 0 else jnp.where(lane == a, both, out)
        part = cot_turned[a * head_width : (a + 1) * head_width]
        left = mm(part, w[:, :half])
        right = mm(part[:, half:], w[half:, half:])
        turned.append(jnp.concatenate([left, right], axis=1))
    out_ref[...] = out.astype(out_ref.dtype)
    grad_ref[...] = jnp.concatenate(turned, axis=0).T.astype(grad_ref.dtype)

    @pl.when(index == pl.num_programs(0) - 1)
    def _():
        high, low = split_two(mixed_ref[...])
        gc_ref[...] = mm(high, b_ref[...]) + mm(low, b_ref[...])
        high, low = split_two(mixed_ref[...].T)
        gb_ref[...] = mm(high, c_ref[...]) + mm(low, c_ref[...])


def node_inner(x, cot, b, c, low, src, chunk, heads, head_width):
    length, state = b.shape
    width = heads * head_width
    count = width // LANES
    whole = lambda i: (0, 0)
    spot = lambda i: (0, i)
    return pl.pallas_call(
        functools.partial(inner_kernel, heads, head_width),
        grid=(count,),
        in_specs=[
            pl.BlockSpec((length, LANES), lambda i: (0, chunk * count + i)),
            pl.BlockSpec((length, LANES), lambda i: (0, chunk * count + i)),
            pl.BlockSpec((length, state), whole),
            pl.BlockSpec((length, state), whole),
            pl.BlockSpec((heads, length), whole),
            pl.BlockSpec((heads, length), whole),
        ],
        out_specs=[
            pl.BlockSpec((length, LANES), spot),
            pl.BlockSpec((length, LANES), spot),
            pl.BlockSpec((length, state), whole),
            pl.BlockSpec((length, state), whole),
        ],
        out_shape=[
            jax.ShapeDtypeStruct((length, width), f32),
            jax.ShapeDtypeStruct((length, width), f32),
            jax.ShapeDtypeStruct((length, state), f32),
            jax.ShapeDtypeStruct((length, state), f32),
        ],
        scratch_shapes=[
            pltpu.VMEM((length, length), f32),
            pltpu.VMEM((length, length), f32),
            pltpu.VMEM((length, length), bf16),
            pltpu.VMEM((length, length), bf16),
        ],
        name="node_inner",
        cost_estimate=pl.CostEstimate(
            flops=24 * length * length * width,
            bytes_accessed=12 * length * width,
            transcendentals=length * length * heads,
        ),
    )(x, cot, b, c, low, src)


def tree_kernel(heads, head_width, parents_ref, recv_ref, out_ref, decay_ref, back_ref):
    nodes, rows = recv_ref.shape[:2]
    width = heads * head_width
    totals = recv_ref[:, :, 2 * width :].astype(f32).reshape(nodes * rows, LANES).astype(bf16)
    spread = spread_matrix(LANES, LANES, width, head_width, 0)
    decay_ref[...] = mm(totals, spread).reshape(nodes, rows, width)
    back_ref[...] = jnp.zeros_like(back_ref)

    def visit(n, carry):
        seed = recv_ref[n, :, width : 2 * width].astype(f32)
        start = jnp.zeros((rows, width), f32)
        factor = jnp.ones((rows, width), f32)
        at = n
        valid = jnp.bool_(True)
        for level in range(LEVELS):
            up = parents_ref[at]
            valid = jnp.logical_and(valid, up >= 0)
            at = jnp.maximum(up, 0)
            keep = jnp.where(valid, f32(1), f32(0))
            factor = factor * keep
            start = start + factor * recv_ref[at, :, :width].astype(f32)
            back_ref[at] = back_ref[at] + factor * seed
            if level < LEVELS - 1:
                factor = factor * decay_ref[at]
        out_ref[n, :, :width] = start.astype(bf16)
        return carry

    lax.fori_loop(0, nodes, visit, 0)
    out_ref[:, :, width:] = back_ref[...].astype(bf16)


def combine(parents, recv, heads, head_width):
    nodes, rows, _ = recv.shape
    width = heads * head_width
    return pl.pallas_call(
        functools.partial(tree_kernel, heads, head_width),
        in_specs=[
            pl.BlockSpec(memory_space=pltpu.SMEM),
            pl.BlockSpec(memory_space=pltpu.VMEM),
        ],
        out_specs=pl.BlockSpec(memory_space=pltpu.VMEM),
        out_shape=jax.ShapeDtypeStruct((nodes, rows, 2 * width), bf16),
        scratch_shapes=[
            pltpu.VMEM((nodes, rows, width), f32),
            pltpu.VMEM((nodes, rows, width), f32),
        ],
        name="tree_combine",
        cost_estimate=pl.CostEstimate(
            flops=20 * nodes * rows * width,
            bytes_accessed=8 * nodes * rows * width,
            transcendentals=0,
        ),
    )(parents, recv)


def outer_kernel(
    heads,
    head_width,
    aliased,
    x_ref,
    cot_ref,
    b_ref,
    c_ref,
    grow_ref,
    tail_ref,
    start_ref,
    back_ref,
    inner_ref,
    grad_ref,
    *refs,
):
    out_ref, gx_ref, gc_ref, gb_ref = refs[2:] if aliased else refs
    block = x_ref.shape[1]
    index = pl.program_id(0)
    spread = spread_matrix(2 * heads, heads, block, head_width, index * block)
    grow_wide = mm(grow_ref[...], spread)
    tail_wide = mm(tail_ref[...], spread)
    start = start_ref[...]
    back = back_ref[...]
    out_ref[...] = (inner_ref[...] + grow_wide * mm(c_ref[...], start)).astype(bf16)
    gx_ref[...] = (grad_ref[...] + tail_wide * mm(b_ref[...], back)).astype(bf16)
    emitted = (grow_wide * cot_ref[...].astype(f32)).astype(bf16)
    tailed = (tail_wide * x_ref[...].astype(f32)).astype(bf16)
    gc = mm(emitted, start, NT)
    gb = mm(tailed, back, NT)

    @pl.when(index == 0)
    def _():
        gc_ref[...] = gc
        gb_ref[...] = gb

    @pl.when(index > 0)
    def _():
        gc_ref[...] += gc
        gb_ref[...] += gb


def node_outer(x, cot, b, c, grow, tail, states, inner, grad, prior, chunk, heads, head_width):
    length, state = b.shape
    width = heads * head_width
    block = min(width, 4 * LANES)
    count = width // block
    whole = lambda i: (0, 0)
    spot = lambda i: (0, i)
    place = lambda i: (0, chunk * count + i)
    aliased = prior is not None
    operands = [x, cot, b, c, grow, tail, states, states, inner, grad]
    in_specs = [
        pl.BlockSpec((length, block), place),
        pl.BlockSpec((length, block), place),
        pl.BlockSpec((length, state), whole),
        pl.BlockSpec((length, state), whole),
        pl.BlockSpec((length, 2 * heads), whole),
        pl.BlockSpec((length, 2 * heads), whole),
        pl.BlockSpec((state, block), spot),
        pl.BlockSpec((state, block), lambda i: (0, count + i)),
        pl.BlockSpec((length, block), spot),
        pl.BlockSpec((length, block), spot),
    ]
    aliases = {}
    if aliased:
        aliases = {len(operands): 0, len(operands) + 1: 1}
        operands += list(prior)
        in_specs += [pl.BlockSpec(memory_space=pl.ANY)] * 2
    return pl.pallas_call(
        functools.partial(outer_kernel, heads, head_width, aliased),
        grid=(count,),
        in_specs=in_specs,
        out_specs=[
            pl.BlockSpec((length, block), place),
            pl.BlockSpec((length, block), place),
            pl.BlockSpec((length, state), whole),
            pl.BlockSpec((length, state), whole),
        ],
        out_shape=[
            jax.ShapeDtypeStruct(x.shape, bf16),
            jax.ShapeDtypeStruct(x.shape, bf16),
            jax.ShapeDtypeStruct((length, state), f32),
            jax.ShapeDtypeStruct((length, state), f32),
        ],
        input_output_aliases=aliases,
        name="node_outer",
        cost_estimate=pl.CostEstimate(
            flops=8 * length * state * width,
            bytes_accessed=16 * length * width,
            transcendentals=0,
        ),
    )(*operands)


def scatter_sum(parts):
    size = lax.axis_size("head")
    me = lax.axis_index("head")
    rows = parts.shape[1] // size
    total = lax.dynamic_slice_in_dim(parts, me * rows, rows, axis=1)
    for shift in range(1, size):
        target = (me + shift) % size
        piece = lax.dynamic_slice_in_dim(parts, target * rows, rows, axis=1).astype(bf16)
        moved = lax.ppermute(piece, "head", [(i, (i + shift) % size) for i in range(size)])
        total = total + moved.astype(f32)
    return total


def on_device(inputs, b_matrix, c_matrix, step_size, decay_rate, parents, cotangent):
    state = b_matrix.shape[1]
    head_count = step_size.shape[0]
    head_width = inputs.shape[1] // head_count
    nodes = lax.axis_size("node")
    heads = head_count // CHUNKS
    rows = state // nodes
    rate = decay_rate[:, None]

    def swap(v):
        moved = lax.all_to_all(
            v.reshape(nodes, rows, v.shape[-1]), "node", split_axis=0, concat_axis=0, tiled=True
        )
        return moved

    chunks = range(CHUNKS)
    made = [
        node_states(
            inputs, cotangent, b_matrix, c_matrix, step_size, rate, k, heads, head_width
        )
        for k in chunks
    ]
    received = [swap(made[k][0]) for k in chunks]
    inner = [
        node_inner(
            inputs, cotangent, b_matrix, c_matrix, made[k][1], made[k][2], k, heads, head_width
        )
        for k in chunks
    ]
    joined = [combine(parents, received[k], heads, head_width) for k in chunks]
    states = [swap(joined[k]).reshape(state, -1) for k in chunks]
    prior = None
    grad_c = sum(inner[k][2] for k in chunks)
    grad_b = sum(inner[k][3] for k in chunks)
    for k in chunks:
        result = node_outer(
            inputs,
            cotangent,
            b_matrix,
            c_matrix,
            made[k][3],
            made[k][4],
            states[k],
            inner[k][0],
            inner[k][1],
            prior,
            k,
            heads,
            head_width,
        )
        prior = result[:2]
        grad_c = grad_c + result[2]
        grad_b = grad_b + result[3]
    grads = scatter_sum(jnp.stack([grad_b, grad_c]))
    return prior[0], prior[1], grads[0], grads[1]


def solution(mesh):
    return jax.shard_map(
        on_device,
        mesh=mesh,
        in_specs=(
            P("node", "head"),
            P("node", None),
            P("node", None),
            P("head", "node"),
            P("head"),
            P(),
            P("node", "head"),
        ),
        out_specs=(
            P("node", "head"),
            P("node", "head"),
            P(("node", "head"), None),
            P(("node", "head"), None),
        ),
        check_vma=False,
    )
```

```python
import functools
import math

import jax
import jax.numpy as jnp
from jax import lax
from jax.experimental import pallas as pl
from jax.experimental.pallas import tpu as pltpu
from jax.sharding import PartitionSpec as P

LEVELS = 3
LANES = 128
CHUNKS = 2
PARTS = 2

f32 = jnp.float32
bf16 = jnp.bfloat16
NN = (((1,), (0,)), ((), ()))
NT = (((1,), (1,)), ((), ()))


def mm(a, b, dims=NN):
    return lax.dot_general(a, b, dims, preferred_element_type=f32)


def ordered(kernel, in_specs, operands, after, aliases=None):
    if after is None:
        return kernel, in_specs, operands, aliases or {}

    def body(after_ref, *refs):
        kernel(*refs)

    shifted = {key + 1: value for key, value in (aliases or {}).items()}
    return body, [pl.BlockSpec(memory_space=pl.ANY)] + in_specs, [after] + operands, shifted


def split_two(v):
    high = v.astype(bf16)
    return high, (v - high.astype(f32)).astype(bf16)


def spread_matrix(rows, heads, width, head_width, offset):
    row = lax.broadcasted_iota(jnp.int32, (rows, width), 0) % heads
    lane = (lax.broadcasted_iota(jnp.int32, (rows, width), 1) + offset) // head_width
    return (row == lane).astype(bf16)


def states_kernel(
    heads,
    head_width,
    chunk,
    x_ref,
    cot_ref,
    b_ref,
    c_ref,
    step_ref,
    rate_ref,
    send_ref,
    low_ref,
    src_ref,
    grow_ref,
    tail_ref,
    bt_ref,
    ct_ref,
):
    block = x_ref.shape[1]
    length = step_ref.shape[1]
    index = pl.program_id(0)
    width = heads * head_width

    @pl.when(index == 0)
    def _():
        step = step_ref[...]
        rates = jnp.broadcast_to(rate_ref[...], (LANES, rate_ref.shape[1])).T
        terms = -step * rates[chunk * heads : (chunk + 1) * heads, :1]
        row = lax.broadcasted_iota(jnp.int32, (length, length), 0)
        col = lax.broadcasted_iota(jnp.int32, (length, length), 1)
        upper = (row <= col).astype(bf16)
        first = terms.astype(bf16)
        rest = terms - first.astype(f32)
        second, third = split_two(rest)
        cumulative = mm(third, upper) + mm(second, upper) + mm(first, upper)
        last = cumulative[:, length - 1 :]
        low_ref[...] = cumulative
        src_ref[...] = cumulative - jnp.log(step)
        growth = jnp.exp(cumulative)
        tail = jnp.exp(last - cumulative) * step
        grow_ref[...] = jnp.concatenate(split_two(growth.T), axis=1)
        tail_ref[...] = jnp.concatenate(split_two(tail.T), axis=1)
        bt_ref[...] = b_ref[...].T
        ct_ref[...] = c_ref[...].T
        total = jnp.exp(jnp.broadcast_to(last, (heads, send_ref.shape[0])))
        pad = jnp.zeros((LANES - heads, send_ref.shape[0]), f32)
        totals = jnp.concatenate([total, pad], axis=0).T
        send_ref[:, 2 * width :] = totals.astype(bf16)

    spread = spread_matrix(2 * heads, heads, block, head_width, index * block)
    tail_wide = mm(tail_ref[...], spread)
    grow_wide = mm(grow_ref[...], spread)
    tailed = (tail_wide * x_ref[...].astype(f32)).astype(bf16)
    emitted = (grow_wide * cot_ref[...].astype(f32)).astype(bf16)
    at = pl.multiple_of(index * block, block)
    send_ref[:, pl.ds(at, block)] = mm(bt_ref[...], tailed).astype(bf16)
    send_ref[:, pl.ds(at + width, block)] = mm(ct_ref[...], emitted).astype(bf16)


def node_states(x, cot, b, c, step, rate, chunk, heads, head_width):
    length, state = b.shape
    width = heads * head_width
    block = min(width, 4 * LANES)
    count = width // block
    whole = lambda i: (0, 0)
    return pl.pallas_call(
        functools.partial(states_kernel, heads, head_width, chunk),
        grid=(count,),
        in_specs=[
            pl.BlockSpec((length, block), lambda i: (0, chunk * count + i)),
            pl.BlockSpec((length, block), lambda i: (0, chunk * count + i)),
            pl.BlockSpec((length, state), whole),
            pl.BlockSpec((length, state), whole),
            pl.BlockSpec((heads, length), lambda i: (chunk, 0)),
            pl.BlockSpec(rate.shape, whole),
        ],
        out_specs=[
            pl.BlockSpec((state, 2 * width + LANES), whole),
            pl.BlockSpec((heads, length), whole),
            pl.BlockSpec((heads, length), whole),
            pl.BlockSpec((length, 2 * heads), whole),
            pl.BlockSpec((length, 2 * heads), whole),
        ],
        out_shape=[
            jax.ShapeDtypeStruct((state, 2 * width + LANES), bf16),
            jax.ShapeDtypeStruct((heads, length), f32),
            jax.ShapeDtypeStruct((heads, length), f32),
            jax.ShapeDtypeStruct((length, 2 * heads), bf16),
            jax.ShapeDtypeStruct((length, 2 * heads), bf16),
        ],
        scratch_shapes=[pltpu.VMEM((state, length), bf16), pltpu.VMEM((state, length), bf16)],
        name="node_states",
        cost_estimate=pl.CostEstimate(
            flops=4 * length * state * width,
            bytes_accessed=4 * length * width + 4 * state * width,
            transcendentals=0,
        ),
    )(x, cot, b, c, step, rate)


def inner_kernel(
    heads,
    head_width,
    first,
    aliased,
    x_ref,
    cot_ref,
    b_ref,
    c_ref,
    low_ref,
    src_ref,
    *refs,
):
    if aliased:
        refs = refs[2:]
    out_ref, grad_ref, gc_ref, gb_ref, gram_ref, mixed_ref, wa_ref, wb_ref = refs
    length = x_ref.shape[0]
    index = pl.program_id(0)
    pack = LANES // head_width
    blocks = length // LANES
    half = length // 2
    weights = (wa_ref, wb_ref)

    @pl.when(index == 0)
    def _():
        gram_ref[...] = mm(c_ref[...], b_ref[...], NT)
        mixed_ref[...] = jnp.zeros_like(mixed_ref)
        for ref in weights:
            ref[...] = jnp.zeros_like(ref)

    lane = lax.broadcasted_iota(jnp.int32, (1, LANES), 1) // head_width
    causal = lax.broadcasted_iota(jnp.int32, (LANES, LANES), 0) >= lax.broadcasted_iota(
        jnp.int32, (LANES, LANES), 1
    )
    x = x_ref[...]
    cot = cot_ref[...]
    cots = [jnp.where(lane == a, cot, jnp.zeros_like(cot)) for a in range(pack)]
    place = (first + index) * pack
    columns = [
        jnp.broadcast_to(low_ref[pl.ds(place + a, 1), :], (LANES, length)).T for a in range(pack)
    ]
    sources = [src_ref[pl.ds(place + a, 1), :] for a in range(pack)]
    for i in range(blocks):
        rows = slice(i * LANES, (i + 1) * LANES)
        until = (i + 1) * LANES
        scores = [mm(cots[a][rows], x[:until], NT) for a in range(pack)]
        for j in range(i + 1):
            cols = slice(j * LANES, (j + 1) * LANES)
            gram = gram_ref[rows, cols]
            mixed = mixed_ref[rows, cols]
            for a in range(pack):
                differ = columns[a][rows] - sources[a][:, cols]
                if i == j:
                    differ = jnp.where(causal, differ, -jnp.inf)
                decay = jnp.exp(differ)
                weights[a][rows, cols] = (decay * gram).astype(bf16)
                mixed = mixed + decay * scores[a][:, cols]
            mixed_ref[rows, cols] = mixed
    cot_turned = cot.T
    turned = []
    for a in range(pack):
        w = weights[a]
        top = mm(w[:half, :half], x[:half])
        bottom = mm(w[half:, :], x)
        both = jnp.concatenate([top, bottom], axis=0)
        out = both if a == 0 else jnp.where(lane == a, both, out)
        part = cot_turned[a * head_width : (a + 1) * head_width]
        left = mm(part, w[:, :half])
        right = mm(part[:, half:], w[half:, half:])
        turned.append(jnp.concatenate([left, right], axis=1))
    out_ref[...] = out.astype(out_ref.dtype)
    grad_ref[...] = jnp.concatenate(turned, axis=0).T.astype(grad_ref.dtype)

    @pl.when(index == pl.num_programs(0) - 1)
    def _():
        high, low = split_two(mixed_ref[...])
        gc_ref[...] = mm(high, b_ref[...]) + mm(low, b_ref[...])
        high, low = split_two(mixed_ref[...].T)
        gb_ref[...] = mm(high, c_ref[...]) + mm(low, c_ref[...])


def node_inner(x, cot, b, c, low, src, prior, after, chunk, part, parts, heads, head_width):
    length, state = b.shape
    width = heads * head_width
    count = width // LANES // parts
    offset = (chunk * parts + part) * count
    whole = lambda i: (0, 0)
    place = lambda i: (0, offset + i)
    aliased = prior is not None
    operands = [x, cot, b, c, low, src]
    in_specs = [
        pl.BlockSpec((length, LANES), place),
        pl.BlockSpec((length, LANES), place),
        pl.BlockSpec((length, state), whole),
        pl.BlockSpec((length, state), whole),
        pl.BlockSpec((heads, length), whole),
        pl.BlockSpec((heads, length), whole),
    ]
    aliases = {}
    if aliased:
        aliases = {len(operands): 0, len(operands) + 1: 1}
        operands += list(prior)
        in_specs += [pl.BlockSpec(memory_space=pl.ANY)] * 2
    kernel = functools.partial(inner_kernel, heads, head_width, part * count, aliased)
    kernel, in_specs, operands, aliases = ordered(kernel, in_specs, operands, after, aliases)
    return pl.pallas_call(
        kernel,
        grid=(count,),
        in_specs=in_specs,
        out_specs=[
            pl.BlockSpec((length, LANES), place),
            pl.BlockSpec((length, LANES), place),
            pl.BlockSpec((length, state), whole),
            pl.BlockSpec((length, state), whole),
        ],
        out_shape=[
            jax.ShapeDtypeStruct(x.shape, bf16),
            jax.ShapeDtypeStruct(x.shape, bf16),
            jax.ShapeDtypeStruct((length, state), f32),
            jax.ShapeDtypeStruct((length, state), f32),
        ],
        scratch_shapes=[
            pltpu.VMEM((length, length), f32),
            pltpu.VMEM((length, length), f32),
            pltpu.VMEM((length, length), bf16),
            pltpu.VMEM((length, length), bf16),
        ],
        input_output_aliases=aliases,
        name="node_inner",
        cost_estimate=pl.CostEstimate(
            flops=24 * length * length * count * LANES,
            bytes_accessed=12 * length * count * LANES,
            transcendentals=length * length * heads // parts,
        ),
    )(*operands)


def tree_kernel(
    heads, head_width, parents_ref, recv_ref, out_ref, token_ref, decay_ref, back_ref
):
    nodes, rows = recv_ref.shape[:2]
    width = heads * head_width
    totals = recv_ref[:, :, 2 * width :].astype(f32).reshape(nodes * rows, LANES).astype(bf16)
    spread = spread_matrix(LANES, LANES, width, head_width, 0)
    decay_ref[...] = mm(totals, spread).reshape(nodes, rows, width)
    back_ref[...] = jnp.zeros_like(back_ref)

    def visit(n, carry):
        seed = recv_ref[n, :, width : 2 * width].astype(f32)
        start = jnp.zeros((rows, width), f32)
        factor = jnp.ones((rows, width), f32)
        at = n
        valid = jnp.bool_(True)
        for level in range(LEVELS):
            up = parents_ref[at]
            valid = jnp.logical_and(valid, up >= 0)
            at = jnp.maximum(up, 0)
            keep = jnp.where(valid, f32(1), f32(0))
            factor = factor * keep
            start = start + factor * recv_ref[at, :, :width].astype(f32)
            back_ref[at] = back_ref[at] + factor * seed
            if level < LEVELS - 1:
                factor = factor * decay_ref[at]
        out_ref[n, :, :width] = start.astype(bf16)
        return carry

    lax.fori_loop(0, nodes, visit, 0)
    out_ref[:, :, width:] = back_ref[...].astype(bf16)
    token_ref[...] = jnp.zeros_like(token_ref)


def combine(parents, recv, after, heads, head_width):
    nodes, rows, _ = recv.shape
    width = heads * head_width
    in_specs = [
        pl.BlockSpec(memory_space=pltpu.SMEM),
        pl.BlockSpec(memory_space=pltpu.VMEM),
    ]
    kernel = functools.partial(tree_kernel, heads, head_width)
    kernel, in_specs, operands, _ = ordered(kernel, in_specs, [parents, recv], after)
    return pl.pallas_call(
        kernel,
        in_specs=in_specs,
        out_specs=[
            pl.BlockSpec(memory_space=pltpu.VMEM),
            pl.BlockSpec(memory_space=pltpu.VMEM),
        ],
        out_shape=[
            jax.ShapeDtypeStruct((nodes, rows, 2 * width), bf16),
            jax.ShapeDtypeStruct((8, LANES), f32),
        ],
        scratch_shapes=[
            pltpu.VMEM((nodes, rows, width), f32),
            pltpu.VMEM((nodes, rows, width), f32),
        ],
        name="tree_combine",
        cost_estimate=pl.CostEstimate(
            flops=20 * nodes * rows * width,
            bytes_accessed=8 * nodes * rows * width,
            transcendentals=0,
        ),
    )(*operands)


def outer_kernel(
    heads,
    head_width,
    aliased,
    x_ref,
    cot_ref,
    b_ref,
    c_ref,
    grow_ref,
    tail_ref,
    start_ref,
    back_ref,
    inner_ref,
    grad_ref,
    *refs,
):
    out_ref, gx_ref, gc_ref, gb_ref = refs[2:] if aliased else refs
    block = x_ref.shape[1]
    index = pl.program_id(0)
    spread = spread_matrix(2 * heads, heads, block, head_width, index * block)
    grow_wide = mm(grow_ref[...], spread)
    tail_wide = mm(tail_ref[...], spread)
    start = start_ref[...]
    back = back_ref[...]
    out_ref[...] = (inner_ref[...].astype(f32) + grow_wide * mm(c_ref[...], start)).astype(bf16)
    gx_ref[...] = (grad_ref[...].astype(f32) + tail_wide * mm(b_ref[...], back)).astype(bf16)
    emitted = (grow_wide * cot_ref[...].astype(f32)).astype(bf16)
    tailed = (tail_wide * x_ref[...].astype(f32)).astype(bf16)
    gc = mm(emitted, start, NT)
    gb = mm(tailed, back, NT)

    @pl.when(index == 0)
    def _():
        gc_ref[...] = gc
        gb_ref[...] = gb

    @pl.when(index > 0)
    def _():
        gc_ref[...] += gc
        gb_ref[...] += gb


def node_outer(x, cot, b, c, grow, tail, states, inner, grad, prior, chunk, heads, head_width):
    length, state = b.shape
    width = heads * head_width
    block = min(width, 4 * LANES)
    count = width // block
    whole = lambda i: (0, 0)
    spot = lambda i: (0, i)
    place = lambda i: (0, chunk * count + i)
    aliased = prior is not None
    operands = [x, cot, b, c, grow, tail, states, states, inner, grad]
    in_specs = [
        pl.BlockSpec((length, block), place),
        pl.BlockSpec((length, block), place),
        pl.BlockSpec((length, state), whole),
        pl.BlockSpec((length, state), whole),
        pl.BlockSpec((length, 2 * heads), whole),
        pl.BlockSpec((length, 2 * heads), whole),
        pl.BlockSpec((state, block), spot),
        pl.BlockSpec((state, block), lambda i: (0, count + i)),
        pl.BlockSpec((length, block), place),
        pl.BlockSpec((length, block), place),
    ]
    aliases = {}
    if aliased:
        aliases = {len(operands): 0, len(operands) + 1: 1}
        operands += list(prior)
        in_specs += [pl.BlockSpec(memory_space=pl.ANY)] * 2
    return pl.pallas_call(
        functools.partial(outer_kernel, heads, head_width, aliased),
        grid=(count,),
        in_specs=in_specs,
        out_specs=[
            pl.BlockSpec((length, block), place),
            pl.BlockSpec((length, block), place),
            pl.BlockSpec((length, state), whole),
            pl.BlockSpec((length, state), whole),
        ],
        out_shape=[
            jax.ShapeDtypeStruct(x.shape, bf16),
            jax.ShapeDtypeStruct(x.shape, bf16),
            jax.ShapeDtypeStruct((length, state), f32),
            jax.ShapeDtypeStruct((length, state), f32),
        ],
        input_output_aliases=aliases,
        name="node_outer",
        cost_estimate=pl.CostEstimate(
            flops=8 * length * state * width,
            bytes_accessed=16 * length * width,
            transcendentals=0,
        ),
    )(*operands)


def scatter_sum(parts):
    size = lax.axis_size("head")
    me = lax.axis_index("head")
    rows = parts.shape[1] // size
    total = lax.dynamic_slice_in_dim(parts, me * rows, rows, axis=1)
    for shift in range(1, size):
        target = (me + shift) % size
        piece = lax.dynamic_slice_in_dim(parts, target * rows, rows, axis=1).astype(bf16)
        moved = lax.ppermute(piece, "head", [(i, (i + shift) % size) for i in range(size)])
        total = total + moved.astype(f32)
    return total


def on_device(inputs, b_matrix, c_matrix, step_size, decay_rate, parents, cotangent):
    state = b_matrix.shape[1]
    head_count = step_size.shape[0]
    head_width = inputs.shape[1] // head_count
    nodes = lax.axis_size("node")
    heads = head_count // CHUNKS
    rows = state // nodes
    rate = decay_rate[None, :]

    def swap(v):
        moved = lax.all_to_all(
            v.reshape(nodes, rows, v.shape[-1]), "node", split_axis=0, concat_axis=0, tiled=True
        )
        return moved

    shared = (inputs, cotangent, b_matrix, c_matrix)
    sizes = (heads, head_width)
    made = [node_states(*shared, step_size, rate, k, *sizes) for k in range(CHUNKS)]
    received = [swap(made[k][0]) for k in range(CHUNKS)]
    prior = None
    token = made[CHUNKS - 1][1]
    grad_c = grad_b = 0.0
    waiting = list(range(CHUNKS))
    states = []
    for k in range(CHUNKS):
        for part in range(PARTS):
            *prior, gc, gb = node_inner(
                *shared, made[k][1], made[k][2], prior, token, k, part, PARTS, *sizes
            )
            token = gc
            grad_c += gc
            grad_b += gb
            if waiting:
                which = waiting.pop(0)
                joined, token = combine(parents, received[which], token, *sizes)
                states.append(swap(joined).reshape(state, -1))
    inner = prior
    prior = None
    for k in range(CHUNKS):
        *prior, gc, gb = node_outer(
            *shared, made[k][3], made[k][4], states[k], *inner, prior, k, *sizes
        )
        grad_c += gc
        grad_b += gb
    grads = scatter_sum(jnp.stack([grad_b, grad_c]))
    return prior[0], prior[1], grads[0], grads[1]


def solution(mesh):
    return jax.shard_map(
        on_device,
        mesh=mesh,
        in_specs=(
            P("node", "head"),
            P("node", None),
            P("node", None),
            P("head", "node"),
            P("head"),
            P(),
            P("node", "head"),
        ),
        out_specs=(
            P("node", "head"),
            P("node", "head"),
            P(("node", "head"), None),
            P(("node", "head"), None),
        ),
        check_vma=False,
    )
```

```python
import functools
import math

import jax
import jax.numpy as jnp
from jax import lax
from jax.experimental import pallas as pl
from jax.experimental.pallas import tpu as pltpu
from jax.sharding import PartitionSpec as P

LEVELS = 3
LANES = 128
CHUNKS = 2
PARTS = 2

f32 = jnp.float32
bf16 = jnp.bfloat16
NN = (((1,), (0,)), ((), ()))
NT = (((1,), (1,)), ((), ()))


def mm(a, b, dims=NN):
    return lax.dot_general(a, b, dims, preferred_element_type=f32)


def ordered(kernel, in_specs, operands, after, aliases=None):
    if after is None:
        return kernel, in_specs, operands, aliases or {}

    def body(after_ref, *refs):
        kernel(*refs)

    shifted = {key + 1: value for key, value in (aliases or {}).items()}
    return body, [pl.BlockSpec(memory_space=pl.ANY)] + in_specs, [after] + operands, shifted


def split_two(v):
    high = v.astype(bf16)
    return high, (v - high.astype(f32)).astype(bf16)


def spread_matrix(rows, heads, width, head_width, offset):
    row = lax.broadcasted_iota(jnp.int32, (rows, width), 0) % heads
    lane = (lax.broadcasted_iota(jnp.int32, (rows, width), 1) + offset) // head_width
    return (row == lane).astype(bf16)


def states_kernel(
    heads,
    head_width,
    chunk,
    x_ref,
    cot_ref,
    b_ref,
    c_ref,
    step_ref,
    rate_ref,
    send_ref,
    low_ref,
    src_ref,
    grow_ref,
    tail_ref,
    bt_ref,
    ct_ref,
):
    block = x_ref.shape[1]
    length = step_ref.shape[1]
    index = pl.program_id(0)
    width = heads * head_width

    @pl.when(index == 0)
    def _():
        step = step_ref[...]
        rates = jnp.broadcast_to(rate_ref[...], (LANES, rate_ref.shape[1])).T
        terms = -step * rates[chunk * heads : (chunk + 1) * heads, :1]
        row = lax.broadcasted_iota(jnp.int32, (length, length), 0)
        col = lax.broadcasted_iota(jnp.int32, (length, length), 1)
        upper = (row <= col).astype(bf16)
        first = terms.astype(bf16)
        rest = terms - first.astype(f32)
        second, third = split_two(rest)
        cumulative = mm(third, upper) + mm(second, upper) + mm(first, upper)
        last = cumulative[:, length - 1 :]
        low_ref[...] = cumulative
        src_ref[...] = cumulative - jnp.log(step)
        growth = jnp.exp(cumulative)
        tail = jnp.exp(last - cumulative) * step
        grow_ref[...] = jnp.concatenate(split_two(growth.T), axis=1)
        tail_ref[...] = jnp.concatenate(split_two(tail.T), axis=1)
        bt_ref[...] = b_ref[...].T
        ct_ref[...] = c_ref[...].T
        total = jnp.exp(jnp.broadcast_to(last, (heads, send_ref.shape[0])))
        pad = jnp.zeros((LANES - heads, send_ref.shape[0]), f32)
        totals = jnp.concatenate([total, pad], axis=0).T
        send_ref[:, 2 * width :] = totals.astype(bf16)

    spread = spread_matrix(2 * heads, heads, block, head_width, index * block)
    tail_wide = mm(tail_ref[...], spread)
    grow_wide = mm(grow_ref[...], spread)
    tailed = (tail_wide * x_ref[...].astype(f32)).astype(bf16)
    emitted = (grow_wide * cot_ref[...].astype(f32)).astype(bf16)
    at = pl.multiple_of(index * block, block)
    send_ref[:, pl.ds(at, block)] = mm(bt_ref[...], tailed).astype(bf16)
    send_ref[:, pl.ds(at + width, block)] = mm(ct_ref[...], emitted).astype(bf16)


def node_states(x, cot, b, c, step, rate, chunk, heads, head_width):
    length, state = b.shape
    width = heads * head_width
    block = min(width, 4 * LANES)
    count = width // block
    whole = lambda i: (0, 0)
    return pl.pallas_call(
        functools.partial(states_kernel, heads, head_width, chunk),
        grid=(count,),
        in_specs=[
            pl.BlockSpec((length, block), lambda i: (0, chunk * count + i)),
            pl.BlockSpec((length, block), lambda i: (0, chunk * count + i)),
            pl.BlockSpec((length, state), whole),
            pl.BlockSpec((length, state), whole),
            pl.BlockSpec((heads, length), lambda i: (chunk, 0)),
            pl.BlockSpec(rate.shape, whole),
        ],
        out_specs=[
            pl.BlockSpec((state, 2 * width + LANES), whole),
            pl.BlockSpec((heads, length), whole),
            pl.BlockSpec((heads, length), whole),
            pl.BlockSpec((length, 2 * heads), whole),
            pl.BlockSpec((length, 2 * heads), whole),
        ],
        out_shape=[
            jax.ShapeDtypeStruct((state, 2 * width + LANES), bf16),
            jax.ShapeDtypeStruct((heads, length), f32),
            jax.ShapeDtypeStruct((heads, length), f32),
            jax.ShapeDtypeStruct((length, 2 * heads), bf16),
            jax.ShapeDtypeStruct((length, 2 * heads), bf16),
        ],
        scratch_shapes=[pltpu.VMEM((state, length), bf16), pltpu.VMEM((state, length), bf16)],
        name="node_states",
        cost_estimate=pl.CostEstimate(
            flops=4 * length * state * width,
            bytes_accessed=4 * length * width + 4 * state * width,
            transcendentals=0,
        ),
    )(x, cot, b, c, step, rate)


def inner_kernel(
    heads,
    head_width,
    first,
    aliased,
    x_ref,
    cot_ref,
    b_ref,
    c_ref,
    low_ref,
    src_ref,
    *refs,
):
    if aliased:
        refs = refs[2:]
    out_ref, grad_ref, gc_ref, gb_ref, gram_ref, mixed_ref, wa_ref, wb_ref = refs
    length = x_ref.shape[0]
    index = pl.program_id(0)
    pack = LANES // head_width
    blocks = length // LANES
    half = length // 2
    weights = (wa_ref, wb_ref)

    @pl.when(index == 0)
    def _():
        gram_ref[...] = mm(c_ref[...], b_ref[...], NT)
        mixed_ref[...] = jnp.zeros_like(mixed_ref)
        for ref in weights:
            ref[...] = jnp.zeros_like(ref)

    lane = lax.broadcasted_iota(jnp.int32, (1, LANES), 1) // head_width
    causal = lax.broadcasted_iota(jnp.int32, (LANES, LANES), 0) >= lax.broadcasted_iota(
        jnp.int32, (LANES, LANES), 1
    )
    x = x_ref[...]
    cot = cot_ref[...]
    cots = [jnp.where(lane == a, cot, jnp.zeros_like(cot)) for a in range(pack)]
    place = (first + index) * pack
    columns = [
        jnp.broadcast_to(low_ref[pl.ds(place + a, 1), :], (LANES, length)).T for a in range(pack)
    ]
    sources = [src_ref[pl.ds(place + a, 1), :] for a in range(pack)]
    for i in range(blocks):
        rows = slice(i * LANES, (i + 1) * LANES)
        until = (i + 1) * LANES
        scores = [mm(cots[a][rows], x[:until], NT) for a in range(pack)]
        for j in range(i + 1):
            cols = slice(j * LANES, (j + 1) * LANES)
            gram = gram_ref[rows, cols]
            mixed = mixed_ref[rows, cols]
            for a in range(pack):
                differ = columns[a][rows] - sources[a][:, cols]
                if i == j:
                    differ = jnp.where(causal, differ, -jnp.inf)
                decay = jnp.exp(differ)
                weights[a][rows, cols] = (decay * gram).astype(bf16)
                mixed = mixed + decay * scores[a][:, cols]
            mixed_ref[rows, cols] = mixed
    cot_turned = cot.T
    turned = []
    for a in range(pack):
        w = weights[a]
        top = mm(w[:half, :half], x[:half])
        bottom = mm(w[half:, :], x)
        both = jnp.concatenate([top, bottom], axis=0)
        out = both if a == 0 else jnp.where(lane == a, both, out)
        part = cot_turned[a * head_width : (a + 1) * head_width]
        left = mm(part, w[:, :half])
        right = mm(part[:, half:], w[half:, half:])
        turned.append(jnp.concatenate([left, right], axis=1))
    out_ref[...] = out.astype(out_ref.dtype)
    grad_ref[...] = jnp.concatenate(turned, axis=0).T.astype(grad_ref.dtype)

    @pl.when(index == pl.num_programs(0) - 1)
    def _():
        high, low = split_two(mixed_ref[...])
        gc_ref[...] = mm(high, b_ref[...]) + mm(low, b_ref[...])
        high, low = split_two(mixed_ref[...].T)
        gb_ref[...] = mm(high, c_ref[...]) + mm(low, c_ref[...])


def node_inner(x, cot, b, c, low, src, prior, after, chunk, part, parts, heads, head_width):
    length, state = b.shape
    width = heads * head_width
    count = width // LANES // parts
    offset = (chunk * parts + part) * count
    whole = lambda i: (0, 0)
    place = lambda i: (0, offset + i)
    aliased = prior is not None
    operands = [x, cot, b, c, low, src]
    in_specs = [
        pl.BlockSpec((length, LANES), place),
        pl.BlockSpec((length, LANES), place),
        pl.BlockSpec((length, state), whole),
        pl.BlockSpec((length, state), whole),
        pl.BlockSpec((heads, length), whole),
        pl.BlockSpec((heads, length), whole),
    ]
    aliases = {}
    if aliased:
        aliases = {len(operands): 0, len(operands) + 1: 1}
        operands += list(prior)
        in_specs += [pl.BlockSpec(memory_space=pl.ANY)] * 2
    kernel = functools.partial(inner_kernel, heads, head_width, part * count, aliased)
    kernel, in_specs, operands, aliases = ordered(kernel, in_specs, operands, after, aliases)
    return pl.pallas_call(
        kernel,
        grid=(count,),
        in_specs=in_specs,
        out_specs=[
            pl.BlockSpec((length, LANES), place),
            pl.BlockSpec((length, LANES), place),
            pl.BlockSpec((length, state), whole),
            pl.BlockSpec((length, state), whole),
        ],
        out_shape=[
            jax.ShapeDtypeStruct(x.shape, bf16),
            jax.ShapeDtypeStruct(x.shape, bf16),
            jax.ShapeDtypeStruct((length, state), f32),
            jax.ShapeDtypeStruct((length, state), f32),
        ],
        scratch_shapes=[
            pltpu.VMEM((length, length), f32),
            pltpu.VMEM((length, length), f32),
            pltpu.VMEM((length, length), bf16),
            pltpu.VMEM((length, length), bf16),
        ],
        input_output_aliases=aliases,
        name="node_inner",
        cost_estimate=pl.CostEstimate(
            flops=24 * length * length * count * LANES,
            bytes_accessed=12 * length * count * LANES,
            transcendentals=length * length * heads // parts,
        ),
    )(*operands)


def rank_nodes(parents_ref, rank_ref, half):
    nodes = rank_ref.shape[0]

    def clear(n, carry):
        rank_ref[n] = 0
        return carry

    def mark(n, carry):
        up = parents_ref[n]

        @pl.when(jnp.logical_and(up >= 0, (up >= half) != (n >= half)))
        def _():
            rank_ref[up] = 1

        return carry

    def place(n, count):
        crosses = rank_ref[n]
        rank_ref[n] = jnp.where(crosses > 0, count, -1)
        return count + crosses

    lax.fori_loop(0, nodes, clear, 0)
    lax.fori_loop(0, nodes, mark, 0)
    lax.fori_loop(0, nodes, place, 0)


def widen(narrow, heads, head_width):
    count, rows = narrow.shape[:2]
    width = heads * head_width
    flat = narrow.astype(f32).reshape(count * rows, LANES).astype(bf16)
    spread = spread_matrix(LANES, LANES, width, head_width, 0)
    return mm(flat, spread).reshape(count, rows, width)


def pack_kernel(
    heads, head_width, parents_ref, recv_ref, main_ref, more_ref, decay_ref, slot_ref, chain_ref, rank_ref
):
    half = recv_ref.shape[0]
    width = heads * head_width
    base = lax.axis_index("node") // half * half
    rank_nodes(parents_ref, rank_ref, half)
    decay_ref[...] = widen(recv_ref[:, :, 2 * width :], heads, head_width)
    slot_ref[...] = jnp.zeros_like(slot_ref)
    chain_ref[...] = jnp.zeros_like(chain_ref)

    def inside(n):
        return jnp.logical_and(n >= base, n < base + half)

    def spot(n):
        return jnp.clip(n - base, 0, half - 1)

    def visit(m, carry):
        node = base + m
        flow = recv_ref[m, :, width : 2 * width].astype(f32)
        at = node
        live = jnp.bool_(True)
        for level in range(LEVELS):
            up = parents_ref[at]
            exists = jnp.logical_and(live, up >= 0)
            live = jnp.logical_and(exists, inside(up))
            away = jnp.logical_and(exists, jnp.logical_not(live))

            @pl.when(away)
            def _(flow=flow, up=up):
                slot = rank_ref[up]
                slot_ref[slot] = slot_ref[slot] + flow

            if level < LEVELS - 1:
                flow = flow * jnp.where(live, decay_ref[spot(up)], 1.0)
            at = jnp.where(live, up, at)

        @pl.when(rank_ref[node] >= 0)
        def _():
            total = recv_ref[m, :, :width].astype(f32)
            factor = decay_ref[m]
            chain = recv_ref[m, :, 2 * width :].astype(f32)
            at = node
            live = jnp.bool_(True)
            for level in range(LEVELS - 1):
                up = parents_ref[at]
                live = jnp.logical_and(jnp.logical_and(live, up >= 0), inside(up))
                where = spot(up)
                total = total + jnp.where(live, factor * recv_ref[where, :, :width].astype(f32), 0.0)
                factor = factor * jnp.where(live, decay_ref[where], 1.0)
                chain = chain * jnp.where(live, recv_ref[where, :, 2 * width :].astype(f32), 1.0)
                at = jnp.where(live, up, at)
            slot_ref[rank_ref[node]] = total
            chain_ref[rank_ref[node]] = chain

        return carry

    lax.fori_loop(0, half, visit, 0)
    main = main_ref.shape[0]
    main_ref[:, :, :width] = slot_ref[:main].astype(bf16)
    main_ref[:, :, width:] = chain_ref[:main].astype(bf16)
    more_ref[:, :, :width] = slot_ref[main:].astype(bf16)
    more_ref[:, :, width:] = chain_ref[main:].astype(bf16)


def slot_counts(nodes):
    most = nodes * LEVELS // (LEVELS + 1)
    return most // 2, most - most // 2


def pack_slots(parents, recv, after, nodes, heads, head_width):
    half, rows, _ = recv.shape
    width = heads * head_width
    main, more = slot_counts(nodes)
    in_specs = [pl.BlockSpec(memory_space=pltpu.SMEM), pl.BlockSpec(memory_space=pltpu.VMEM)]
    kernel = functools.partial(pack_kernel, heads, head_width)
    kernel, in_specs, operands, _ = ordered(kernel, in_specs, [parents, recv], after)
    return pl.pallas_call(
        kernel,
        in_specs=in_specs,
        out_specs=[pl.BlockSpec(memory_space=pltpu.VMEM)] * 2,
        out_shape=[
            jax.ShapeDtypeStruct((main, rows, width + LANES), bf16),
            jax.ShapeDtypeStruct((more, rows, width + LANES), bf16),
        ],
        scratch_shapes=[
            pltpu.VMEM((half, rows, width), f32),
            pltpu.VMEM((main + more, rows, width), f32),
            pltpu.VMEM((main + more, rows, LANES), f32),
            pltpu.SMEM((nodes,), jnp.int32),
        ],
        name="pack_slots",
        cost_estimate=pl.CostEstimate(
            flops=20 * half * rows * width,
            bytes_accessed=8 * half * rows * width,
            transcendentals=0,
        ),
    )(*operands)


def join_kernel(
    heads,
    head_width,
    parents_ref,
    recv_ref,
    main_ref,
    more_ref,
    out_ref,
    token_ref,
    decay_ref,
    slot_ref,
    chain_ref,
    back_ref,
    rank_ref,
):
    half = recv_ref.shape[0]
    nodes = rank_ref.shape[0]
    width = heads * head_width
    main = main_ref.shape[0]
    base = lax.axis_index("node") // half * half
    rank_nodes(parents_ref, rank_ref, half)
    decay_ref[...] = widen(recv_ref[:, :, 2 * width :], heads, head_width)
    slot_ref[:main] = main_ref[:, :, :width].astype(f32)
    slot_ref[main:] = more_ref[:, :, :width].astype(f32)
    chain_ref[:main] = widen(main_ref[:, :, width:], heads, head_width)
    chain_ref[main:] = widen(more_ref[:, :, width:], heads, head_width)
    back_ref[...] = jnp.zeros_like(back_ref)

    def inside(n):
        return jnp.logical_and(n >= base, n < base + half)

    def climb(at, flow, start):
        factor = None
        live = jnp.bool_(True)
        for level in range(LEVELS):
            up = parents_ref[at]
            live = jnp.logical_and(live, up >= 0)
            near = jnp.logical_and(live, inside(up))
            far = jnp.logical_and(live, jnp.logical_not(near))
            where = jnp.clip(up - base, 0, half - 1)
            slot = jnp.where(far, rank_ref[jnp.maximum(up, 0)], 0)

            @pl.when(near)
            def _(flow=flow, where=where):
                back_ref[where] = back_ref[where] + flow

            if start is not None:
                value = jnp.where(near, recv_ref[where, :, :width].astype(f32), slot_ref[slot])
                value = jnp.where(live, value, 0.0)
                start = start + (value if factor is None else factor * value)
            if level < LEVELS - 1:
                step = jnp.where(near, decay_ref[where], chain_ref[slot])
                flow = flow * step
                factor = step if factor is None else factor * step
                top = jnp.maximum(up, 0)
                for _ in range(LEVELS - 1):
                    above = parents_ref[top]
                    more = jnp.logical_and(far, above >= 0)
                    more = jnp.logical_and(more, jnp.logical_not(inside(above)))
                    top = jnp.where(more, above, top)
                at = top
        return start

    def visit(m, carry):
        node = base + m
        seed = recv_ref[m, :, width : 2 * width].astype(f32)
        start = climb(node, seed, jnp.zeros(seed.shape, f32))
        out_ref[m, :, :width] = start.astype(bf16)

        @pl.when(rank_ref[node] >= 0)
        def _():
            extra = slot_ref[rank_ref[node]]
            back_ref[m] = back_ref[m] + extra
            climb(node, extra * decay_ref[m], None)

        return carry

    lax.fori_loop(0, half, visit, 0)
    out_ref[:, :, width:] = back_ref[...].astype(bf16)
    token_ref[...] = jnp.zeros_like(token_ref)


def join_slots(parents, recv, main, more, after, nodes, heads, head_width):
    half, rows, _ = recv.shape
    width = heads * head_width
    in_specs = [pl.BlockSpec(memory_space=pltpu.SMEM)] + [pl.BlockSpec(memory_space=pltpu.VMEM)] * 3
    kernel = functools.partial(join_kernel, heads, head_width)
    kernel, in_specs, operands, _ = ordered(kernel, in_specs, [parents, recv, main, more], after)
    slots = main.shape[0] + more.shape[0]
    return pl.pallas_call(
        kernel,
        in_specs=in_specs,
        out_specs=[pl.BlockSpec(memory_space=pltpu.VMEM)] * 2,
        out_shape=[
            jax.ShapeDtypeStruct((half, rows, 2 * width), bf16),
            jax.ShapeDtypeStruct((8, LANES), f32),
        ],
        scratch_shapes=[
            pltpu.VMEM((half, rows, width), f32),
            pltpu.VMEM((slots, rows, width), f32),
            pltpu.VMEM((slots, rows, width), f32),
            pltpu.VMEM((half, rows, width), f32),
            pltpu.SMEM((nodes,), jnp.int32),
        ],
        name="join_slots",
        cost_estimate=pl.CostEstimate(
            flops=20 * half * rows * width,
            bytes_accessed=8 * half * rows * width,
            transcendentals=0,
        ),
    )(*operands)


def outer_kernel(
    heads,
    head_width,
    aliased,
    x_ref,
    cot_ref,
    b_ref,
    c_ref,
    grow_ref,
    tail_ref,
    start_ref,
    back_ref,
    inner_ref,
    grad_ref,
    *refs,
):
    out_ref, gx_ref, gc_ref, gb_ref = refs[2:] if aliased else refs
    block = x_ref.shape[1]
    index = pl.program_id(0)
    spread = spread_matrix(2 * heads, heads, block, head_width, index * block)
    grow_wide = mm(grow_ref[...], spread)
    tail_wide = mm(tail_ref[...], spread)
    start = start_ref[...]
    back = back_ref[...]
    out_ref[...] = (inner_ref[...].astype(f32) + grow_wide * mm(c_ref[...], start)).astype(bf16)
    gx_ref[...] = (grad_ref[...].astype(f32) + tail_wide * mm(b_ref[...], back)).astype(bf16)
    emitted = (grow_wide * cot_ref[...].astype(f32)).astype(bf16)
    tailed = (tail_wide * x_ref[...].astype(f32)).astype(bf16)
    gc = mm(emitted, start, NT)
    gb = mm(tailed, back, NT)

    @pl.when(index == 0)
    def _():
        gc_ref[...] = gc
        gb_ref[...] = gb

    @pl.when(index > 0)
    def _():
        gc_ref[...] += gc
        gb_ref[...] += gb


def node_outer(x, cot, b, c, grow, tail, states, inner, grad, prior, chunk, heads, head_width):
    length, state = b.shape
    width = heads * head_width
    block = min(width, 4 * LANES)
    count = width // block
    whole = lambda i: (0, 0)
    spot = lambda i: (0, i)
    place = lambda i: (0, chunk * count + i)
    aliased = prior is not None
    operands = [x, cot, b, c, grow, tail, states, states, inner, grad]
    in_specs = [
        pl.BlockSpec((length, block), place),
        pl.BlockSpec((length, block), place),
        pl.BlockSpec((length, state), whole),
        pl.BlockSpec((length, state), whole),
        pl.BlockSpec((length, 2 * heads), whole),
        pl.BlockSpec((length, 2 * heads), whole),
        pl.BlockSpec((state, block), spot),
        pl.BlockSpec((state, block), lambda i: (0, count + i)),
        pl.BlockSpec((length, block), place),
        pl.BlockSpec((length, block), place),
    ]
    aliases = {}
    if aliased:
        aliases = {len(operands): 0, len(operands) + 1: 1}
        operands += list(prior)
        in_specs += [pl.BlockSpec(memory_space=pl.ANY)] * 2
    return pl.pallas_call(
        functools.partial(outer_kernel, heads, head_width, aliased),
        grid=(count,),
        in_specs=in_specs,
        out_specs=[
            pl.BlockSpec((length, block), place),
            pl.BlockSpec((length, block), place),
            pl.BlockSpec((length, state), whole),
            pl.BlockSpec((length, state), whole),
        ],
        out_shape=[
            jax.ShapeDtypeStruct(x.shape, bf16),
            jax.ShapeDtypeStruct(x.shape, bf16),
            jax.ShapeDtypeStruct((length, state), f32),
            jax.ShapeDtypeStruct((length, state), f32),
        ],
        input_output_aliases=aliases,
        name="node_outer",
        cost_estimate=pl.CostEstimate(
            flops=8 * length * state * width,
            bytes_accessed=16 * length * width,
            transcendentals=0,
        ),
    )(*operands)


def scatter_sum(parts):
    size = lax.axis_size("head")
    me = lax.axis_index("head")
    rows = parts.shape[1] // size
    total = lax.dynamic_slice_in_dim(parts, me * rows, rows, axis=1)
    for shift in range(1, size):
        target = (me + shift) % size
        piece = lax.dynamic_slice_in_dim(parts, target * rows, rows, axis=1).astype(bf16)
        moved = lax.ppermute(piece, "head", [(i, (i + shift) % size) for i in range(size)])
        total = total + moved.astype(f32)
    return total


def on_device(inputs, b_matrix, c_matrix, step_size, decay_rate, parents, cotangent):
    state = b_matrix.shape[1]
    head_count = step_size.shape[0]
    head_width = inputs.shape[1] // head_count
    nodes = lax.axis_size("node")
    heads = head_count // CHUNKS
    half = nodes // 2
    rate = decay_rate[None, :]
    groups = [list(range(half)), list(range(half, nodes))]
    across = [(n, (n + half) % nodes) for n in range(nodes)]

    def swap(v):
        return lax.all_to_all(
            v.reshape(half, state // half, v.shape[-1]),
            "node",
            split_axis=0,
            concat_axis=0,
            tiled=True,
            axis_index_groups=groups,
        )

    def cross(v):
        return lax.ppermute(v, "node", across)

    places = jnp.arange(nodes)
    child = jnp.logical_and(
        parents[:, None] == places[None, :], (places[:, None] < half) != (places[None, :] < half)
    )
    crossing = jnp.sum(jnp.any(child, axis=0).astype(jnp.int32))
    crowded = crossing > slot_counts(nodes)[0]

    shared = (inputs, cotangent, b_matrix, c_matrix)
    sizes = (heads, head_width)
    made = [node_states(*shared, step_size, rate, k, *sizes) for k in range(CHUNKS)]
    received = [swap(made[k][0]) for k in range(CHUNKS)]
    grads_found = []
    prior = None
    token = made[CHUNKS - 1][1]

    def inner_part(prior, token, k, part):
        *prior, gc, gb = node_inner(
            *shared, made[k][1], made[k][2], prior, token, k, part, PARTS, *sizes
        )
        grads_found.append((gb, gc))
        return prior, gc

    todo = [(k, part) for k in range(CHUNKS) for part in range(PARTS)]
    packed = []
    for k in range(CHUNKS):
        prior, token = inner_part(prior, token, *todo.pop(0))
        main, more = pack_slots(parents, received[k], token, nodes, *sizes)
        packed.append((main, more, cross(main)))
        token = more
    others = lax.cond(
        crowded,
        lambda vs: tuple(cross(v) for v in vs),
        lambda vs: vs,
        tuple(p[1] for p in packed),
    )
    states = []
    for k in range(CHUNKS):
        joined, token = join_slots(
            parents, received[k], packed[k][2], others[k], token, nodes, *sizes
        )
        states.append(swap(joined).reshape(state, -1))
        prior, token = inner_part(prior, token, *todo.pop(0))
    inner = prior
    prior = None
    for k in range(CHUNKS):
        *prior, gc, gb = node_outer(
            *shared, made[k][3], made[k][4], states[k], *inner, prior, k, *sizes
        )
        grads_found.append((gb, gc))
    grad_b = sum(g[0] for g in grads_found)
    grad_c = sum(g[1] for g in grads_found)
    grads = scatter_sum(jnp.stack([grad_b, grad_c]))
    return prior[0], prior[1], grads[0], grads[1]


def solution(mesh):
    return jax.shard_map(
        on_device,
        mesh=mesh,
        in_specs=(
            P("node", "head"),
            P("node", None),
            P("node", None),
            P("head", "node"),
            P("head"),
            P(),
            P("node", "head"),
        ),
        out_specs=(
            P("node", "head"),
            P("node", "head"),
            P(("node", "head"), None),
            P(("node", "head"), None),
        ),
        check_vma=False,
    )
```

```python
import functools
import math

import jax
import jax.numpy as jnp
from jax import lax
from jax.experimental import pallas as pl
from jax.experimental.pallas import tpu as pltpu
from jax.sharding import PartitionSpec as P

LEVELS = 3
LANES = 128
CHUNKS = 2
PARTS = 2

LOG2E = 1.0 / math.log(2.0)

f32 = jnp.float32
bf16 = jnp.bfloat16
NN = (((1,), (0,)), ((), ()))
NT = (((1,), (1,)), ((), ()))


def mm(a, b, dims=NN):
    return lax.dot_general(a, b, dims, preferred_element_type=f32)


def ordered(kernel, in_specs, operands, after, aliases=None):
    if after is None:
        return kernel, in_specs, operands, aliases or {}

    def body(after_ref, *refs):
        kernel(*refs)

    shifted = {key + 1: value for key, value in (aliases or {}).items()}
    return body, [pl.BlockSpec(memory_space=pl.ANY)] + in_specs, [after] + operands, shifted


def split_two(v):
    high = v.astype(bf16)
    return high, (v - high.astype(f32)).astype(bf16)


def spread_matrix(rows, width, head_width):
    row = lax.broadcasted_iota(jnp.int32, (rows, width), 0)
    lane = lax.broadcasted_iota(jnp.int32, (rows, width), 1) // head_width
    return (row == lane).astype(bf16)


def head_lanes(columns, first, head_width):
    lane = lax.broadcasted_iota(jnp.int32, columns.shape, 1) // head_width + first
    return jnp.take_along_axis(columns, lane, axis=1)


def pad_lanes(v):
    gap = LANES - v.shape[0]
    if gap:
        v = jnp.concatenate([v, jnp.zeros((gap, v.shape[1]), v.dtype)], axis=0)
    return v.T


def states_kernel(
    heads,
    head_width,
    chunk,
    x_ref,
    cot_ref,
    b_ref,
    c_ref,
    step_ref,
    rate_ref,
    send_ref,
    low_ref,
    src_ref,
    grow_ref,
    tail_ref,
    gram_ref,
    bt_ref,
    ct_ref,
):
    block = x_ref.shape[1]
    length = step_ref.shape[1]
    index = pl.program_id(0)
    width = heads * head_width
    pack = LANES // head_width

    @pl.when(index == 0)
    def _():
        step = step_ref[...]
        rates = jnp.broadcast_to(rate_ref[...], (LANES, rate_ref.shape[1])).T
        terms = -step * rates[chunk * heads : (chunk + 1) * heads, :1]
        row = lax.broadcasted_iota(jnp.int32, (length, length), 0)
        col = lax.broadcasted_iota(jnp.int32, (length, length), 1)
        upper = (row <= col).astype(bf16)
        first = terms.astype(bf16)
        rest = terms - first.astype(f32)
        second, third = split_two(rest)
        cumulative = mm(third, upper) + mm(second, upper) + mm(first, upper)
        last = cumulative[:, length - 1 :]
        low_ref[...] = pad_lanes(cumulative * LOG2E)
        src_ref[...] = (cumulative - jnp.log(step)) * LOG2E
        grow_ref[...] = pad_lanes(jnp.exp(cumulative))
        tail_ref[...] = pad_lanes(jnp.exp(last - cumulative) * step)
        bt_ref[...] = b_ref[...].T
        ct_ref[...] = c_ref[...].T
        total = jnp.exp(jnp.broadcast_to(last, (heads, send_ref.shape[0])))
        send_ref[:, 2 * width :] = pad_lanes(total).astype(bf16)
        gram_ref[...] = mm(c_ref[...], b_ref[...], NT).astype(bf16)

    grow = grow_ref[...]
    tail = tail_ref[...]
    parts = range(block // LANES)
    tailed = []
    emitted = []
    for q in parts:
        lanes = slice(q * LANES, (q + 1) * LANES)
        first = (index * (block // LANES) + q) * pack
        tail_wide = head_lanes(tail, first, head_width)
        grow_wide = head_lanes(grow, first, head_width)
        tailed.append((tail_wide * x_ref[:, lanes].astype(f32)).astype(bf16))
        emitted.append((grow_wide * cot_ref[:, lanes].astype(f32)).astype(bf16))
    at = pl.multiple_of(index * block, block)
    send_ref[:, pl.ds(at, block)] = mm(bt_ref[...], jnp.concatenate(tailed, axis=1)).astype(bf16)
    send_ref[:, pl.ds(at + width, block)] = mm(
        ct_ref[...], jnp.concatenate(emitted, axis=1)
    ).astype(bf16)


def node_states(x, cot, b, c, step, rate, chunk, heads, head_width):
    length, state = b.shape
    width = heads * head_width
    block = min(width, 4 * LANES)
    count = width // block
    whole = lambda i: (0, 0)
    return pl.pallas_call(
        functools.partial(states_kernel, heads, head_width, chunk),
        grid=(count,),
        in_specs=[
            pl.BlockSpec((length, block), lambda i: (0, chunk * count + i)),
            pl.BlockSpec((length, block), lambda i: (0, chunk * count + i)),
            pl.BlockSpec((length, state), whole),
            pl.BlockSpec((length, state), whole),
            pl.BlockSpec((heads, length), lambda i: (chunk, 0)),
            pl.BlockSpec(rate.shape, whole),
        ],
        out_specs=[
            pl.BlockSpec((state, 2 * width + LANES), whole),
            pl.BlockSpec((length, LANES), whole),
            pl.BlockSpec((heads, length), whole),
            pl.BlockSpec((length, LANES), whole),
            pl.BlockSpec((length, LANES), whole),
            pl.BlockSpec((length, length), whole),
        ],
        out_shape=[
            jax.ShapeDtypeStruct((state, 2 * width + LANES), bf16),
            jax.ShapeDtypeStruct((length, LANES), f32),
            jax.ShapeDtypeStruct((heads, length), f32),
            jax.ShapeDtypeStruct((length, LANES), f32),
            jax.ShapeDtypeStruct((length, LANES), f32),
            jax.ShapeDtypeStruct((length, length), bf16),
        ],
        scratch_shapes=[pltpu.VMEM((state, length), bf16), pltpu.VMEM((state, length), bf16)],
        name="node_states",
        cost_estimate=pl.CostEstimate(
            flops=4 * length * state * width,
            bytes_accessed=4 * length * width + 4 * state * width,
            transcendentals=0,
        ),
    )(x, cot, b, c, step, rate)


def inner_kernel(
    head_width,
    first,
    aliased,
    x_ref,
    cot_ref,
    b_ref,
    c_ref,
    gram_ref,
    low_ref,
    src_ref,
    *refs,
):
    if aliased:
        refs = refs[2:]
    out_ref, grad_ref, gc_ref, gb_ref, mixed_ref, turned_ref, wa_ref, wb_ref = refs
    length = x_ref.shape[0]
    index = pl.program_id(0)
    pack = LANES // head_width
    pairs = x_ref.shape[1] // LANES
    wide = 2 * LANES
    tiles = length // wide
    weights = (wa_ref, wb_ref)

    @pl.when(index == 0)
    def _():
        mixed_ref[...] = jnp.zeros_like(mixed_ref)
        for ref in weights:
            ref[...] = jnp.zeros_like(ref)

    lane = lax.broadcasted_iota(jnp.int32, (1, LANES), 1) // head_width
    causal = lax.broadcasted_iota(jnp.int32, (LANES, LANES), 0) >= lax.broadcasted_iota(
        jnp.int32, (LANES, LANES), 1
    )
    xs = [x_ref[:, q * LANES : (q + 1) * LANES] for q in range(pairs)]
    turned_cots = [cot_ref[:, q * LANES : (q + 1) * LANES].T for q in range(pairs)]
    low = low_ref[...]

    def decays(h):
        q, a = h // pack, h % pack
        w = weights[h % 2]
        cot = cot_ref[:, q * LANES : (q + 1) * LANES]
        cot = jnp.where(lane == a, cot, jnp.zeros_like(cot))
        place = (first + index * pairs + q) * pack + a
        column = head_lanes(low, place, LANES)
        source = src_ref[pl.ds(place, 1), :]
        for tile in range(tiles):
            scores = mm(cot[tile * wide :], xs[q][tile * wide : (tile + 1) * wide], NT)
            for i in range(2 * tile, 2 * tiles):
                rows = slice(i * LANES, (i + 1) * LANES)
                here = slice((i - 2 * tile) * LANES, (i - 2 * tile + 1) * LANES)
                for j in range(2 * tile, min(2 * tile + 1, i) + 1):
                    cols = slice(j * LANES, (j + 1) * LANES)
                    side = slice((j - 2 * tile) * LANES, (j - 2 * tile + 1) * LANES)
                    differ = column[rows] - source[:, cols]
                    if i == j:
                        differ = jnp.where(causal, differ, -jnp.inf)
                    decay = jnp.exp2(differ)
                    w[rows, cols] = decay.astype(bf16) * gram_ref[rows, cols]
                    mixed_ref[rows, cols] += decay * scores[here, side]
                yield

    def products(h):
        q, a = h // pack, h % pack
        w = weights[h % 2]
        x = xs[q]
        part = turned_cots[q][a * head_width : (a + 1) * head_width]
        mine = slice(q * LANES + a * head_width, q * LANES + (a + 1) * head_width)
        own = slice(a * head_width, (a + 1) * head_width)
        for tile in range(tiles):
            rows = slice(tile * wide, (tile + 1) * wide)
            found = mm(w[rows, : (tile + 1) * wide], x[: (tile + 1) * wide])
            out_ref[rows, mine] = found[:, own].astype(bf16)
            yield
            found = mm(part[:, tile * wide :], w[tile * wide :, rows])
            turned_ref[mine, rows] = found.astype(bf16)
            yield

    def finish(q):
        lanes = slice(q * LANES, (q + 1) * LANES)
        grad_ref[:, lanes] = turned_ref[lanes, :].T

    before = None
    for h in range(pairs * pack):
        for _ in decays(h):
            if before is not None:
                next(before, None)
        if before is not None:
            for _ in before:
                pass
            if h % pack == 0:
                finish(h // pack - 1)
        before = products(h)
    for _ in before:
        pass
    finish(pairs - 1)

    @pl.when(index == pl.num_programs(0) - 1)
    def _():
        mixed = mixed_ref[...].astype(bf16)
        gc_ref[...] = mm(mixed, b_ref[...])
        gb_ref[...] = mm(mixed.T, c_ref[...])


def node_inner(x, cot, b, c, gram, low, src, prior, after, chunk, part, parts, heads, head_width):
    length, state = b.shape
    width = heads * head_width
    block = min(width // parts, 2 * LANES)
    count = width // block // parts
    offset = (chunk * parts + part) * count
    whole = lambda i: (0, 0)
    place = lambda i: (0, offset + i)
    aliased = prior is not None
    operands = [x, cot, b, c, gram, low, src]
    in_specs = [
        pl.BlockSpec((length, block), place),
        pl.BlockSpec((length, block), place),
        pl.BlockSpec((length, state), whole),
        pl.BlockSpec((length, state), whole),
        pl.BlockSpec((length, length), whole),
        pl.BlockSpec((length, LANES), whole),
        pl.BlockSpec((heads, length), whole),
    ]
    aliases = {}
    if aliased:
        aliases = {len(operands): 0, len(operands) + 1: 1}
        operands += list(prior)
        in_specs += [pl.BlockSpec(memory_space=pl.ANY)] * 2
    kernel = functools.partial(inner_kernel, head_width, part * count * block // LANES, aliased)
    kernel, in_specs, operands, aliases = ordered(kernel, in_specs, operands, after, aliases)
    return pl.pallas_call(
        kernel,
        grid=(count,),
        in_specs=in_specs,
        out_specs=[
            pl.BlockSpec((length, block), place),
            pl.BlockSpec((length, block), place),
            pl.BlockSpec((length, state), whole),
            pl.BlockSpec((length, state), whole),
        ],
        out_shape=[
            jax.ShapeDtypeStruct(x.shape, bf16),
            jax.ShapeDtypeStruct(x.shape, bf16),
            jax.ShapeDtypeStruct((length, state), f32),
            jax.ShapeDtypeStruct((length, state), f32),
        ],
        scratch_shapes=[
            pltpu.VMEM((length, length), f32),
            pltpu.VMEM((block, length), bf16),
            pltpu.VMEM((length, length), bf16),
            pltpu.VMEM((length, length), bf16),
        ],
        input_output_aliases=aliases,
        name="node_inner",
        cost_estimate=pl.CostEstimate(
            flops=24 * length * length * count * block,
            bytes_accessed=12 * length * count * block,
            transcendentals=length * length * heads // parts,
        ),
    )(*operands)


def rank_nodes(parents_ref, rank_ref, half):
    nodes = rank_ref.shape[0]

    def clear(n, carry):
        rank_ref[n] = 0
        return carry

    def mark(n, carry):
        up = parents_ref[n]

        @pl.when(jnp.logical_and(up >= 0, (up >= half) != (n >= half)))
        def _():
            rank_ref[up] = 1

        return carry

    def place(n, count):
        crosses = rank_ref[n]
        rank_ref[n] = jnp.where(crosses > 0, count, -1)
        return count + crosses

    lax.fori_loop(0, nodes, clear, 0)
    lax.fori_loop(0, nodes, mark, 0)
    lax.fori_loop(0, nodes, place, 0)


def widen(narrow, heads, head_width):
    count = narrow.shape[0]
    flat = jnp.concatenate([narrow[n, :1].astype(f32) for n in range(count)], axis=0)
    return mm(flat.astype(bf16), spread_matrix(LANES, heads * head_width, head_width))


def pack_kernel(
    heads, head_width, parents_ref, recv_ref, main_ref, more_ref, decay_ref, slot_ref, chain_ref, rank_ref
):
    half = recv_ref.shape[0]
    width = heads * head_width
    base = lax.axis_index("node") // half * half
    rank_nodes(parents_ref, rank_ref, half)
    decay_ref[...] = widen(recv_ref[:, :, 2 * width :], heads, head_width)
    slot_ref[...] = jnp.zeros_like(slot_ref)
    chain_ref[...] = jnp.zeros_like(chain_ref)

    def inside(n):
        return jnp.logical_and(n >= base, n < base + half)

    def spot(n):
        return jnp.clip(n - base, 0, half - 1)

    def visit(m, carry):
        node = base + m
        flow = recv_ref[m, :, width : 2 * width].astype(f32)
        at = node
        live = jnp.bool_(True)
        for level in range(LEVELS):
            up = parents_ref[at]
            exists = jnp.logical_and(live, up >= 0)
            live = jnp.logical_and(exists, inside(up))
            away = jnp.logical_and(exists, jnp.logical_not(live))

            @pl.when(away)
            def _(flow=flow, up=up):
                slot = rank_ref[up]
                slot_ref[slot] = slot_ref[slot] + flow

            if level < LEVELS - 1:
                flow = flow * jnp.where(live, decay_ref[pl.ds(spot(up), 1)], 1.0)
            at = jnp.where(live, up, at)

        @pl.when(rank_ref[node] >= 0)
        def _():
            total = recv_ref[m, :, :width].astype(f32)
            factor = decay_ref[pl.ds(m, 1)]
            chain = recv_ref[m, :, 2 * width :].astype(f32)
            at = node
            live = jnp.bool_(True)
            for level in range(LEVELS - 1):
                up = parents_ref[at]
                live = jnp.logical_and(jnp.logical_and(live, up >= 0), inside(up))
                where = spot(up)
                total = total + jnp.where(live, factor * recv_ref[where, :, :width].astype(f32), 0.0)
                factor = factor * jnp.where(live, decay_ref[pl.ds(where, 1)], 1.0)
                chain = chain * jnp.where(live, recv_ref[where, :, 2 * width :].astype(f32), 1.0)
                at = jnp.where(live, up, at)
            slot_ref[rank_ref[node]] = total
            chain_ref[rank_ref[node]] = chain

        return carry

    lax.fori_loop(0, half, visit, 0)
    main = main_ref.shape[0]
    main_ref[:, :, :width] = slot_ref[:main].astype(bf16)
    main_ref[:, :, width:] = chain_ref[:main].astype(bf16)
    more_ref[:, :, :width] = slot_ref[main:].astype(bf16)
    more_ref[:, :, width:] = chain_ref[main:].astype(bf16)


def slot_counts(nodes):
    most = nodes * LEVELS // (LEVELS + 1)
    return most // 2, most - most // 2


def pack_slots(parents, recv, after, nodes, heads, head_width):
    half, rows, _ = recv.shape
    width = heads * head_width
    main, more = slot_counts(nodes)
    in_specs = [pl.BlockSpec(memory_space=pltpu.SMEM), pl.BlockSpec(memory_space=pltpu.VMEM)]
    kernel = functools.partial(pack_kernel, heads, head_width)
    kernel, in_specs, operands, _ = ordered(kernel, in_specs, [parents, recv], after)
    return pl.pallas_call(
        kernel,
        in_specs=in_specs,
        out_specs=[pl.BlockSpec(memory_space=pltpu.VMEM)] * 2,
        out_shape=[
            jax.ShapeDtypeStruct((main, rows, width + LANES), bf16),
            jax.ShapeDtypeStruct((more, rows, width + LANES), bf16),
        ],
        scratch_shapes=[
            pltpu.VMEM((half, width), f32),
            pltpu.VMEM((main + more, rows, width), f32),
            pltpu.VMEM((main + more, rows, LANES), f32),
            pltpu.SMEM((nodes,), jnp.int32),
        ],
        name="pack_slots",
        cost_estimate=pl.CostEstimate(
            flops=20 * half * rows * width,
            bytes_accessed=8 * half * rows * width,
            transcendentals=0,
        ),
    )(*operands)


def join_kernel(
    heads,
    head_width,
    parents_ref,
    recv_ref,
    main_ref,
    more_ref,
    out_ref,
    token_ref,
    decay_ref,
    slot_ref,
    chain_ref,
    back_ref,
    rank_ref,
):
    half = recv_ref.shape[0]
    nodes = rank_ref.shape[0]
    width = heads * head_width
    main = main_ref.shape[0]
    base = lax.axis_index("node") // half * half
    rank_nodes(parents_ref, rank_ref, half)
    decay_ref[...] = widen(recv_ref[:, :, 2 * width :], heads, head_width)
    slot_ref[:main] = main_ref[:, :, :width].astype(f32)
    slot_ref[main:] = more_ref[:, :, :width].astype(f32)
    chain_ref[:main] = widen(main_ref[:, :, width:], heads, head_width)
    chain_ref[main:] = widen(more_ref[:, :, width:], heads, head_width)
    back_ref[...] = jnp.zeros_like(back_ref)

    def inside(n):
        return jnp.logical_and(n >= base, n < base + half)

    def climb(at, flow, start):
        factor = None
        live = jnp.bool_(True)
        for level in range(LEVELS):
            up = parents_ref[at]
            live = jnp.logical_and(live, up >= 0)
            near = jnp.logical_and(live, inside(up))
            far = jnp.logical_and(live, jnp.logical_not(near))
            where = jnp.clip(up - base, 0, half - 1)
            slot = jnp.where(far, rank_ref[jnp.maximum(up, 0)], 0)

            @pl.when(near)
            def _(flow=flow, where=where):
                back_ref[where] = back_ref[where] + flow

            if start is not None:
                value = jnp.where(near, recv_ref[where, :, :width].astype(f32), slot_ref[slot])
                value = jnp.where(live, value, 0.0)
                start = start + (value if factor is None else factor * value)
            if level < LEVELS - 1:
                step = jnp.where(near, decay_ref[pl.ds(where, 1)], chain_ref[pl.ds(slot, 1)])
                flow = flow * step
                factor = step if factor is None else factor * step
                top = jnp.maximum(up, 0)
                for _ in range(LEVELS - 1):
                    above = parents_ref[top]
                    more = jnp.logical_and(far, above >= 0)
                    more = jnp.logical_and(more, jnp.logical_not(inside(above)))
                    top = jnp.where(more, above, top)
                at = top
        return start

    def visit(m, carry):
        node = base + m
        seed = recv_ref[m, :, width : 2 * width].astype(f32)
        start = climb(node, seed, jnp.zeros(seed.shape, f32))
        out_ref[m, :, :width] = start.astype(bf16)

        @pl.when(rank_ref[node] >= 0)
        def _():
            extra = slot_ref[rank_ref[node]]
            back_ref[m] = back_ref[m] + extra
            climb(node, extra * decay_ref[pl.ds(m, 1)], None)

        return carry

    lax.fori_loop(0, half, visit, 0)
    out_ref[:, :, width:] = back_ref[...].astype(bf16)
    token_ref[...] = jnp.zeros_like(token_ref)


def join_slots(parents, recv, main, more, after, nodes, heads, head_width):
    half, rows, _ = recv.shape
    width = heads * head_width
    in_specs = [pl.BlockSpec(memory_space=pltpu.SMEM)] + [pl.BlockSpec(memory_space=pltpu.VMEM)] * 3
    kernel = functools.partial(join_kernel, heads, head_width)
    kernel, in_specs, operands, _ = ordered(kernel, in_specs, [parents, recv, main, more], after)
    slots = main.shape[0] + more.shape[0]
    return pl.pallas_call(
        kernel,
        in_specs=in_specs,
        out_specs=[pl.BlockSpec(memory_space=pltpu.VMEM)] * 2,
        out_shape=[
            jax.ShapeDtypeStruct((half, rows, 2 * width), bf16),
            jax.ShapeDtypeStruct((8, LANES), f32),
        ],
        scratch_shapes=[
            pltpu.VMEM((half, width), f32),
            pltpu.VMEM((slots, rows, width), f32),
            pltpu.VMEM((slots, width), f32),
            pltpu.VMEM((half, rows, width), f32),
            pltpu.SMEM((nodes,), jnp.int32),
        ],
        name="join_slots",
        cost_estimate=pl.CostEstimate(
            flops=20 * half * rows * width,
            bytes_accessed=8 * half * rows * width,
            transcendentals=0,
        ),
    )(*operands)


def outer_kernel(
    heads,
    head_width,
    aliased,
    x_ref,
    cot_ref,
    b_ref,
    c_ref,
    grow_ref,
    tail_ref,
    start_ref,
    back_ref,
    inner_ref,
    grad_ref,
    *refs,
):
    out_ref, gx_ref, gc_ref, gb_ref = refs[2:] if aliased else refs
    block = x_ref.shape[1]
    index = pl.program_id(0)
    pack = LANES // head_width
    firsts = [(index * (block // LANES) + q) * pack for q in range(block // LANES)]
    grow = grow_ref[...]
    tail = tail_ref[...]
    grow_wide = jnp.concatenate([head_lanes(grow, v, head_width) for v in firsts], axis=1)
    tail_wide = jnp.concatenate([head_lanes(tail, v, head_width) for v in firsts], axis=1)
    start = start_ref[...]
    back = back_ref[...]
    out_ref[...] = (inner_ref[...].astype(f32) + grow_wide * mm(c_ref[...], start)).astype(bf16)
    gx_ref[...] = (grad_ref[...].astype(f32) + tail_wide * mm(b_ref[...], back)).astype(bf16)
    emitted = (grow_wide * cot_ref[...].astype(f32)).astype(bf16)
    tailed = (tail_wide * x_ref[...].astype(f32)).astype(bf16)
    gc = mm(emitted, start, NT)
    gb = mm(tailed, back, NT)

    @pl.when(index == 0)
    def _():
        gc_ref[...] = gc
        gb_ref[...] = gb

    @pl.when(index > 0)
    def _():
        gc_ref[...] += gc
        gb_ref[...] += gb


def node_outer(x, cot, b, c, grow, tail, states, inner, grad, prior, chunk, heads, head_width):
    length, state = b.shape
    width = heads * head_width
    block = min(width, 4 * LANES)
    count = width // block
    whole = lambda i: (0, 0)
    spot = lambda i: (0, i)
    place = lambda i: (0, chunk * count + i)
    aliased = prior is not None
    operands = [x, cot, b, c, grow, tail, states, states, inner, grad]
    in_specs = [
        pl.BlockSpec((length, block), place),
        pl.BlockSpec((length, block), place),
        pl.BlockSpec((length, state), whole),
        pl.BlockSpec((length, state), whole),
        pl.BlockSpec((length, LANES), whole),
        pl.BlockSpec((length, LANES), whole),
        pl.BlockSpec((state, block), spot),
        pl.BlockSpec((state, block), lambda i: (0, count + i)),
        pl.BlockSpec((length, block), place),
        pl.BlockSpec((length, block), place),
    ]
    aliases = {}
    if aliased:
        aliases = {len(operands): 0, len(operands) + 1: 1}
        operands += list(prior)
        in_specs += [pl.BlockSpec(memory_space=pl.ANY)] * 2
    return pl.pallas_call(
        functools.partial(outer_kernel, heads, head_width, aliased),
        grid=(count,),
        in_specs=in_specs,
        out_specs=[
            pl.BlockSpec((length, block), place),
            pl.BlockSpec((length, block), place),
            pl.BlockSpec((length, state), whole),
            pl.BlockSpec((length, state), whole),
        ],
        out_shape=[
            jax.ShapeDtypeStruct(x.shape, bf16),
            jax.ShapeDtypeStruct(x.shape, bf16),
            jax.ShapeDtypeStruct((length, state), f32),
            jax.ShapeDtypeStruct((length, state), f32),
        ],
        input_output_aliases=aliases,
        name="node_outer",
        cost_estimate=pl.CostEstimate(
            flops=8 * length * state * width,
            bytes_accessed=16 * length * width,
            transcendentals=0,
        ),
    )(*operands)


def scatter_sum(parts):
    size = lax.axis_size("head")
    me = lax.axis_index("head")
    rows = parts.shape[1] // size
    total = lax.dynamic_slice_in_dim(parts, me * rows, rows, axis=1)
    for shift in range(1, size):
        target = (me + shift) % size
        piece = lax.dynamic_slice_in_dim(parts, target * rows, rows, axis=1).astype(bf16)
        moved = lax.ppermute(piece, "head", [(i, (i + shift) % size) for i in range(size)])
        total = total + moved.astype(f32)
    return total


def on_device(inputs, b_matrix, c_matrix, step_size, decay_rate, parents, cotangent):
    state = b_matrix.shape[1]
    head_count = step_size.shape[0]
    head_width = inputs.shape[1] // head_count
    nodes = lax.axis_size("node")
    heads = head_count // CHUNKS
    half = nodes // 2
    rate = decay_rate[None, :]
    groups = [list(range(half)), list(range(half, nodes))]
    across = [(n, (n + half) % nodes) for n in range(nodes)]

    def swap(v):
        return lax.all_to_all(
            v.reshape(half, state // half, v.shape[-1]),
            "node",
            split_axis=0,
            concat_axis=0,
            tiled=True,
            axis_index_groups=groups,
        )

    def cross(v):
        return lax.ppermute(v, "node", across)

    places = jnp.arange(nodes)
    child = jnp.logical_and(
        parents[:, None] == places[None, :], (places[:, None] < half) != (places[None, :] < half)
    )
    crossing = jnp.sum(jnp.any(child, axis=0).astype(jnp.int32))
    crowded = crossing > slot_counts(nodes)[0]

    shared = (inputs, cotangent, b_matrix, c_matrix)
    sizes = (heads, head_width)
    made = [node_states(*shared, step_size, rate, k, *sizes) for k in range(CHUNKS)]
    received = [swap(made[k][0]) for k in range(CHUNKS)]
    grads_found = []
    prior = None
    token = made[CHUNKS - 1][1]

    def inner_part(prior, token, k, part):
        *prior, gc, gb = node_inner(
            *shared, made[0][5], made[k][1], made[k][2], prior, token, k, part, PARTS, *sizes
        )
        grads_found.append((gb, gc))
        return prior, gc

    todo = [(k, part) for k in range(CHUNKS) for part in range(PARTS)]
    packed = []
    for k in range(CHUNKS):
        prior, token = inner_part(prior, token, *todo.pop(0))
        main, more = pack_slots(parents, received[k], token, nodes, *sizes)
        packed.append((main, more, cross(main)))
        token = more
    others = lax.cond(
        crowded,
        lambda vs: tuple(cross(v) for v in vs),
        lambda vs: vs,
        tuple(p[1] for p in packed),
    )
    states = []
    for k in range(CHUNKS):
        joined, token = join_slots(
            parents, received[k], packed[k][2], others[k], token, nodes, *sizes
        )
        states.append(swap(joined).reshape(state, -1))
        prior, token = inner_part(prior, token, *todo.pop(0))
    inner = prior
    prior = None
    for k in range(CHUNKS):
        *prior, gc, gb = node_outer(
            *shared, made[k][3], made[k][4], states[k], *inner, prior, k, *sizes
        )
        grads_found.append((gb, gc))
    grad_b = sum(g[0] for g in grads_found)
    grad_c = sum(g[1] for g in grads_found)
    grads = scatter_sum(jnp.stack([grad_b, grad_c]))
    return prior[0], prior[1], grads[0], grads[1]


def solution(mesh):
    return jax.shard_map(
        on_device,
        mesh=mesh,
        in_specs=(
            P("node", "head"),
            P("node", None),
            P("node", None),
            P("head", "node"),
            P("head"),
            P(),
            P("node", "head"),
        ),
        out_specs=(
            P("node", "head"),
            P("node", "head"),
            P(("node", "head"), None),
            P(("node", "head"), None),
        ),
        check_vma=False,
    )
```

```python
import functools
import math

import jax
import jax.numpy as jnp
from jax import lax
from jax.experimental import pallas as pl
from jax.experimental.pallas import tpu as pltpu
from jax.sharding import PartitionSpec as P


LEVELS = 3
VMEM_BYTES = 24 << 20
LANES = 128
CHUNKS = 2
PARTS = 2

LOG2E = 1.0 / math.log(2.0)

f32 = jnp.float32
bf16 = jnp.bfloat16
NN = (((1,), (0,)), ((), ()))
NT = (((1,), (1,)), ((), ()))


def mm(a, b, dims=NN):
    return lax.dot_general(a, b, dims, preferred_element_type=f32)


def ordered(kernel, in_specs, operands, after, aliases=None):
    if after is None:
        return kernel, in_specs, operands, aliases or {}

    def body(after_ref, *refs):
        kernel(*refs)

    shifted = {key + 1: value for key, value in (aliases or {}).items()}
    return body, [pl.BlockSpec(memory_space=pl.ANY)] + in_specs, [after] + operands, shifted


def split_two(v):
    high = v.astype(bf16)
    return high, (v - high.astype(f32)).astype(bf16)


def spread_matrix(rows, width, head_width, offset=0):
    row = lax.broadcasted_iota(jnp.int32, (rows, width), 0)
    lane = (lax.broadcasted_iota(jnp.int32, (rows, width), 1) + offset) // head_width
    return (row == lane).astype(bf16)


def head_lanes(columns, first, head_width):
    lane = lax.broadcasted_iota(jnp.int32, columns.shape, 1) // head_width + first
    return jnp.take_along_axis(columns, lane, axis=1)


def pad_lanes(v):
    gap = LANES - v.shape[0]
    if gap:
        v = jnp.concatenate([v, jnp.zeros((gap, v.shape[1]), v.dtype)], axis=0)
    return v.T


def states_kernel(
    heads,
    head_width,
    chunk,
    x_ref,
    cot_ref,
    b_ref,
    c_ref,
    step_ref,
    rate_ref,
    send_ref,
    low_ref,
    src_ref,
    grow_ref,
    tail_ref,
    gram_ref,
    bt_ref,
    ct_ref,
):
    block = x_ref.shape[1]
    length = step_ref.shape[1]
    index = pl.program_id(0)
    width = heads * head_width

    @pl.when(index == 0)
    def _():
        step = step_ref[...]
        rates = jnp.broadcast_to(rate_ref[...], (LANES, rate_ref.shape[1])).T
        terms = -step * rates[chunk * heads : (chunk + 1) * heads, :1]
        row = lax.broadcasted_iota(jnp.int32, (length, length), 0)
        col = lax.broadcasted_iota(jnp.int32, (length, length), 1)
        upper = (row <= col).astype(bf16)
        first = terms.astype(bf16)
        rest = terms - first.astype(f32)
        second, third = split_two(rest)
        cumulative = mm(third, upper) + mm(second, upper) + mm(first, upper)
        last = cumulative[:, length - 1 :]
        low_ref[...] = pad_lanes(cumulative * LOG2E)
        src_ref[...] = (cumulative - jnp.log(step)) * LOG2E
        grow_ref[...] = pad_lanes(jnp.exp(cumulative)).astype(bf16)
        tail_ref[...] = pad_lanes(jnp.exp(last - cumulative) * step).astype(bf16)
        bt_ref[...] = b_ref[...].T
        ct_ref[...] = c_ref[...].T
        total = jnp.exp(jnp.broadcast_to(last, (heads, send_ref.shape[0])))
        send_ref[:, 2 * width :] = pad_lanes(total).astype(bf16)
        gram_ref[...] = mm(c_ref[...], b_ref[...], NT).astype(bf16)

    spread = spread_matrix(LANES, block, head_width, index * block)
    tailed = mm(tail_ref[...], spread).astype(bf16) * x_ref[...]
    emitted = mm(grow_ref[...], spread).astype(bf16) * cot_ref[...]
    at = pl.multiple_of(index * block, block)
    send_ref[:, pl.ds(at, block)] = mm(bt_ref[...], tailed).astype(bf16)
    send_ref[:, pl.ds(at + width, block)] = mm(ct_ref[...], emitted).astype(bf16)


def node_states(x, cot, b, c, step, rate, chunk, heads, head_width):
    length, state = b.shape
    width = heads * head_width
    block = min(width, 4 * LANES)
    count = width // block
    whole = lambda i: (0, 0)
    return pl.pallas_call(
        functools.partial(states_kernel, heads, head_width, chunk),
        grid=(count,),
        in_specs=[
            pl.BlockSpec((length, block), lambda i: (0, chunk * count + i)),
            pl.BlockSpec((length, block), lambda i: (0, chunk * count + i)),
            pl.BlockSpec((length, state), whole),
            pl.BlockSpec((length, state), whole),
            pl.BlockSpec((heads, length), lambda i: (chunk, 0)),
            pl.BlockSpec(rate.shape, whole),
        ],
        out_specs=[
            pl.BlockSpec((state, 2 * width + LANES), whole),
            pl.BlockSpec((length, LANES), whole),
            pl.BlockSpec((heads, length), whole),
            pl.BlockSpec((length, LANES), whole),
            pl.BlockSpec((length, LANES), whole),
            pl.BlockSpec((length, length), whole),
        ],
        out_shape=[
            jax.ShapeDtypeStruct((state, 2 * width + LANES), bf16),
            jax.ShapeDtypeStruct((length, LANES), f32),
            jax.ShapeDtypeStruct((heads, length), f32),
            jax.ShapeDtypeStruct((length, LANES), bf16),
            jax.ShapeDtypeStruct((length, LANES), bf16),
            jax.ShapeDtypeStruct((length, length), bf16),
        ],
        scratch_shapes=[pltpu.VMEM((state, length), bf16), pltpu.VMEM((state, length), bf16)],
        name="node_states",
        cost_estimate=pl.CostEstimate(
            flops=4 * length * state * width,
            bytes_accessed=4 * length * width + 4 * state * width,
            transcendentals=0,
        ),
    )(x, cot, b, c, step, rate)


def inner_kernel(
    head_width,
    first,
    aliased,
    x_ref,
    cot_ref,
    b_ref,
    c_ref,
    given_ref,
    low_ref,
    src_ref,
    *refs,
):
    if aliased:
        refs = refs[2:]
    out_ref, grad_ref, gc_ref, gb_ref, mixed_ref, turned_ref, wa_ref, wb_ref, gram_ref = refs
    length = x_ref.shape[0]
    index = pl.program_id(0)
    pack = LANES // head_width
    pairs = x_ref.shape[1] // LANES
    wide = 2 * LANES
    tiles = length // wide
    weights = (wa_ref, wb_ref)

    @pl.when(index == 0)
    def _():
        gram_ref[...] = given_ref[...]
        mixed_ref[...] = jnp.zeros_like(mixed_ref)
        for ref in weights:
            ref[...] = jnp.zeros_like(ref)

    lane = lax.broadcasted_iota(jnp.int32, (1, LANES), 1) // head_width
    causal = lax.broadcasted_iota(jnp.int32, (LANES, LANES), 0) >= lax.broadcasted_iota(
        jnp.int32, (LANES, LANES), 1
    )
    xs = [x_ref[:, q * LANES : (q + 1) * LANES] for q in range(pairs)]
    turned_cots = [cot_ref[:, q * LANES : (q + 1) * LANES].T for q in range(pairs)]
    low = low_ref[...]

    def decays(h):
        q, a = h // pack, h % pack
        w = weights[h % 2]
        cot = cot_ref[:, q * LANES : (q + 1) * LANES]
        cot = jnp.where(lane == a, cot, jnp.zeros_like(cot))
        place = (first + index * pairs + q) * pack + a
        column = head_lanes(low, place, LANES)
        source = src_ref[pl.ds(place, 1), :]
        for tile in range(tiles):
            scores = mm(cot[tile * wide :], xs[q][tile * wide : (tile + 1) * wide], NT)
            for i in range(2 * tile, 2 * tiles):
                rows = slice(i * LANES, (i + 1) * LANES)
                here = slice((i - 2 * tile) * LANES, (i - 2 * tile + 1) * LANES)
                for j in range(2 * tile, min(2 * tile + 1, i) + 1):
                    cols = slice(j * LANES, (j + 1) * LANES)
                    side = slice((j - 2 * tile) * LANES, (j - 2 * tile + 1) * LANES)
                    differ = column[rows] - source[:, cols]
                    if i == j:
                        differ = jnp.where(causal, differ, -jnp.inf)
                    decay = jnp.exp2(differ)
                    w[rows, cols] = decay.astype(bf16) * gram_ref[rows, cols]
                    mixed_ref[rows, cols] += decay * scores[here, side]
                yield

    def products(h):
        q, a = h // pack, h % pack
        w = weights[h % 2]
        x = xs[q]
        part = turned_cots[q][a * head_width : (a + 1) * head_width]
        mine = slice(q * LANES + a * head_width, q * LANES + (a + 1) * head_width)
        own = slice(a * head_width, (a + 1) * head_width)
        for tile in range(tiles):
            rows = slice(tile * wide, (tile + 1) * wide)
            found = mm(w[rows, : (tile + 1) * wide], x[: (tile + 1) * wide])
            out_ref[rows, mine] = found[:, own].astype(bf16)
            yield
            found = mm(part[:, tile * wide :], w[tile * wide :, rows])
            turned_ref[mine, rows] = found.astype(bf16)
            yield

    def finish(q):
        lanes = slice(q * LANES, (q + 1) * LANES)
        grad_ref[:, lanes] = turned_ref[lanes, :].T

    before = None
    for h in range(pairs * pack):
        for _ in decays(h):
            if before is not None:
                next(before, None)
        if before is not None:
            for _ in before:
                pass
            if h % pack == 0:
                finish(h // pack - 1)
        before = products(h)
    for _ in before:
        pass
    finish(pairs - 1)

    @pl.when(index == pl.num_programs(0) - 1)
    def _():
        mixed = mixed_ref[...].astype(bf16)
        gc_ref[...] = mm(mixed, b_ref[...])
        gb_ref[...] = mm(mixed.T, c_ref[...])


def node_inner(x, cot, b, c, gram, low, src, prior, after, chunk, part, parts, heads, head_width):
    length, state = b.shape
    width = heads * head_width
    block = min(width // parts, 2 * LANES)
    count = width // block // parts
    offset = (chunk * parts + part) * count
    whole = lambda i: (0, 0)
    place = lambda i: (0, offset + i)
    aliased = prior is not None
    operands = [x, cot, b, c, gram, low, src]
    in_specs = [
        pl.BlockSpec((length, block), place),
        pl.BlockSpec((length, block), place),
        pl.BlockSpec((length, state), whole),
        pl.BlockSpec((length, state), whole),
        pl.BlockSpec((length, length), whole),
        pl.BlockSpec((length, LANES), whole),
        pl.BlockSpec((heads, length), whole),
    ]
    aliases = {}
    if aliased:
        aliases = {len(operands): 0, len(operands) + 1: 1}
        operands += list(prior)
        in_specs += [pl.BlockSpec(memory_space=pl.ANY)] * 2
    kernel = functools.partial(inner_kernel, head_width, part * count * block // LANES, aliased)
    kernel, in_specs, operands, aliases = ordered(kernel, in_specs, operands, after, aliases)
    return pl.pallas_call(
        kernel,
        grid=(count,),
        in_specs=in_specs,
        out_specs=[
            pl.BlockSpec((length, block), place),
            pl.BlockSpec((length, block), place),
            pl.BlockSpec((length, state), whole),
            pl.BlockSpec((length, state), whole),
        ],
        out_shape=[
            jax.ShapeDtypeStruct(x.shape, bf16),
            jax.ShapeDtypeStruct(x.shape, bf16),
            jax.ShapeDtypeStruct((length, state), f32),
            jax.ShapeDtypeStruct((length, state), f32),
        ],
        scratch_shapes=[
            pltpu.VMEM((length, length), f32),
            pltpu.VMEM((block, length), bf16),
            pltpu.VMEM((length, length), bf16),
            pltpu.VMEM((length, length), bf16),
            pltpu.VMEM((length, length), bf16),
        ],
        input_output_aliases=aliases,
        name="node_inner",
        cost_estimate=pl.CostEstimate(
            flops=24 * length * length * count * block,
            bytes_accessed=12 * length * count * block,
            transcendentals=length * length * heads // parts,
        ),
    )(*operands)


def rank_nodes(parents_ref, rank_ref, half):
    nodes = rank_ref.shape[0]

    def clear(n, carry):
        rank_ref[n] = 0
        return carry

    def mark(n, carry):
        up = parents_ref[n]

        @pl.when(jnp.logical_and(up >= 0, (up >= half) != (n >= half)))
        def _():
            rank_ref[up] = 1

        return carry

    def place(n, count):
        crosses = rank_ref[n]
        rank_ref[n] = jnp.where(crosses > 0, count, -1)
        return count + crosses

    lax.fori_loop(0, nodes, clear, 0)
    lax.fori_loop(0, nodes, mark, 0)
    lax.fori_loop(0, nodes, place, 0)


def widen(narrow, heads, head_width):
    count = narrow.shape[0]
    flat = jnp.concatenate([narrow[n, :1].astype(f32) for n in range(count)], axis=0)
    return mm(flat.astype(bf16), spread_matrix(LANES, heads * head_width, head_width))


def pack_kernel(
    heads, head_width, parents_ref, recv_ref, main_ref, more_ref, decay_ref, slot_ref, chain_ref, rank_ref
):
    half = recv_ref.shape[0]
    width = heads * head_width
    base = lax.axis_index("node") // half * half
    rank_nodes(parents_ref, rank_ref, half)
    decay_ref[...] = widen(recv_ref[:, :, 2 * width :], heads, head_width)
    slot_ref[...] = jnp.zeros_like(slot_ref)
    chain_ref[...] = jnp.zeros_like(chain_ref)

    def inside(n):
        return jnp.logical_and(n >= base, n < base + half)

    def spot(n):
        return jnp.clip(n - base, 0, half - 1)

    def visit(m, carry):
        node = base + m
        flow = recv_ref[m, :, width : 2 * width].astype(f32)
        at = node
        live = jnp.bool_(True)
        for level in range(LEVELS):
            up = parents_ref[at]
            exists = jnp.logical_and(live, up >= 0)
            live = jnp.logical_and(exists, inside(up))
            away = jnp.logical_and(exists, jnp.logical_not(live))

            @pl.when(away)
            def _(flow=flow, up=up):
                slot = rank_ref[up]
                slot_ref[slot] = slot_ref[slot] + flow

            if level < LEVELS - 1:
                flow = flow * jnp.where(live, decay_ref[pl.ds(spot(up), 1)], 1.0)
            at = jnp.where(live, up, at)

        @pl.when(rank_ref[node] >= 0)
        def _():
            total = recv_ref[m, :, :width].astype(f32)
            factor = decay_ref[pl.ds(m, 1)]
            chain = recv_ref[m, :, 2 * width :].astype(f32)
            at = node
            live = jnp.bool_(True)
            for _ in range(LEVELS - 1):
                up = parents_ref[at]
                live = jnp.logical_and(jnp.logical_and(live, up >= 0), inside(up))
                where = spot(up)
                total = total + jnp.where(live, factor * recv_ref[where, :, :width].astype(f32), 0.0)
                factor = factor * jnp.where(live, decay_ref[pl.ds(where, 1)], 1.0)
                chain = chain * jnp.where(live, recv_ref[where, :, 2 * width :].astype(f32), 1.0)
                at = jnp.where(live, up, at)
            slot_ref[rank_ref[node]] = total
            chain_ref[rank_ref[node]] = chain

        return carry

    lax.fori_loop(0, half, visit, 0)
    main = main_ref.shape[0]
    main_ref[:, :, :width] = slot_ref[:main].astype(bf16)
    main_ref[:, :, width:] = chain_ref[:main].astype(bf16)
    more_ref[:, :, :width] = slot_ref[main:].astype(bf16)
    more_ref[:, :, width:] = chain_ref[main:].astype(bf16)


def slot_counts(nodes):
    most = nodes * LEVELS // (LEVELS + 1)
    return most // 2, most - most // 2


def pack_slots(parents, recv, after, nodes, heads, head_width):
    half, rows, _ = recv.shape
    width = heads * head_width
    main, more = slot_counts(nodes)
    in_specs = [pl.BlockSpec(memory_space=pltpu.SMEM), pl.BlockSpec(memory_space=pltpu.VMEM)]
    kernel = functools.partial(pack_kernel, heads, head_width)
    kernel, in_specs, operands, _ = ordered(kernel, in_specs, [parents, recv], after)
    return pl.pallas_call(
        kernel,
        in_specs=in_specs,
        out_specs=[pl.BlockSpec(memory_space=pltpu.VMEM)] * 2,
        out_shape=[
            jax.ShapeDtypeStruct((main, rows, width + LANES), bf16),
            jax.ShapeDtypeStruct((more, rows, width + LANES), bf16),
        ],
        scratch_shapes=[
            pltpu.VMEM((half, width), f32),
            pltpu.VMEM((main + more, rows, width), f32),
            pltpu.VMEM((main + more, rows, LANES), f32),
            pltpu.SMEM((nodes,), jnp.int32),
        ],
        compiler_params=pltpu.CompilerParams(vmem_limit_bytes=VMEM_BYTES),
        name="pack_slots",
        cost_estimate=pl.CostEstimate(
            flops=20 * half * rows * width,
            bytes_accessed=8 * half * rows * width,
            transcendentals=0,
        ),
    )(*operands)


def join_kernel(
    heads,
    head_width,
    parents_ref,
    recv_ref,
    main_ref,
    more_ref,
    out_ref,
    token_ref,
    decay_ref,
    slot_ref,
    chain_ref,
    back_ref,
    rank_ref,
):
    half = recv_ref.shape[0]
    width = heads * head_width
    main = main_ref.shape[0]
    base = lax.axis_index("node") // half * half
    rank_nodes(parents_ref, rank_ref, half)
    decay_ref[...] = widen(recv_ref[:, :, 2 * width :], heads, head_width)
    slot_ref[:main] = main_ref[:, :, :width].astype(f32)
    slot_ref[main:] = more_ref[:, :, :width].astype(f32)
    chain_ref[:main] = widen(main_ref[:, :, width:], heads, head_width)
    chain_ref[main:] = widen(more_ref[:, :, width:], heads, head_width)
    back_ref[...] = jnp.zeros_like(back_ref)

    def inside(n):
        return jnp.logical_and(n >= base, n < base + half)

    def climb(at, flow, start):
        factor = None
        live = jnp.bool_(True)
        for level in range(LEVELS):
            up = parents_ref[at]
            live = jnp.logical_and(live, up >= 0)
            near = jnp.logical_and(live, inside(up))
            far = jnp.logical_and(live, jnp.logical_not(near))
            where = jnp.clip(up - base, 0, half - 1)
            slot = jnp.where(far, rank_ref[jnp.maximum(up, 0)], 0)

            @pl.when(near)
            def _(flow=flow, where=where):
                back_ref[where] = back_ref[where] + flow

            if start is not None:
                value = jnp.where(near, recv_ref[where, :, :width].astype(f32), slot_ref[slot])
                value = jnp.where(live, value, 0.0)
                start = start + (value if factor is None else factor * value)
            if level < LEVELS - 1:
                step = jnp.where(near, decay_ref[pl.ds(where, 1)], chain_ref[pl.ds(slot, 1)])
                flow = flow * step
                factor = step if factor is None else factor * step
                top = jnp.maximum(up, 0)
                for _ in range(LEVELS - 1):
                    above = parents_ref[top]
                    more = jnp.logical_and(far, above >= 0)
                    more = jnp.logical_and(more, jnp.logical_not(inside(above)))
                    top = jnp.where(more, above, top)
                at = top
        return start

    def visit(m, carry):
        node = base + m
        seed = recv_ref[m, :, width : 2 * width].astype(f32)
        start = climb(node, seed, jnp.zeros(seed.shape, f32))
        out_ref[m, :, :width] = start.astype(bf16)

        @pl.when(rank_ref[node] >= 0)
        def _():
            extra = slot_ref[rank_ref[node]]
            back_ref[m] = back_ref[m] + extra
            climb(node, extra * decay_ref[pl.ds(m, 1)], None)

        return carry

    lax.fori_loop(0, half, visit, 0)
    out_ref[:, :, width:] = back_ref[...].astype(bf16)
    token_ref[...] = jnp.zeros_like(token_ref)


def join_slots(parents, recv, main, more, after, nodes, heads, head_width):
    half, rows, _ = recv.shape
    width = heads * head_width
    in_specs = [pl.BlockSpec(memory_space=pltpu.SMEM)] + [pl.BlockSpec(memory_space=pltpu.VMEM)] * 3
    kernel = functools.partial(join_kernel, heads, head_width)
    kernel, in_specs, operands, _ = ordered(kernel, in_specs, [parents, recv, main, more], after)
    slots = main.shape[0] + more.shape[0]
    return pl.pallas_call(
        kernel,
        in_specs=in_specs,
        out_specs=[pl.BlockSpec(memory_space=pltpu.VMEM)] * 2,
        out_shape=[
            jax.ShapeDtypeStruct((half, rows, 2 * width), bf16),
            jax.ShapeDtypeStruct((8, LANES), f32),
        ],
        scratch_shapes=[
            pltpu.VMEM((half, width), f32),
            pltpu.VMEM((slots, rows, width), f32),
            pltpu.VMEM((slots, width), f32),
            pltpu.VMEM((half, rows, width), f32),
            pltpu.SMEM((nodes,), jnp.int32),
        ],
        compiler_params=pltpu.CompilerParams(vmem_limit_bytes=VMEM_BYTES),
        name="join_slots",
        cost_estimate=pl.CostEstimate(
            flops=20 * half * rows * width,
            bytes_accessed=8 * half * rows * width,
            transcendentals=0,
        ),
    )(*operands)


def outer_kernel(
    head_width,
    extras,
    final,
    x_ref,
    cot_ref,
    b_ref,
    c_ref,
    grow_ref,
    tail_ref,
    start_ref,
    back_ref,
    inner_ref,
    grad_ref,
    *refs,
):
    added = refs[: 2 * extras]
    refs = refs[2 * extras :]
    if not final:
        out_ref, gx_ref, gc_ref, gb_ref = refs
    else:
        out_ref, gx_ref, own_ref = refs[2:5]
        pieces = refs[5:-2]
        gc_ref, gb_ref = refs[-2:]
    block = x_ref.shape[1]
    index = pl.program_id(0)

    @pl.when(index == 0)
    def _():
        gc_ref[...] = sum(ref[...] for ref in added[:extras])
        gb_ref[...] = sum(ref[...] for ref in added[extras:])

    spread = spread_matrix(LANES, block, head_width, index * block)
    grow_wide = mm(grow_ref[...], spread)
    tail_wide = mm(tail_ref[...], spread)
    start = start_ref[...]
    back = back_ref[...]
    out_ref[...] = (inner_ref[...].astype(f32) + grow_wide * mm(c_ref[...], start)).astype(bf16)
    gx_ref[...] = (grad_ref[...].astype(f32) + tail_wide * mm(b_ref[...], back)).astype(bf16)
    gc_ref[...] += mm(grow_wide.astype(bf16) * cot_ref[...], start, NT)
    gb_ref[...] += mm(tail_wide.astype(bf16) * x_ref[...], back, NT)

    if final:

        @pl.when(index == pl.num_programs(0) - 1)
        def _():
            size = len(pieces) + 1
            me = lax.axis_index("head")
            rows = own_ref.shape[1]
            for shift in range(size):
                at = pl.multiple_of(lax.rem(me + shift, size) * rows, rows)
                for n, ref in enumerate((gb_ref, gc_ref)):
                    if shift == 0:
                        own_ref[n] = ref[pl.ds(at, rows)]
                    else:
                        pieces[shift - 1][n] = ref[pl.ds(at, rows)].astype(bf16)


def node_outer(x, cot, b, c, grow, tail, states, inner, grad, found, prior, chunk, heads, head_width):
    length, state = b.shape
    width = heads * head_width
    block = min(width, 4 * LANES)
    count = width // block
    whole = lambda i: (0, 0)
    spot = lambda i: (0, i)
    place = lambda i: (0, chunk * count + i)
    final = prior is not None
    operands = [x, cot, b, c, grow, tail, states, states, inner, grad]
    in_specs = [
        pl.BlockSpec((length, block), place),
        pl.BlockSpec((length, block), place),
        pl.BlockSpec((length, state), whole),
        pl.BlockSpec((length, state), whole),
        pl.BlockSpec((length, LANES), whole),
        pl.BlockSpec((length, LANES), whole),
        pl.BlockSpec((state, block), spot),
        pl.BlockSpec((state, block), lambda i: (0, count + i)),
        pl.BlockSpec((length, block), place),
        pl.BlockSpec((length, block), place),
    ]
    operands += [v[1] for v in found] + [v[0] for v in found]
    in_specs += [pl.BlockSpec((length, state), whole)] * (2 * len(found))
    out_specs = [pl.BlockSpec((length, block), place)] * 2
    out_shape = [jax.ShapeDtypeStruct(x.shape, bf16)] * 2
    grads = jax.ShapeDtypeStruct((length, state), f32)
    scratch = []
    aliases = {}
    if final:
        aliases = {len(operands): 0, len(operands) + 1: 1}
        operands += list(prior)
        in_specs += [pl.BlockSpec(memory_space=pl.ANY)] * 2
        size = lax.axis_size("head")
        kept = (2, length // size, state)
        cube = lambda i: (0, 0, 0)
        out_specs += [pl.BlockSpec(kept, cube)] * size
        out_shape += [jax.ShapeDtypeStruct(kept, f32)]
        out_shape += [jax.ShapeDtypeStruct(kept, bf16)] * (size - 1)
        scratch = [pltpu.VMEM((length, state), f32)] * 2
    else:
        out_specs += [pl.BlockSpec((length, state), whole)] * 2
        out_shape += [grads] * 2
    return pl.pallas_call(
        functools.partial(outer_kernel, head_width, len(found), final),
        grid=(count,),
        in_specs=in_specs,
        out_specs=out_specs,
        out_shape=out_shape,
        scratch_shapes=scratch,
        input_output_aliases=aliases,
        name="node_outer",
        cost_estimate=pl.CostEstimate(
            flops=8 * length * state * width,
            bytes_accessed=12 * length * width,
            transcendentals=0,
        ),
    )(*operands)


def scatter_sum(own, pieces):
    size = lax.axis_size("head")
    for shift, piece in enumerate(pieces, 1):
        pairs = [(i, (i + shift) % size) for i in range(size)]
        own = own + lax.ppermute(piece, "head", pairs).astype(f32)
    return own


def one_device(inputs, b_matrix, c_matrix, step_size, decay_rate, parents, cotangent):
    state = b_matrix.shape[1]
    head_count = step_size.shape[0]
    head_width = inputs.shape[1] // head_count
    nodes = lax.axis_size("node")
    heads = head_count // CHUNKS
    half = nodes // 2
    rate = decay_rate[None, :]
    groups = [list(range(half)), list(range(half, nodes))]
    across = [(n, (n + half) % nodes) for n in range(nodes)]

    def swap(v):
        return lax.all_to_all(
            v.reshape(half, state // half, v.shape[-1]),
            "node",
            split_axis=0,
            concat_axis=0,
            tiled=True,
            axis_index_groups=groups,
        )

    def cross(v):
        return lax.ppermute(v, "node", across)

    places = jnp.arange(nodes)
    child = jnp.logical_and(
        parents[:, None] == places[None, :], (places[:, None] < half) != (places[None, :] < half)
    )
    crossing = jnp.sum(jnp.any(child, axis=0).astype(jnp.int32))
    crowded = crossing > slot_counts(nodes)[0]

    shared = (inputs, cotangent, b_matrix, c_matrix)
    sizes = (heads, head_width)
    made = [node_states(*shared, step_size, rate, k, *sizes) for k in range(CHUNKS)]
    received = [swap(made[k][0]) for k in range(CHUNKS)]
    found = []
    prior = None
    token = made[CHUNKS - 1][1]

    def inner_part(prior, token, k, part):
        *prior, gc, gb = node_inner(
            *shared, made[0][5], made[k][1], made[k][2], prior, token, k, part, PARTS, *sizes
        )
        found.append((gb, gc))
        return prior, gc

    todo = [(k, part) for k in range(CHUNKS) for part in range(PARTS)]
    packed = []
    for k in range(CHUNKS):
        prior, token = inner_part(prior, token, *todo.pop(0))
        main, more = pack_slots(parents, received[k], token, nodes, *sizes)
        packed.append((main, more, cross(main)))
        token = more
    others = lax.cond(
        crowded,
        lambda vs: tuple(cross(v) for v in vs),
        lambda vs: vs,
        tuple(p[1] for p in packed),
    )
    states = []
    for k in range(CHUNKS):
        joined, token = join_slots(
            parents, received[k], packed[k][2], others[k], token, nodes, *sizes
        )
        states.append(swap(joined).reshape(state, -1))
        prior, token = inner_part(prior, token, *todo.pop(0))
    inner = prior
    prior = None
    for k in range(CHUNKS):
        result = node_outer(
            *shared, made[k][3], made[k][4], states[k], *inner, found, prior, k, *sizes
        )
        prior = result[:2]
        if k == 0:
            found = [(result[3], result[2])]
    grads = scatter_sum(result[2], result[3:])
    return prior[0], prior[1], grads[0], grads[1]


def solution(mesh):
    return jax.shard_map(
        one_device,
        mesh=mesh,
        in_specs=(
            P("node", "head"),
            P("node", None),
            P("node", None),
            P("head", "node"),
            P("head"),
            P(),
            P("node", "head"),
        ),
        out_specs=(
            P("node", "head"),
            P("node", "head"),
            P(("node", "head"), None),
            P(("node", "head"), None),
        ),
        check_vma=False,
    )
```

```python
import functools
import math

import jax
import jax.numpy as jnp
from jax import lax
from jax.experimental import pallas as pl
from jax.experimental.pallas import tpu as pltpu
from jax.sharding import PartitionSpec as P


LEVELS = 3
VMEM_BYTES = 24 << 20
LANES = 128
CHUNKS = 2
PARTS = 2

LOG2E = 1.0 / math.log(2.0)

f32 = jnp.float32
bf16 = jnp.bfloat16
NN = (((1,), (0,)), ((), ()))
NT = (((1,), (1,)), ((), ()))


def mm(a, b, dims=NN):
    return lax.dot_general(a, b, dims, preferred_element_type=f32)


def split_two(v):
    high = v.astype(bf16)
    return high, (v - high.astype(f32)).astype(bf16)


def spread_matrix(rows, width, head_width, offset=0):
    row = lax.broadcasted_iota(jnp.int32, (rows, width), 0)
    lane = (lax.broadcasted_iota(jnp.int32, (rows, width), 1) + offset) // head_width
    return (row == lane).astype(bf16)


def head_lanes(columns, first, head_width):
    lane = lax.broadcasted_iota(jnp.int32, columns.shape, 1) // head_width + first
    return jnp.take_along_axis(columns, lane, axis=1)


def pad_lanes(v):
    gap = LANES - v.shape[0]
    if gap:
        v = jnp.concatenate([v, jnp.zeros((gap, v.shape[1]), v.dtype)], axis=0)
    return v.T


def states_kernel(
    heads,
    head_width,
    chunk,
    x_ref,
    cot_ref,
    b_ref,
    c_ref,
    step_ref,
    rate_ref,
    send_ref,
    low_ref,
    src_ref,
    grow_ref,
    tail_ref,
    gram_ref,
    bt_ref,
    ct_ref,
):
    block = x_ref.shape[1]
    length = step_ref.shape[1]
    index = pl.program_id(0)
    width = heads * head_width

    @pl.when(index == 0)
    def _():
        step = step_ref[...]
        rates = jnp.broadcast_to(rate_ref[...], (LANES, rate_ref.shape[1])).T
        terms = -step * rates[chunk * heads : (chunk + 1) * heads, :1]
        row = lax.broadcasted_iota(jnp.int32, (length, length), 0)
        col = lax.broadcasted_iota(jnp.int32, (length, length), 1)
        upper = (row <= col).astype(bf16)
        first = terms.astype(bf16)
        rest = terms - first.astype(f32)
        second, third = split_two(rest)
        cumulative = mm(third, upper) + mm(second, upper) + mm(first, upper)
        last = cumulative[:, length - 1 :]
        low_ref[...] = pad_lanes(cumulative * LOG2E)
        src_ref[...] = (cumulative - jnp.log(step)) * LOG2E
        grow_ref[...] = pad_lanes(jnp.exp(cumulative)).astype(bf16)
        tail_ref[...] = pad_lanes(jnp.exp(last - cumulative) * step).astype(bf16)
        bt_ref[...] = b_ref[...].T
        ct_ref[...] = c_ref[...].T
        total = jnp.exp(jnp.broadcast_to(last, (heads, send_ref.shape[0])))
        send_ref[:, 2 * width :] = pad_lanes(total).astype(bf16)
        gram_ref[...] = mm(c_ref[...], b_ref[...], NT).astype(bf16)

    spread = spread_matrix(LANES, block, head_width, index * block)
    tailed = mm(tail_ref[...], spread).astype(bf16) * x_ref[...]
    emitted = mm(grow_ref[...], spread).astype(bf16) * cot_ref[...]
    at = pl.multiple_of(index * block, block)
    send_ref[:, pl.ds(at, block)] = mm(bt_ref[...], tailed).astype(bf16)
    send_ref[:, pl.ds(at + width, block)] = mm(ct_ref[...], emitted).astype(bf16)


def node_states(x, cot, b, c, step, rate, chunk, heads, head_width):
    length, state = b.shape
    width = heads * head_width
    block = min(width, 4 * LANES)
    count = width // block
    whole = lambda i: (0, 0)
    return pl.pallas_call(
        functools.partial(states_kernel, heads, head_width, chunk),
        grid=(count,),
        in_specs=[
            pl.BlockSpec((length, block), lambda i: (0, chunk * count + i)),
            pl.BlockSpec((length, block), lambda i: (0, chunk * count + i)),
            pl.BlockSpec((length, state), whole),
            pl.BlockSpec((length, state), whole),
            pl.BlockSpec((heads, length), lambda i: (chunk, 0)),
            pl.BlockSpec(rate.shape, whole),
        ],
        out_specs=[
            pl.BlockSpec((state, 2 * width + LANES), whole),
            pl.BlockSpec((length, LANES), whole),
            pl.BlockSpec((heads, length), whole),
            pl.BlockSpec((length, LANES), whole),
            pl.BlockSpec((length, LANES), whole),
            pl.BlockSpec((length, length), whole),
        ],
        out_shape=[
            jax.ShapeDtypeStruct((state, 2 * width + LANES), bf16),
            jax.ShapeDtypeStruct((length, LANES), f32),
            jax.ShapeDtypeStruct((heads, length), f32),
            jax.ShapeDtypeStruct((length, LANES), bf16),
            jax.ShapeDtypeStruct((length, LANES), bf16),
            jax.ShapeDtypeStruct((length, length), bf16),
        ],
        scratch_shapes=[pltpu.VMEM((state, length), bf16), pltpu.VMEM((state, length), bf16)],
        name="node_states",
        cost_estimate=pl.CostEstimate(
            flops=4 * length * state * width,
            bytes_accessed=4 * length * width + 4 * state * width,
            transcendentals=0,
        ),
    )(x, cot, b, c, step, rate)


def inner_kernel(
    head_width,
    first,
    aliased,
    x_ref,
    cot_ref,
    b_ref,
    c_ref,
    given_ref,
    low_ref,
    src_ref,
    *refs,
):
    if aliased:
        refs = refs[2:]
    out_ref, grad_ref, gc_ref, gb_ref, mixed_ref, turned_ref, wa_ref, wb_ref, gram_ref = refs
    length = x_ref.shape[0]
    index = pl.program_id(0)
    pack = LANES // head_width
    pairs = x_ref.shape[1] // LANES
    wide = 2 * LANES
    tiles = length // wide
    weights = (wa_ref, wb_ref)

    @pl.when(index == 0)
    def _():
        gram_ref[...] = given_ref[...]
        mixed_ref[...] = jnp.zeros_like(mixed_ref)
        for ref in weights:
            ref[...] = jnp.zeros_like(ref)

    lane = lax.broadcasted_iota(jnp.int32, (1, LANES), 1) // head_width
    causal = lax.broadcasted_iota(jnp.int32, (LANES, LANES), 0) >= lax.broadcasted_iota(
        jnp.int32, (LANES, LANES), 1
    )
    xs = [x_ref[:, q * LANES : (q + 1) * LANES] for q in range(pairs)]
    turned_cots = [cot_ref[:, q * LANES : (q + 1) * LANES].T for q in range(pairs)]
    low = low_ref[...]

    def decays(h):
        q, a = h // pack, h % pack
        w = weights[h % 2]
        cot = cot_ref[:, q * LANES : (q + 1) * LANES]
        cot = jnp.where(lane == a, cot, jnp.zeros_like(cot))
        place = (first + index * pairs + q) * pack + a
        column = head_lanes(low, place, LANES)
        source = src_ref[pl.ds(place, 1), :]
        for tile in range(tiles):
            scores = mm(cot[tile * wide :], xs[q][tile * wide : (tile + 1) * wide], NT)
            for i in range(2 * tile, 2 * tiles):
                rows = slice(i * LANES, (i + 1) * LANES)
                here = slice((i - 2 * tile) * LANES, (i - 2 * tile + 1) * LANES)
                for j in range(2 * tile, min(2 * tile + 1, i) + 1):
                    cols = slice(j * LANES, (j + 1) * LANES)
                    side = slice((j - 2 * tile) * LANES, (j - 2 * tile + 1) * LANES)
                    differ = column[rows] - source[:, cols]
                    if i == j:
                        differ = jnp.where(causal, differ, -jnp.inf)
                    decay = jnp.exp2(differ)
                    w[rows, cols] = decay.astype(bf16) * gram_ref[rows, cols]
                    mixed_ref[rows, cols] += decay * scores[here, side]
                yield

    def products(h):
        q, a = h // pack, h % pack
        w = weights[h % 2]
        x = xs[q]
        part = turned_cots[q][a * head_width : (a + 1) * head_width]
        mine = slice(q * LANES + a * head_width, q * LANES + (a + 1) * head_width)
        own = slice(a * head_width, (a + 1) * head_width)
        for tile in range(tiles):
            rows = slice(tile * wide, (tile + 1) * wide)
            found = mm(w[rows, : (tile + 1) * wide], x[: (tile + 1) * wide])
            out_ref[rows, mine] = found[:, own].astype(bf16)
            yield
            found = mm(part[:, tile * wide :], w[tile * wide :, rows])
            turned_ref[mine, rows] = found.astype(bf16)
            yield

    def finish(q):
        lanes = slice(q * LANES, (q + 1) * LANES)
        grad_ref[:, lanes] = turned_ref[lanes, :].T

    before = None
    for h in range(pairs * pack):
        for _ in decays(h):
            if before is not None:
                next(before, None)
        if before is not None:
            for _ in before:
                pass
            if h % pack == 0:
                finish(h // pack - 1)
        before = products(h)
    for _ in before:
        pass
    finish(pairs - 1)

    @pl.when(index == pl.num_programs(0) - 1)
    def _():
        mixed = mixed_ref[...].astype(bf16)
        gc_ref[...] = mm(mixed, b_ref[...])
        gb_ref[...] = mm(mixed.T, c_ref[...])


def node_inner(x, cot, b, c, gram, low, src, prior, chunk, part, parts, heads, head_width):
    length, state = b.shape
    width = heads * head_width
    block = min(width // parts, 2 * LANES)
    count = width // block // parts
    offset = (chunk * parts + part) * count
    whole = lambda i: (0, 0)
    place = lambda i: (0, offset + i)
    aliased = prior is not None
    operands = [x, cot, b, c, gram, low, src]
    in_specs = [
        pl.BlockSpec((length, block), place),
        pl.BlockSpec((length, block), place),
        pl.BlockSpec((length, state), whole),
        pl.BlockSpec((length, state), whole),
        pl.BlockSpec((length, length), whole),
        pl.BlockSpec((length, LANES), whole),
        pl.BlockSpec((heads, length), whole),
    ]
    aliases = {}
    if aliased:
        aliases = {len(operands): 0, len(operands) + 1: 1}
        operands += list(prior)
        in_specs += [pl.BlockSpec(memory_space=pl.ANY)] * 2
    kernel = functools.partial(inner_kernel, head_width, part * count * block // LANES, aliased)
    return pl.pallas_call(
        kernel,
        grid=(count,),
        in_specs=in_specs,
        out_specs=[
            pl.BlockSpec((length, block), place),
            pl.BlockSpec((length, block), place),
            pl.BlockSpec((length, state), whole),
            pl.BlockSpec((length, state), whole),
        ],
        out_shape=[
            jax.ShapeDtypeStruct(x.shape, bf16),
            jax.ShapeDtypeStruct(x.shape, bf16),
            jax.ShapeDtypeStruct((length, state), f32),
            jax.ShapeDtypeStruct((length, state), f32),
        ],
        scratch_shapes=[
            pltpu.VMEM((length, length), f32),
            pltpu.VMEM((block, length), bf16),
            pltpu.VMEM((length, length), bf16),
            pltpu.VMEM((length, length), bf16),
            pltpu.VMEM((length, length), bf16),
        ],
        input_output_aliases=aliases,
        name="node_inner",
        cost_estimate=pl.CostEstimate(
            flops=24 * length * length * count * block,
            bytes_accessed=12 * length * count * block,
            transcendentals=length * length * heads // parts,
        ),
    )(*operands)


def rank_nodes(parents_ref, rank_ref, half):
    nodes = rank_ref.shape[0]

    def clear(n, carry):
        rank_ref[n] = 0
        return carry

    def mark(n, carry):
        up = parents_ref[n]

        @pl.when(jnp.logical_and(up >= 0, (up >= half) != (n >= half)))
        def _():
            rank_ref[up] = 1

        return carry

    def place(n, count):
        crosses = rank_ref[n]
        rank_ref[n] = jnp.where(crosses > 0, count, -1)
        return count + crosses

    lax.fori_loop(0, nodes, clear, 0)
    lax.fori_loop(0, nodes, mark, 0)
    lax.fori_loop(0, nodes, place, 0)


def widen(narrow, heads, head_width):
    count = narrow.shape[0]
    flat = jnp.concatenate([narrow[n, :1].astype(f32) for n in range(count)], axis=0)
    return mm(flat.astype(bf16), spread_matrix(LANES, heads * head_width, head_width))


def pack_kernel(
    heads, head_width, parents_ref, recv_ref, main_ref, more_ref, decay_ref, slot_ref, chain_ref, rank_ref
):
    half = recv_ref.shape[0]
    width = heads * head_width
    base = lax.axis_index("node") // half * half
    rank_nodes(parents_ref, rank_ref, half)
    decay_ref[...] = widen(recv_ref[:, :, 2 * width :], heads, head_width)
    slot_ref[...] = jnp.zeros_like(slot_ref)
    chain_ref[...] = jnp.zeros_like(chain_ref)

    def inside(n):
        return jnp.logical_and(n >= base, n < base + half)

    def spot(n):
        return jnp.clip(n - base, 0, half - 1)

    def visit(m, carry):
        node = base + m
        flow = recv_ref[m, :, width : 2 * width].astype(f32)
        at = node
        live = jnp.bool_(True)
        for level in range(LEVELS):
            up = parents_ref[at]
            exists = jnp.logical_and(live, up >= 0)
            live = jnp.logical_and(exists, inside(up))
            away = jnp.logical_and(exists, jnp.logical_not(live))

            @pl.when(away)
            def _(flow=flow, up=up):
                slot = rank_ref[up]
                slot_ref[slot] = slot_ref[slot] + flow

            if level < LEVELS - 1:
                flow = flow * jnp.where(live, decay_ref[pl.ds(spot(up), 1)], 1.0)
            at = jnp.where(live, up, at)

        @pl.when(rank_ref[node] >= 0)
        def _():
            total = recv_ref[m, :, :width].astype(f32)
            factor = decay_ref[pl.ds(m, 1)]
            chain = recv_ref[m, :, 2 * width :].astype(f32)
            at = node
            live = jnp.bool_(True)
            for _ in range(LEVELS - 1):
                up = parents_ref[at]
                live = jnp.logical_and(jnp.logical_and(live, up >= 0), inside(up))
                where = spot(up)
                total = total + jnp.where(live, factor * recv_ref[where, :, :width].astype(f32), 0.0)
                factor = factor * jnp.where(live, decay_ref[pl.ds(where, 1)], 1.0)
                chain = chain * jnp.where(live, recv_ref[where, :, 2 * width :].astype(f32), 1.0)
                at = jnp.where(live, up, at)
            slot_ref[rank_ref[node]] = total
            chain_ref[rank_ref[node]] = chain

        return carry

    lax.fori_loop(0, half, visit, 0)
    main = main_ref.shape[0]
    main_ref[:, :, :width] = slot_ref[:main].astype(bf16)
    main_ref[:, :, width:] = chain_ref[:main].astype(bf16)
    more_ref[:, :, :width] = slot_ref[main:].astype(bf16)
    more_ref[:, :, width:] = chain_ref[main:].astype(bf16)


def slot_counts(nodes):
    most = nodes * LEVELS // (LEVELS + 1)
    return most // 2, most - most // 2


def pack_slots(parents, recv, nodes, heads, head_width):
    half, rows, _ = recv.shape
    width = heads * head_width
    main, more = slot_counts(nodes)
    in_specs = [pl.BlockSpec(memory_space=pltpu.SMEM), pl.BlockSpec(memory_space=pltpu.VMEM)]
    kernel = functools.partial(pack_kernel, heads, head_width)
    operands = [parents, recv]
    return pl.pallas_call(
        kernel,
        in_specs=in_specs,
        out_specs=[pl.BlockSpec(memory_space=pltpu.VMEM)] * 2,
        out_shape=[
            jax.ShapeDtypeStruct((main, rows, width + LANES), bf16),
            jax.ShapeDtypeStruct((more, rows, width + LANES), bf16),
        ],
        scratch_shapes=[
            pltpu.VMEM((half, width), f32),
            pltpu.VMEM((main + more, rows, width), f32),
            pltpu.VMEM((main + more, rows, LANES), f32),
            pltpu.SMEM((nodes,), jnp.int32),
        ],
        compiler_params=pltpu.CompilerParams(vmem_limit_bytes=VMEM_BYTES),
        name="pack_slots",
        cost_estimate=pl.CostEstimate(
            flops=20 * half * rows * width,
            bytes_accessed=8 * half * rows * width,
            transcendentals=0,
        ),
    )(*operands)


def join_kernel(
    heads,
    head_width,
    parents_ref,
    recv_ref,
    main_ref,
    more_ref,
    out_ref,
    decay_ref,
    slot_ref,
    chain_ref,
    back_ref,
    rank_ref,
):
    half = recv_ref.shape[0]
    width = heads * head_width
    main = main_ref.shape[0]
    base = lax.axis_index("node") // half * half
    rank_nodes(parents_ref, rank_ref, half)
    decay_ref[...] = widen(recv_ref[:, :, 2 * width :], heads, head_width)
    slot_ref[:main] = main_ref[:, :, :width].astype(f32)
    slot_ref[main:] = more_ref[:, :, :width].astype(f32)
    chain_ref[:main] = widen(main_ref[:, :, width:], heads, head_width)
    chain_ref[main:] = widen(more_ref[:, :, width:], heads, head_width)
    back_ref[...] = jnp.zeros_like(back_ref)

    def inside(n):
        return jnp.logical_and(n >= base, n < base + half)

    def climb(at, flow, start):
        factor = None
        live = jnp.bool_(True)
        for level in range(LEVELS):
            up = parents_ref[at]
            live = jnp.logical_and(live, up >= 0)
            near = jnp.logical_and(live, inside(up))
            far = jnp.logical_and(live, jnp.logical_not(near))
            where = jnp.clip(up - base, 0, half - 1)
            slot = jnp.where(far, rank_ref[jnp.maximum(up, 0)], 0)

            @pl.when(near)
            def _(flow=flow, where=where):
                back_ref[where] = back_ref[where] + flow

            if start is not None:
                value = jnp.where(near, recv_ref[where, :, :width].astype(f32), slot_ref[slot])
                value = jnp.where(live, value, 0.0)
                start = start + (value if factor is None else factor * value)
            if level < LEVELS - 1:
                step = jnp.where(near, decay_ref[pl.ds(where, 1)], chain_ref[pl.ds(slot, 1)])
                flow = flow * step
                factor = step if factor is None else factor * step
                top = jnp.maximum(up, 0)
                for _ in range(LEVELS - 1):
                    above = parents_ref[top]
                    more = jnp.logical_and(far, above >= 0)
                    more = jnp.logical_and(more, jnp.logical_not(inside(above)))
                    top = jnp.where(more, above, top)
                at = top
        return start

    def visit(m, carry):
        node = base + m
        seed = recv_ref[m, :, width : 2 * width].astype(f32)
        start = climb(node, seed, jnp.zeros(seed.shape, f32))
        out_ref[m, :, :width] = start.astype(bf16)

        @pl.when(rank_ref[node] >= 0)
        def _():
            extra = slot_ref[rank_ref[node]]
            back_ref[m] = back_ref[m] + extra
            climb(node, extra * decay_ref[pl.ds(m, 1)], None)

        return carry

    lax.fori_loop(0, half, visit, 0)
    out_ref[:, :, width:] = back_ref[...].astype(bf16)


def join_slots(parents, recv, main, more, nodes, heads, head_width):
    half, rows, _ = recv.shape
    width = heads * head_width
    in_specs = [pl.BlockSpec(memory_space=pltpu.SMEM)] + [pl.BlockSpec(memory_space=pltpu.VMEM)] * 3
    kernel = functools.partial(join_kernel, heads, head_width)
    operands = [parents, recv, main, more]
    slots = main.shape[0] + more.shape[0]
    return pl.pallas_call(
        kernel,
        in_specs=in_specs,
        out_specs=pl.BlockSpec(memory_space=pltpu.VMEM),
        out_shape=jax.ShapeDtypeStruct((half, rows, 2 * width), bf16),
        scratch_shapes=[
            pltpu.VMEM((half, width), f32),
            pltpu.VMEM((slots, rows, width), f32),
            pltpu.VMEM((slots, width), f32),
            pltpu.VMEM((half, rows, width), f32),
            pltpu.SMEM((nodes,), jnp.int32),
        ],
        compiler_params=pltpu.CompilerParams(vmem_limit_bytes=VMEM_BYTES),
        name="join_slots",
        cost_estimate=pl.CostEstimate(
            flops=20 * half * rows * width,
            bytes_accessed=8 * half * rows * width,
            transcendentals=0,
        ),
    )(*operands)


def outer_kernel(
    head_width,
    extras,
    final,
    x_ref,
    cot_ref,
    b_ref,
    c_ref,
    grow_ref,
    tail_ref,
    start_ref,
    back_ref,
    inner_ref,
    grad_ref,
    *refs,
):
    added = refs[: 2 * extras]
    refs = refs[2 * extras :]
    if not final:
        out_ref, gx_ref, gc_ref, gb_ref = refs
    else:
        out_ref, gx_ref, own_ref = refs[2:5]
        pieces = refs[5:-2]
        gc_ref, gb_ref = refs[-2:]
    block = x_ref.shape[1]
    index = pl.program_id(0)

    @pl.when(index == 0)
    def _():
        gc_ref[...] = sum(ref[...] for ref in added[:extras])
        gb_ref[...] = sum(ref[...] for ref in added[extras:])

    spread = spread_matrix(LANES, block, head_width, index * block)
    grow_wide = mm(grow_ref[...], spread)
    tail_wide = mm(tail_ref[...], spread)
    start = start_ref[...]
    back = back_ref[...]
    out_ref[...] = (inner_ref[...].astype(f32) + grow_wide * mm(c_ref[...], start)).astype(bf16)
    gx_ref[...] = (grad_ref[...].astype(f32) + tail_wide * mm(b_ref[...], back)).astype(bf16)
    gc_ref[...] += mm(grow_wide.astype(bf16) * cot_ref[...], start, NT)
    gb_ref[...] += mm(tail_wide.astype(bf16) * x_ref[...], back, NT)

    if final:

        @pl.when(index == pl.num_programs(0) - 1)
        def _():
            size = len(pieces) + 1
            me = lax.axis_index("head")
            rows = own_ref.shape[1]
            for shift in range(size):
                at = pl.multiple_of(lax.rem(me + shift, size) * rows, rows)
                for n, ref in enumerate((gb_ref, gc_ref)):
                    if shift == 0:
                        own_ref[n] = ref[pl.ds(at, rows)]
                    else:
                        pieces[shift - 1][n] = ref[pl.ds(at, rows)].astype(bf16)


def node_outer(
    x, cot, b, c, grow, tail, states, inner, grad, found, prior, chunk, heads, head_width
):
    length, state = b.shape
    width = heads * head_width
    block = min(width, 4 * LANES)
    count = width // block
    whole = lambda i: (0, 0)
    spot = lambda i: (0, i)
    place = lambda i: (0, chunk * count + i)
    final = prior is not None
    operands = [x, cot, b, c, grow, tail, states, states, inner, grad]
    in_specs = [
        pl.BlockSpec((length, block), place),
        pl.BlockSpec((length, block), place),
        pl.BlockSpec((length, state), whole),
        pl.BlockSpec((length, state), whole),
        pl.BlockSpec((length, LANES), whole),
        pl.BlockSpec((length, LANES), whole),
        pl.BlockSpec((state, block), spot),
        pl.BlockSpec((state, block), lambda i: (0, count + i)),
        pl.BlockSpec((length, block), place),
        pl.BlockSpec((length, block), place),
    ]
    operands += [v[1] for v in found] + [v[0] for v in found]
    in_specs += [pl.BlockSpec((length, state), whole)] * (2 * len(found))
    out_specs = [pl.BlockSpec((length, block), place)] * 2
    out_shape = [jax.ShapeDtypeStruct(x.shape, bf16)] * 2
    grads = jax.ShapeDtypeStruct((length, state), f32)
    scratch = []
    aliases = {}
    if final:
        aliases = {len(operands): 0, len(operands) + 1: 1}
        operands += list(prior)
        in_specs += [pl.BlockSpec(memory_space=pl.ANY)] * 2
        size = lax.axis_size("head")
        kept = (2, length // size, state)
        cube = lambda i: (0, 0, 0)
        out_specs += [pl.BlockSpec(kept, cube)] * size
        out_shape += [jax.ShapeDtypeStruct(kept, f32)]
        out_shape += [jax.ShapeDtypeStruct(kept, bf16)] * (size - 1)
        scratch = [pltpu.VMEM((length, state), f32)] * 2
    else:
        out_specs += [pl.BlockSpec((length, state), whole)] * 2
        out_shape += [grads] * 2
    kernel = functools.partial(outer_kernel, head_width, len(found), final)
    return pl.pallas_call(
        kernel,
        grid=(count,),
        in_specs=in_specs,
        out_specs=out_specs,
        out_shape=out_shape,
        scratch_shapes=scratch,
        input_output_aliases=aliases,
        name="node_outer",
        cost_estimate=pl.CostEstimate(
            flops=8 * length * state * width,
            bytes_accessed=12 * length * width,
            transcendentals=0,
        ),
    )(*operands)


def scatter_sum(own, pieces):
    size = lax.axis_size("head")
    for shift, piece in enumerate(pieces, 1):
        pairs = [(i, (i + shift) % size) for i in range(size)]
        own = own + lax.ppermute(piece, "head", pairs).astype(f32)
    return own


def one_device(inputs, b_matrix, c_matrix, step_size, decay_rate, parents, cotangent):
    state = b_matrix.shape[1]
    head_count = step_size.shape[0]
    head_width = inputs.shape[1] // head_count
    nodes = lax.axis_size("node")
    heads = head_count // CHUNKS
    half = nodes // 2
    rate = decay_rate[None, :]
    groups = [list(range(half)), list(range(half, nodes))]
    across = [(n, (n + half) % nodes) for n in range(nodes)]

    def swap(v):
        return lax.all_to_all(
            v.reshape(half, state // half, v.shape[-1]),
            "node",
            split_axis=0,
            concat_axis=0,
            tiled=True,
            axis_index_groups=groups,
        )

    def cross(v):
        return lax.ppermute(v, "node", across)

    places = jnp.arange(nodes)
    child = jnp.logical_and(
        parents[:, None] == places[None, :], (places[:, None] < half) != (places[None, :] < half)
    )
    crossing = jnp.sum(jnp.any(child, axis=0).astype(jnp.int32))
    crowded = crossing > slot_counts(nodes)[0]

    shared = (inputs, cotangent, b_matrix, c_matrix)
    sizes = (heads, head_width)
    made = []
    for k in range(CHUNKS):
        made.append(node_states(*shared, step_size, rate, k, *sizes))
    received = [swap(made[k][0]) for k in range(CHUNKS)]
    found = []
    prior = None
    for k in range(CHUNKS):
        for part in range(PARTS):
            *prior, gc, gb = node_inner(
                *shared, made[0][5], made[k][1], made[k][2], prior, k, part, PARTS, *sizes
            )
            found.append((gb, gc))
    inner = prior
    packed = []
    for k in range(CHUNKS):
        main, more = pack_slots(parents, received[k], nodes, *sizes)
        packed.append((main, more, cross(main)))
    others = lax.cond(
        crowded,
        lambda vs: tuple(cross(v) for v in vs),
        lambda vs: vs,
        tuple(p[1] for p in packed),
    )
    states = []
    for k in range(CHUNKS):
        joined = join_slots(parents, received[k], packed[k][2], others[k], nodes, *sizes)
        states.append(swap(joined).reshape(state, -1))
    prior = None
    for k in range(CHUNKS):
        result = node_outer(
            *shared, made[k][3], made[k][4], states[k], *inner, found, prior, k, *sizes
        )
        prior = result[:2]
        if k == 0:
            found = [(result[3], result[2])]
    grads = scatter_sum(result[2], result[3:])
    return prior[0], prior[1], grads[0], grads[1]


def solution(mesh):
    return jax.shard_map(
        one_device,
        mesh=mesh,
        in_specs=(
            P("node", "head"),
            P("node", None),
            P("node", None),
            P("head", "node"),
            P("head"),
            P(),
            P("node", "head"),
        ),
        out_specs=(
            P("node", "head"),
            P("node", "head"),
            P(("node", "head"), None),
            P(("node", "head"), None),
        ),
        check_vma=False,
    )
```

```python
import functools
import math

import jax
import jax.numpy as jnp
from jax import lax
from jax.experimental import pallas as pl
from jax.experimental.pallas import tpu as pltpu
from jax.sharding import PartitionSpec as P


LEVELS = 3
VMEM_BYTES = 24 << 20
LANES = 128
SUBLANES = 8
CHUNKS = 2
PARTS = 2

LOG2E = 1.0 / math.log(2.0)

f32 = jnp.float32
bf16 = jnp.bfloat16
NN = (((1,), (0,)), ((), ()))
NT = (((1,), (1,)), ((), ()))


def mm(a, b, dims=NN):
    return lax.dot_general(a, b, dims, preferred_element_type=f32)


def split_two(v):
    high = v.astype(bf16)
    return high, (v - high.astype(f32)).astype(bf16)


def spread_matrix(rows, width, head_width, offset=0):
    row = lax.broadcasted_iota(jnp.int32, (rows, width), 0)
    lane = (lax.broadcasted_iota(jnp.int32, (rows, width), 1) + offset) // head_width
    return (row == lane).astype(bf16)


def head_lanes(columns, first, head_width):
    lane = lax.broadcasted_iota(jnp.int32, columns.shape, 1) // head_width + first
    return jnp.take_along_axis(columns, lane, axis=1)


def pad_lanes(v):
    gap = LANES - v.shape[0]
    if gap:
        v = jnp.concatenate([v, jnp.zeros((gap, v.shape[1]), v.dtype)], axis=0)
    return v.T


def half_steps(step_ref, spread):
    steps = mm(step_ref[...], spread)
    return steps[:1], steps[SUBLANES : SUBLANES + 1]


def states_kernel(
    heads,
    head_width,
    chunk,
    x_ref,
    cot_ref,
    b_ref,
    c_ref,
    step_ref,
    rate_ref,
    send_ref,
    low_ref,
    src_ref,
    grow_ref,
    tail_ref,
    gram_ref,
    keep_ref,
    step_out_ref,
    bt_ref,
    ct_ref,
):
    block = x_ref.shape[1]
    length = step_ref.shape[1]
    middle = length // 2
    index = pl.program_id(0)
    width = heads * head_width

    @pl.when(index == 0)
    def _():
        step = step_ref[...]
        rates = jnp.broadcast_to(rate_ref[...], (LANES, rate_ref.shape[1])).T
        terms = -step * rates[chunk * heads : (chunk + 1) * heads, :1]
        row = lax.broadcasted_iota(jnp.int32, (length, length), 0)
        col = lax.broadcasted_iota(jnp.int32, (length, length), 1)
        upper = (row <= col).astype(bf16)
        first = terms.astype(bf16)
        rest = terms - first.astype(f32)
        second, third = split_two(rest)
        cumulative = mm(third, upper) + mm(second, upper) + mm(first, upper)
        last = cumulative[:, length - 1 :]
        mid = cumulative[:, middle - 1 : middle]
        late = lax.broadcasted_iota(jnp.int32, cumulative.shape, 1) >= middle
        low_ref[...] = pad_lanes(cumulative * LOG2E)
        src_ref[...] = (cumulative - jnp.log(step)) * LOG2E
        grow_ref[...] = pad_lanes(jnp.exp(cumulative - jnp.where(late, mid, 0.0))).astype(bf16)
        tail = jnp.exp(jnp.where(late, last, mid) - cumulative) * step
        tail_ref[...] = pad_lanes(tail).astype(bf16)
        bt_ref[...] = b_ref[...].T
        ct_ref[...] = c_ref[...].T
        total = jnp.exp(jnp.broadcast_to(last, (heads, send_ref.shape[0])))
        send_ref[:, 2 * width :] = pad_lanes(total).astype(bf16)
        each = (heads, SUBLANES)
        steps = [jnp.broadcast_to(mid, each), jnp.broadcast_to(last - mid, each)]
        step_out_ref[...] = pad_lanes(jnp.exp(jnp.concatenate(steps, axis=1))).astype(bf16)
        for rows in (slice(0, middle), slice(middle, length)):
            gram_ref[rows] = mm(c_ref[rows], b_ref[rows], NT).astype(bf16)

    spread = spread_matrix(LANES, block, head_width, index * block)
    tailed = mm(tail_ref[...], spread).astype(bf16) * x_ref[...]
    emitted = mm(grow_ref[...], spread).astype(bf16) * cot_ref[...]
    early_step, late_step = half_steps(step_out_ref, spread)
    early_state = mm(bt_ref[:, :middle], tailed[:middle])
    late_state = mm(bt_ref[:, middle:], tailed[middle:])
    early_seed = mm(ct_ref[:, :middle], emitted[:middle])
    late_seed = mm(ct_ref[:, middle:], emitted[middle:])
    here = pl.ds(pl.multiple_of(index * block, block), block)
    there = pl.ds(pl.multiple_of(index * block + width, LANES), block)
    send_ref[:, here] = (late_step * early_state + late_state).astype(bf16)
    send_ref[:, there] = (early_seed + early_step * late_seed).astype(bf16)
    keep_ref[:, here] = early_state.astype(bf16)
    keep_ref[:, there] = late_seed.astype(bf16)


def node_states(x, cot, b, c, step, rate, chunk, heads, head_width):
    length, state = b.shape
    width = heads * head_width
    block = min(width, 4 * LANES)
    count = width // block
    whole = lambda i: (0, 0)
    return pl.pallas_call(
        functools.partial(states_kernel, heads, head_width, chunk),
        grid=(count,),
        in_specs=[
            pl.BlockSpec((length, block), lambda i: (0, chunk * count + i)),
            pl.BlockSpec((length, block), lambda i: (0, chunk * count + i)),
            pl.BlockSpec((length, state), whole),
            pl.BlockSpec((length, state), whole),
            pl.BlockSpec((heads, length), lambda i: (chunk, 0)),
            pl.BlockSpec(rate.shape, whole),
        ],
        out_specs=[
            pl.BlockSpec((state, 2 * width + LANES), whole),
            pl.BlockSpec((length, LANES), whole),
            pl.BlockSpec((heads, length), whole),
            pl.BlockSpec((length, LANES), whole),
            pl.BlockSpec((length, LANES), whole),
            pl.BlockSpec((length, length // 2), whole),
            pl.BlockSpec((state, 2 * width), whole),
            pl.BlockSpec((2 * SUBLANES, LANES), whole),
        ],
        out_shape=[
            jax.ShapeDtypeStruct((state, 2 * width + LANES), bf16),
            jax.ShapeDtypeStruct((length, LANES), f32),
            jax.ShapeDtypeStruct((heads, length), f32),
            jax.ShapeDtypeStruct((length, LANES), bf16),
            jax.ShapeDtypeStruct((length, LANES), bf16),
            jax.ShapeDtypeStruct((length, length // 2), bf16),
            jax.ShapeDtypeStruct((state, 2 * width), bf16),
            jax.ShapeDtypeStruct((2 * SUBLANES, LANES), bf16),
        ],
        scratch_shapes=[pltpu.VMEM((state, length), bf16), pltpu.VMEM((state, length), bf16)],
        name="node_states",
        cost_estimate=pl.CostEstimate(
            flops=4 * length * state * width,
            bytes_accessed=4 * length * width + 4 * state * width,
            transcendentals=0,
        ),
    )(x, cot, b, c, step, rate)


def inner_kernel(
    head_width,
    first,
    aliased,
    x_ref,
    cot_ref,
    b_ref,
    c_ref,
    given_ref,
    low_ref,
    src_ref,
    *refs,
):
    if aliased:
        refs = refs[2:]
    out_ref, grad_ref, gc_ref, gb_ref, mixed_ref, turned_ref, wa_ref, wb_ref, gram_ref = refs
    length = x_ref.shape[0]
    index = pl.program_id(0)
    pack = LANES // head_width
    pairs = x_ref.shape[1] // LANES
    wide = length // 2
    blocks = wide // LANES
    weights = (wa_ref, wb_ref)

    @pl.when(index == 0)
    def _():
        gram_ref[...] = given_ref[...]
        mixed_ref[...] = jnp.zeros_like(mixed_ref)
        for ref in weights:
            ref[...] = jnp.zeros_like(ref)

    lane = lax.broadcasted_iota(jnp.int32, (1, LANES), 1) // head_width
    causal = lax.broadcasted_iota(jnp.int32, (LANES, LANES), 0) >= lax.broadcasted_iota(
        jnp.int32, (LANES, LANES), 1
    )
    halves = (slice(0, wide), slice(wide, length))
    xs = [x_ref[:, q * LANES : (q + 1) * LANES] for q in range(pairs)]
    turned_cots = [cot_ref[:, q * LANES : (q + 1) * LANES].T for q in range(pairs)]
    low = low_ref[...]

    def decays(h):
        q, a = h // pack, h % pack
        w = weights[h % 2]
        cot = cot_ref[:, q * LANES : (q + 1) * LANES]
        cot = jnp.where(lane == a, cot, jnp.zeros_like(cot))
        place = (first + index * pairs + q) * pack + a
        column = head_lanes(low, place, LANES)
        source = src_ref[pl.ds(place, 1), :]
        for part in halves:
            scores = mm(cot[part], xs[q][part], NT)
            for i in range(blocks):
                here = slice(i * LANES, (i + 1) * LANES)
                rows = slice(part.start + here.start, part.start + here.stop)
                for j in range(i + 1):
                    cols = slice(j * LANES, (j + 1) * LANES)
                    differ = column[rows] - source[:, part.start + cols.start : part.start + cols.stop]
                    if i == j:
                        differ = jnp.where(causal, differ, -jnp.inf)
                    decay = jnp.exp2(differ)
                    w[rows, cols] = decay.astype(bf16) * gram_ref[rows, cols]
                    mixed_ref[rows, cols] += decay * scores[here, cols]
                yield

    def products(h):
        q, a = h // pack, h % pack
        w = weights[h % 2]
        turned = turned_cots[q][a * head_width : (a + 1) * head_width]
        mine = slice(q * LANES + a * head_width, q * LANES + (a + 1) * head_width)
        own = slice(a * head_width, (a + 1) * head_width)
        for part in halves:
            out_ref[part, mine] = mm(w[part], xs[q][part])[:, own].astype(bf16)
            yield
            turned_ref[mine, part] = mm(turned[:, part], w[part]).astype(bf16)
            yield

    def finish(q):
        lanes = slice(q * LANES, (q + 1) * LANES)
        grad_ref[:, lanes] = turned_ref[lanes, :].T

    before = None
    for h in range(pairs * pack):
        for _ in decays(h):
            if before is not None:
                next(before, None)
        if before is not None:
            for _ in before:
                pass
            if h % pack == 0:
                finish(h // pack - 1)
        before = products(h)
    for _ in before:
        pass
    finish(pairs - 1)

    @pl.when(index == pl.num_programs(0) - 1)
    def _():
        for part in halves:
            mixed = mixed_ref[part].astype(bf16)
            gc_ref[part] = mm(mixed, b_ref[part])
            gb_ref[part] = mm(mixed.T, c_ref[part])


def node_inner(x, cot, b, c, gram, low, src, prior, chunk, part, parts, heads, head_width):
    length, state = b.shape
    width = heads * head_width
    block = min(width // parts, 2 * LANES)
    count = width // block // parts
    offset = (chunk * parts + part) * count
    whole = lambda i: (0, 0)
    place = lambda i: (0, offset + i)
    aliased = prior is not None
    operands = [x, cot, b, c, gram, low, src]
    in_specs = [
        pl.BlockSpec((length, block), place),
        pl.BlockSpec((length, block), place),
        pl.BlockSpec((length, state), whole),
        pl.BlockSpec((length, state), whole),
        pl.BlockSpec((length, length // 2), whole),
        pl.BlockSpec((length, LANES), whole),
        pl.BlockSpec((heads, length), whole),
    ]
    aliases = {}
    if aliased:
        aliases = {len(operands): 0, len(operands) + 1: 1}
        operands += list(prior)
        in_specs += [pl.BlockSpec(memory_space=pl.ANY)] * 2
    kernel = functools.partial(inner_kernel, head_width, part * count * block // LANES, aliased)
    return pl.pallas_call(
        kernel,
        grid=(count,),
        in_specs=in_specs,
        out_specs=[
            pl.BlockSpec((length, block), place),
            pl.BlockSpec((length, block), place),
            pl.BlockSpec((length, state), whole),
            pl.BlockSpec((length, state), whole),
        ],
        out_shape=[
            jax.ShapeDtypeStruct(x.shape, bf16),
            jax.ShapeDtypeStruct(x.shape, bf16),
            jax.ShapeDtypeStruct((length, state), f32),
            jax.ShapeDtypeStruct((length, state), f32),
        ],
        scratch_shapes=[
            pltpu.VMEM((length, length // 2), f32),
            pltpu.VMEM((block, length), bf16),
            pltpu.VMEM((length, length // 2), bf16),
            pltpu.VMEM((length, length // 2), bf16),
            pltpu.VMEM((length, length // 2), bf16),
        ],
        input_output_aliases=aliases,
        name="node_inner",
        cost_estimate=pl.CostEstimate(
            flops=24 * length * length * count * block,
            bytes_accessed=12 * length * count * block,
            transcendentals=length * length * heads // parts,
        ),
    )(*operands)


def rank_nodes(parents_ref, rank_ref, half):
    nodes = rank_ref.shape[0]

    def clear(n, carry):
        rank_ref[n] = 0
        return carry

    def mark(n, carry):
        up = parents_ref[n]

        @pl.when(jnp.logical_and(up >= 0, (up >= half) != (n >= half)))
        def _():
            rank_ref[up] = 1

        return carry

    def place(n, count):
        crosses = rank_ref[n]
        rank_ref[n] = jnp.where(crosses > 0, count, -1)
        return count + crosses

    lax.fori_loop(0, nodes, clear, 0)
    lax.fori_loop(0, nodes, mark, 0)
    lax.fori_loop(0, nodes, place, 0)


def widen(narrow, heads, head_width):
    count = narrow.shape[0]
    flat = jnp.concatenate([narrow[n, :1].astype(f32) for n in range(count)], axis=0)
    return mm(flat.astype(bf16), spread_matrix(LANES, heads * head_width, head_width))


def pack_kernel(
    heads, head_width, parents_ref, recv_ref, main_ref, more_ref, decay_ref, slot_ref, chain_ref, rank_ref
):
    half = recv_ref.shape[0]
    width = heads * head_width
    base = lax.axis_index("node") // half * half
    rank_nodes(parents_ref, rank_ref, half)
    decay_ref[...] = widen(recv_ref[:, :, 2 * width :], heads, head_width)
    slot_ref[...] = jnp.zeros_like(slot_ref)
    chain_ref[...] = jnp.zeros_like(chain_ref)

    def inside(n):
        return jnp.logical_and(n >= base, n < base + half)

    def spot(n):
        return jnp.clip(n - base, 0, half - 1)

    def visit(m, carry):
        node = base + m
        flow = recv_ref[m, :, width : 2 * width].astype(f32)
        at = node
        live = jnp.bool_(True)
        for level in range(LEVELS):
            up = parents_ref[at]
            exists = jnp.logical_and(live, up >= 0)
            live = jnp.logical_and(exists, inside(up))
            away = jnp.logical_and(exists, jnp.logical_not(live))

            @pl.when(away)
            def _(flow=flow, up=up):
                slot = rank_ref[up]
                slot_ref[slot] = slot_ref[slot] + flow

            if level < LEVELS - 1:
                flow = flow * jnp.where(live, decay_ref[pl.ds(spot(up), 1)], 1.0)
            at = jnp.where(live, up, at)

        @pl.when(rank_ref[node] >= 0)
        def _():
            total = recv_ref[m, :, :width].astype(f32)
            factor = decay_ref[pl.ds(m, 1)]
            chain = recv_ref[m, :, 2 * width :].astype(f32)
            at = node
            live = jnp.bool_(True)
            for _ in range(LEVELS - 1):
                up = parents_ref[at]
                live = jnp.logical_and(jnp.logical_and(live, up >= 0), inside(up))
                where = spot(up)
                total = total + jnp.where(live, factor * recv_ref[where, :, :width].astype(f32), 0.0)
                factor = factor * jnp.where(live, decay_ref[pl.ds(where, 1)], 1.0)
                chain = chain * jnp.where(live, recv_ref[where, :, 2 * width :].astype(f32), 1.0)
                at = jnp.where(live, up, at)
            slot_ref[rank_ref[node]] = total
            chain_ref[rank_ref[node]] = chain

        return carry

    lax.fori_loop(0, half, visit, 0)
    main = main_ref.shape[0]
    main_ref[:, :, :width] = slot_ref[:main].astype(bf16)
    main_ref[:, :, width:] = chain_ref[:main].astype(bf16)
    more_ref[:, :, :width] = slot_ref[main:].astype(bf16)
    more_ref[:, :, width:] = chain_ref[main:].astype(bf16)


def slot_counts(nodes):
    most = nodes * LEVELS // (LEVELS + 1)
    return most // 2, most - most // 2


def pack_slots(parents, recv, nodes, heads, head_width):
    half, rows, _ = recv.shape
    width = heads * head_width
    main, more = slot_counts(nodes)
    in_specs = [pl.BlockSpec(memory_space=pltpu.SMEM), pl.BlockSpec(memory_space=pltpu.VMEM)]
    kernel = functools.partial(pack_kernel, heads, head_width)
    operands = [parents, recv]
    return pl.pallas_call(
        kernel,
        in_specs=in_specs,
        out_specs=[pl.BlockSpec(memory_space=pltpu.VMEM)] * 2,
        out_shape=[
            jax.ShapeDtypeStruct((main, rows, width + LANES), bf16),
            jax.ShapeDtypeStruct((more, rows, width + LANES), bf16),
        ],
        scratch_shapes=[
            pltpu.VMEM((half, width), f32),
            pltpu.VMEM((main + more, rows, width), f32),
            pltpu.VMEM((main + more, rows, LANES), f32),
            pltpu.SMEM((nodes,), jnp.int32),
        ],
        compiler_params=pltpu.CompilerParams(vmem_limit_bytes=VMEM_BYTES),
        name="pack_slots",
        cost_estimate=pl.CostEstimate(
            flops=20 * half * rows * width,
            bytes_accessed=8 * half * rows * width,
            transcendentals=0,
        ),
    )(*operands)


def join_kernel(
    heads,
    head_width,
    parents_ref,
    recv_ref,
    main_ref,
    more_ref,
    out_ref,
    decay_ref,
    slot_ref,
    chain_ref,
    back_ref,
    rank_ref,
):
    half = recv_ref.shape[0]
    width = heads * head_width
    main = main_ref.shape[0]
    base = lax.axis_index("node") // half * half
    rank_nodes(parents_ref, rank_ref, half)
    decay_ref[...] = widen(recv_ref[:, :, 2 * width :], heads, head_width)
    slot_ref[:main] = main_ref[:, :, :width].astype(f32)
    slot_ref[main:] = more_ref[:, :, :width].astype(f32)
    chain_ref[:main] = widen(main_ref[:, :, width:], heads, head_width)
    chain_ref[main:] = widen(more_ref[:, :, width:], heads, head_width)
    back_ref[...] = jnp.zeros_like(back_ref)

    def inside(n):
        return jnp.logical_and(n >= base, n < base + half)

    def climb(at, flow, start):
        factor = None
        live = jnp.bool_(True)
        for level in range(LEVELS):
            up = parents_ref[at]
            live = jnp.logical_and(live, up >= 0)
            near = jnp.logical_and(live, inside(up))
            far = jnp.logical_and(live, jnp.logical_not(near))
            where = jnp.clip(up - base, 0, half - 1)
            slot = jnp.where(far, rank_ref[jnp.maximum(up, 0)], 0)

            @pl.when(near)
            def _(flow=flow, where=where):
                back_ref[where] = back_ref[where] + flow

            if start is not None:
                value = jnp.where(near, recv_ref[where, :, :width].astype(f32), slot_ref[slot])
                value = jnp.where(live, value, 0.0)
                start = start + (value if factor is None else factor * value)
            if level < LEVELS - 1:
                step = jnp.where(near, decay_ref[pl.ds(where, 1)], chain_ref[pl.ds(slot, 1)])
                flow = flow * step
                factor = step if factor is None else factor * step
                top = jnp.maximum(up, 0)
                for _ in range(LEVELS - 1):
                    above = parents_ref[top]
                    more = jnp.logical_and(far, above >= 0)
                    more = jnp.logical_and(more, jnp.logical_not(inside(above)))
                    top = jnp.where(more, above, top)
                at = top
        return start

    def visit(m, carry):
        node = base + m
        seed = recv_ref[m, :, width : 2 * width].astype(f32)
        start = climb(node, seed, jnp.zeros(seed.shape, f32))
        out_ref[m, :, :width] = start.astype(bf16)

        @pl.when(rank_ref[node] >= 0)
        def _():
            extra = slot_ref[rank_ref[node]]
            back_ref[m] = back_ref[m] + extra
            climb(node, extra * decay_ref[pl.ds(m, 1)], None)

        return carry

    lax.fori_loop(0, half, visit, 0)
    out_ref[:, :, width:] = back_ref[...].astype(bf16)


def join_slots(parents, recv, main, more, nodes, heads, head_width):
    half, rows, _ = recv.shape
    width = heads * head_width
    in_specs = [pl.BlockSpec(memory_space=pltpu.SMEM)] + [pl.BlockSpec(memory_space=pltpu.VMEM)] * 3
    kernel = functools.partial(join_kernel, heads, head_width)
    operands = [parents, recv, main, more]
    slots = main.shape[0] + more.shape[0]
    return pl.pallas_call(
        kernel,
        in_specs=in_specs,
        out_specs=pl.BlockSpec(memory_space=pltpu.VMEM),
        out_shape=jax.ShapeDtypeStruct((half, rows, 2 * width), bf16),
        scratch_shapes=[
            pltpu.VMEM((half, width), f32),
            pltpu.VMEM((slots, rows, width), f32),
            pltpu.VMEM((slots, width), f32),
            pltpu.VMEM((half, rows, width), f32),
            pltpu.SMEM((nodes,), jnp.int32),
        ],
        compiler_params=pltpu.CompilerParams(vmem_limit_bytes=VMEM_BYTES),
        name="join_slots",
        cost_estimate=pl.CostEstimate(
            flops=20 * half * rows * width,
            bytes_accessed=8 * half * rows * width,
            transcendentals=0,
        ),
    )(*operands)


def outer_kernel(
    head_width,
    extras,
    final,
    x_ref,
    cot_ref,
    b_ref,
    c_ref,
    grow_ref,
    tail_ref,
    start_ref,
    back_ref,
    early_ref,
    late_ref,
    step_ref,
    inner_ref,
    grad_ref,
    *refs,
):
    added = refs[: 2 * extras]
    refs = refs[2 * extras :]
    if not final:
        out_ref, gx_ref, gc_ref, gb_ref = refs
    else:
        out_ref, gx_ref, own_ref = refs[2:5]
        pieces = refs[5:-2]
        gc_ref, gb_ref = refs[-2:]
    block = x_ref.shape[1]
    index = pl.program_id(0)

    @pl.when(index == 0)
    def _():
        gc_ref[...] = sum(ref[...] for ref in added[:extras])
        gb_ref[...] = sum(ref[...] for ref in added[extras:])

    spread = spread_matrix(LANES, block, head_width, index * block)
    grow_wide = mm(grow_ref[...], spread)
    tail_wide = mm(tail_ref[...], spread)
    early_step, late_step = half_steps(step_ref, spread)
    start = start_ref[...]
    back = back_ref[...]
    starts = (start, (early_step * start.astype(f32) + early_ref[...].astype(f32)).astype(bf16))
    backs = ((late_step * back.astype(f32) + late_ref[...].astype(f32)).astype(bf16), back)
    middle = x_ref.shape[0] // 2
    for n, part in enumerate((slice(0, middle), slice(middle, 2 * middle))):
        grow = grow_wide[part]
        tail = tail_wide[part]
        carried = grow * mm(c_ref[part], starts[n])
        out_ref[part] = (inner_ref[part].astype(f32) + carried).astype(bf16)
        carried = tail * mm(b_ref[part], backs[n])
        gx_ref[part] = (grad_ref[part].astype(f32) + carried).astype(bf16)
        gc_ref[part] += mm(grow.astype(bf16) * cot_ref[part], starts[n], NT)
        gb_ref[part] += mm(tail.astype(bf16) * x_ref[part], backs[n], NT)

    if final:

        @pl.when(index == pl.num_programs(0) - 1)
        def _():
            size = len(pieces) + 1
            me = lax.axis_index("head")
            rows = own_ref.shape[1]
            for shift in range(size):
                at = pl.multiple_of(lax.rem(me + shift, size) * rows, rows)
                for n, ref in enumerate((gb_ref, gc_ref)):
                    if shift == 0:
                        own_ref[n] = ref[pl.ds(at, rows)]
                    else:
                        pieces[shift - 1][n] = ref[pl.ds(at, rows)].astype(bf16)


def node_outer(
    x, cot, b, c, grow, tail, states, keep, steps, inner, grad, found, prior, chunk, heads, head_width
):
    length, state = b.shape
    width = heads * head_width
    block = min(width, 4 * LANES)
    count = width // block
    whole = lambda i: (0, 0)
    spot = lambda i: (0, i)
    place = lambda i: (0, chunk * count + i)
    final = prior is not None
    operands = [x, cot, b, c, grow, tail, states, states, keep, keep, steps, inner, grad]
    in_specs = [
        pl.BlockSpec((length, block), place),
        pl.BlockSpec((length, block), place),
        pl.BlockSpec((length, state), whole),
        pl.BlockSpec((length, state), whole),
        pl.BlockSpec((length, LANES), whole),
        pl.BlockSpec((length, LANES), whole),
        pl.BlockSpec((state, block), spot),
        pl.BlockSpec((state, block), lambda i: (0, count + i)),
        pl.BlockSpec((state, block), spot),
        pl.BlockSpec((state, block), lambda i: (0, count + i)),
        pl.BlockSpec((2 * SUBLANES, LANES), whole),
        pl.BlockSpec((length, block), place),
        pl.BlockSpec((length, block), place),
    ]
    operands += [v[1] for v in found] + [v[0] for v in found]
    in_specs += [pl.BlockSpec((length, state), whole)] * (2 * len(found))
    out_specs = [pl.BlockSpec((length, block), place)] * 2
    out_shape = [jax.ShapeDtypeStruct(x.shape, bf16)] * 2
    grads = jax.ShapeDtypeStruct((length, state), f32)
    scratch = []
    aliases = {}
    if final:
        aliases = {len(operands): 0, len(operands) + 1: 1}
        operands += list(prior)
        in_specs += [pl.BlockSpec(memory_space=pl.ANY)] * 2
        size = lax.axis_size("head")
        kept = (2, length // size, state)
        cube = lambda i: (0, 0, 0)
        out_specs += [pl.BlockSpec(kept, cube)] * size
        out_shape += [jax.ShapeDtypeStruct(kept, f32)]
        out_shape += [jax.ShapeDtypeStruct(kept, bf16)] * (size - 1)
        scratch = [pltpu.VMEM((length, state), f32)] * 2
    else:
        out_specs += [pl.BlockSpec((length, state), whole)] * 2
        out_shape += [grads] * 2
    kernel = functools.partial(outer_kernel, head_width, len(found), final)
    return pl.pallas_call(
        kernel,
        grid=(count,),
        in_specs=in_specs,
        out_specs=out_specs,
        out_shape=out_shape,
        scratch_shapes=scratch,
        input_output_aliases=aliases,
        name="node_outer",
        cost_estimate=pl.CostEstimate(
            flops=8 * length * state * width,
            bytes_accessed=12 * length * width,
            transcendentals=0,
        ),
    )(*operands)


def scatter_sum(own, pieces):
    size = lax.axis_size("head")
    for shift, piece in enumerate(pieces, 1):
        pairs = [(i, (i + shift) % size) for i in range(size)]
        own = own + lax.ppermute(piece, "head", pairs).astype(f32)
    return own


def one_device(inputs, b_matrix, c_matrix, step_size, decay_rate, parents, cotangent):
    state = b_matrix.shape[1]
    head_count = step_size.shape[0]
    head_width = inputs.shape[1] // head_count
    nodes = lax.axis_size("node")
    heads = head_count // CHUNKS
    half = nodes // 2
    rate = decay_rate[None, :]
    groups = [list(range(half)), list(range(half, nodes))]
    across = [(n, (n + half) % nodes) for n in range(nodes)]

    def swap(v):
        return lax.all_to_all(
            v.reshape(half, state // half, v.shape[-1]),
            "node",
            split_axis=0,
            concat_axis=0,
            tiled=True,
            axis_index_groups=groups,
        )

    def cross(v):
        return lax.ppermute(v, "node", across)

    places = jnp.arange(nodes)
    child = jnp.logical_and(
        parents[:, None] == places[None, :], (places[:, None] < half) != (places[None, :] < half)
    )
    crossing = jnp.sum(jnp.any(child, axis=0).astype(jnp.int32))
    crowded = crossing > slot_counts(nodes)[0]

    shared = (inputs, cotangent, b_matrix, c_matrix)
    sizes = (heads, head_width)
    made = []
    for k in range(CHUNKS):
        made.append(node_states(*shared, step_size, rate, k, *sizes))
    received = [swap(made[k][0]) for k in range(CHUNKS)]
    found = []
    prior = None
    for k in range(CHUNKS):
        for part in range(PARTS):
            *prior, gc, gb = node_inner(
                *shared, made[0][5], made[k][1], made[k][2], prior, k, part, PARTS, *sizes
            )
            found.append((gb, gc))
    inner = prior
    packed = []
    for k in range(CHUNKS):
        main, more = pack_slots(parents, received[k], nodes, *sizes)
        packed.append((main, more, cross(main)))
    others = lax.cond(
        crowded,
        lambda vs: tuple(cross(v) for v in vs),
        lambda vs: vs,
        tuple(p[1] for p in packed),
    )
    states = []
    for k in range(CHUNKS):
        joined = join_slots(parents, received[k], packed[k][2], others[k], nodes, *sizes)
        states.append(swap(joined).reshape(state, -1))
    prior = None
    for k in range(CHUNKS):
        result = node_outer(
            *shared, *made[k][3:5], states[k], *made[k][6:8], *inner, found, prior, k, *sizes
        )
        prior = result[:2]
        if k == 0:
            found = [(result[3], result[2])]
    grads = scatter_sum(result[2], result[3:])
    return prior[0], prior[1], grads[0], grads[1]


def solution(mesh):
    return jax.shard_map(
        one_device,
        mesh=mesh,
        in_specs=(
            P("node", "head"),
            P("node", None),
            P("node", None),
            P("head", "node"),
            P("head"),
            P(),
            P("node", "head"),
        ),
        out_specs=(
            P("node", "head"),
            P("node", "head"),
            P(("node", "head"), None),
            P(("node", "head"), None),
        ),
        check_vma=False,
    )
```

```python
import functools
import math

import jax
import jax.numpy as jnp
from jax import lax
from jax.experimental import pallas as pl
from jax.experimental.pallas import tpu as pltpu
from jax.sharding import PartitionSpec as P


LEVELS = 3
VMEM_BYTES = 24 << 20
LANES = 128
SUBLANES = 8
CHUNKS = 2
PARTS = 2

LOG2E = 1.0 / math.log(2.0)

f32 = jnp.float32
bf16 = jnp.bfloat16
NN = (((1,), (0,)), ((), ()))
NT = (((1,), (1,)), ((), ()))


def mm(a, b, dims=NN):
    return lax.dot_general(a, b, dims, preferred_element_type=f32)


def split_two(v):
    high = v.astype(bf16)
    return high, (v - high.astype(f32)).astype(bf16)


def spread_matrix(rows, width, head_width, offset=0):
    row = lax.broadcasted_iota(jnp.int32, (rows, width), 0)
    lane = (lax.broadcasted_iota(jnp.int32, (rows, width), 1) + offset) // head_width
    return (row == lane).astype(bf16)


def head_lanes(columns, first, head_width):
    lane = lax.broadcasted_iota(jnp.int32, columns.shape, 1) // head_width + first
    return jnp.take_along_axis(columns, lane, axis=1)


def pad_lanes(v):
    gap = LANES - v.shape[0]
    if gap:
        v = jnp.concatenate([v, jnp.zeros((gap, v.shape[1]), v.dtype)], axis=0)
    return v.T


def half_steps(step_ref, spread):
    steps = mm(step_ref[...], spread)
    return steps[:1], steps[SUBLANES : SUBLANES + 1]


def states_kernel(
    heads,
    head_width,
    chunk,
    x_ref,
    cot_ref,
    b_ref,
    c_ref,
    step_ref,
    rate_ref,
    send_ref,
    low_ref,
    src_ref,
    grow_ref,
    tail_ref,
    gram_ref,
    keep_ref,
    step_out_ref,
    bt_ref,
    ct_ref,
):
    block = x_ref.shape[1]
    length = step_ref.shape[1]
    middle = length // 2
    index = pl.program_id(0)
    width = heads * head_width

    @pl.when(index == 0)
    def _():
        step = step_ref[...]
        rates = jnp.broadcast_to(rate_ref[...], (LANES, rate_ref.shape[1])).T
        terms = -step * rates[chunk * heads : (chunk + 1) * heads, :1]
        row = lax.broadcasted_iota(jnp.int32, (length, length), 0)
        col = lax.broadcasted_iota(jnp.int32, (length, length), 1)
        upper = (row <= col).astype(bf16)
        first = terms.astype(bf16)
        rest = terms - first.astype(f32)
        second, third = split_two(rest)
        cumulative = mm(third, upper) + mm(second, upper) + mm(first, upper)
        last = cumulative[:, length - 1 :]
        mid = cumulative[:, middle - 1 : middle]
        late = lax.broadcasted_iota(jnp.int32, cumulative.shape, 1) >= middle
        low_ref[...] = pad_lanes(cumulative * LOG2E)
        src_ref[...] = (cumulative - jnp.log(step)) * LOG2E
        grow_ref[...] = pad_lanes(jnp.exp(cumulative - jnp.where(late, mid, 0.0))).astype(bf16)
        tail = jnp.exp(jnp.where(late, last, mid) - cumulative) * step
        tail_ref[...] = pad_lanes(tail).astype(bf16)
        bt_ref[...] = b_ref[...].T
        ct_ref[...] = c_ref[...].T
        total = jnp.exp(jnp.broadcast_to(last, (heads, send_ref.shape[0])))
        send_ref[:, 2 * width :] = pad_lanes(total).astype(bf16)
        each = (heads, SUBLANES)
        steps = [jnp.broadcast_to(mid, each), jnp.broadcast_to(last - mid, each)]
        step_out_ref[...] = pad_lanes(jnp.exp(jnp.concatenate(steps, axis=1))).astype(bf16)
        for rows in (slice(0, middle), slice(middle, length)):
            gram_ref[rows] = mm(c_ref[rows], b_ref[rows], NT).astype(bf16)

    spread = spread_matrix(LANES, block, head_width, index * block)
    tailed = mm(tail_ref[...], spread).astype(bf16) * x_ref[...]
    emitted = mm(grow_ref[...], spread).astype(bf16) * cot_ref[...]
    early_step, late_step = half_steps(step_out_ref, spread)
    early_state = mm(bt_ref[:, :middle], tailed[:middle])
    late_state = mm(bt_ref[:, middle:], tailed[middle:])
    early_seed = mm(ct_ref[:, :middle], emitted[:middle])
    late_seed = mm(ct_ref[:, middle:], emitted[middle:])
    here = pl.ds(pl.multiple_of(index * block, block), block)
    there = pl.ds(pl.multiple_of(index * block + width, LANES), block)
    send_ref[:, here] = (late_step * early_state + late_state).astype(bf16)
    send_ref[:, there] = (early_seed + early_step * late_seed).astype(bf16)
    keep_ref[:, here] = early_state.astype(bf16)
    keep_ref[:, there] = late_seed.astype(bf16)


def node_states(x, cot, b, c, step, rate, chunk, heads, head_width):
    length, state = b.shape
    width = heads * head_width
    block = min(width, 4 * LANES)
    count = width // block
    whole = lambda i: (0, 0)
    return pl.pallas_call(
        functools.partial(states_kernel, heads, head_width, chunk),
        grid=(count,),
        in_specs=[
            pl.BlockSpec((length, block), lambda i: (0, chunk * count + i)),
            pl.BlockSpec((length, block), lambda i: (0, chunk * count + i)),
            pl.BlockSpec((length, state), whole),
            pl.BlockSpec((length, state), whole),
            pl.BlockSpec((heads, length), lambda i: (chunk, 0)),
            pl.BlockSpec(rate.shape, whole),
        ],
        out_specs=[
            pl.BlockSpec((state, 2 * width + LANES), whole),
            pl.BlockSpec((length, LANES), whole),
            pl.BlockSpec((heads, length), whole),
            pl.BlockSpec((length, LANES), whole),
            pl.BlockSpec((length, LANES), whole),
            pl.BlockSpec((length, length // 2), whole),
            pl.BlockSpec((state, 2 * width), whole),
            pl.BlockSpec((2 * SUBLANES, LANES), whole),
        ],
        out_shape=[
            jax.ShapeDtypeStruct((state, 2 * width + LANES), bf16),
            jax.ShapeDtypeStruct((length, LANES), f32),
            jax.ShapeDtypeStruct((heads, length), f32),
            jax.ShapeDtypeStruct((length, LANES), bf16),
            jax.ShapeDtypeStruct((length, LANES), bf16),
            jax.ShapeDtypeStruct((length, length // 2), bf16),
            jax.ShapeDtypeStruct((state, 2 * width), bf16),
            jax.ShapeDtypeStruct((2 * SUBLANES, LANES), bf16),
        ],
        scratch_shapes=[pltpu.VMEM((state, length), bf16), pltpu.VMEM((state, length), bf16)],
        name="node_states",
        cost_estimate=pl.CostEstimate(
            flops=4 * length * state * width,
            bytes_accessed=4 * length * width + 4 * state * width,
            transcendentals=0,
        ),
    )(x, cot, b, c, step, rate)


def inner_kernel(
    head_width,
    first,
    aliased,
    x_ref,
    cot_ref,
    b_ref,
    c_ref,
    given_ref,
    low_ref,
    src_ref,
    *refs,
):
    if aliased:
        refs = refs[2:]
    out_ref, grad_ref, gc_ref, gb_ref, mixed_ref, turned_ref, wa_ref, wb_ref, gram_ref = refs
    length = x_ref.shape[0]
    index = pl.program_id(0)
    pack = LANES // head_width
    pairs = x_ref.shape[1] // LANES
    wide = length // 2
    blocks = wide // LANES
    weights = (wa_ref, wb_ref)

    @pl.when(index == 0)
    def _():
        gram_ref[...] = given_ref[...]
        mixed_ref[...] = jnp.zeros_like(mixed_ref)
        for ref in weights:
            ref[...] = jnp.zeros_like(ref)

    lane = lax.broadcasted_iota(jnp.int32, (1, LANES), 1) // head_width
    causal = lax.broadcasted_iota(jnp.int32, (LANES, LANES), 0) >= lax.broadcasted_iota(
        jnp.int32, (LANES, LANES), 1
    )
    halves = (slice(0, wide), slice(wide, length))
    xs = [x_ref[:, q * LANES : (q + 1) * LANES] for q in range(pairs)]
    turned_cots = [cot_ref[:, q * LANES : (q + 1) * LANES].T for q in range(pairs)]
    low = low_ref[...]

    def decays(h):
        q, a = h // pack, h % pack
        w = weights[h % 2]
        cot = cot_ref[:, q * LANES : (q + 1) * LANES]
        cot = jnp.where(lane == a, cot, jnp.zeros_like(cot))
        place = (first + index * pairs + q) * pack + a
        column = head_lanes(low, place, LANES)
        source = src_ref[pl.ds(place, 1), :]
        for part in halves:
            scores = mm(cot[part], xs[q][part], NT)
            for i in range(blocks):
                here = slice(i * LANES, (i + 1) * LANES)
                rows = slice(part.start + here.start, part.start + here.stop)
                for j in range(i + 1):
                    cols = slice(j * LANES, (j + 1) * LANES)
                    differ = column[rows] - source[:, part.start + cols.start : part.start + cols.stop]
                    if i == j:
                        differ = jnp.where(causal, differ, -jnp.inf)
                    decay = jnp.exp2(differ)
                    w[rows, cols] = decay.astype(bf16) * gram_ref[rows, cols]
                    mixed_ref[rows, cols] += decay * scores[here, cols]
                yield

    def products(h):
        q, a = h // pack, h % pack
        w = weights[h % 2]
        turned = turned_cots[q][a * head_width : (a + 1) * head_width]
        mine = slice(q * LANES + a * head_width, q * LANES + (a + 1) * head_width)
        own = slice(a * head_width, (a + 1) * head_width)
        for part in halves:
            out_ref[part, mine] = mm(w[part], xs[q][part])[:, own].astype(bf16)
            yield
            turned_ref[mine, part] = mm(turned[:, part], w[part]).astype(bf16)
            yield

    def finish(q):
        lanes = slice(q * LANES, (q + 1) * LANES)
        grad_ref[:, lanes] = turned_ref[lanes, :].T

    before = None
    for h in range(pairs * pack):
        for _ in decays(h):
            if before is not None:
                next(before, None)
        if before is not None:
            for _ in before:
                pass
            if h % pack == 0:
                finish(h // pack - 1)
        before = products(h)
    for _ in before:
        pass
    finish(pairs - 1)

    @pl.when(index == pl.num_programs(0) - 1)
    def _():
        for part in halves:
            mixed = mixed_ref[part].astype(bf16)
            gc_ref[part] = mm(mixed, b_ref[part])
            gb_ref[part] = mm(mixed.T, c_ref[part])


def node_inner(x, cot, b, c, gram, low, src, prior, chunk, part, parts, heads, head_width):
    length, state = b.shape
    width = heads * head_width
    block = min(width // parts, 2 * LANES)
    count = width // block // parts
    offset = (chunk * parts + part) * count
    whole = lambda i: (0, 0)
    place = lambda i: (0, offset + i)
    aliased = prior is not None
    operands = [x, cot, b, c, gram, low, src]
    in_specs = [
        pl.BlockSpec((length, block), place),
        pl.BlockSpec((length, block), place),
        pl.BlockSpec((length, state), whole),
        pl.BlockSpec((length, state), whole),
        pl.BlockSpec((length, length // 2), whole),
        pl.BlockSpec((length, LANES), whole),
        pl.BlockSpec((heads, length), whole),
    ]
    aliases = {}
    if aliased:
        aliases = {len(operands): 0, len(operands) + 1: 1}
        operands += list(prior)
        in_specs += [pl.BlockSpec(memory_space=pl.ANY)] * 2
    kernel = functools.partial(inner_kernel, head_width, part * count * block // LANES, aliased)
    return pl.pallas_call(
        kernel,
        grid=(count,),
        in_specs=in_specs,
        out_specs=[
            pl.BlockSpec((length, block), place),
            pl.BlockSpec((length, block), place),
            pl.BlockSpec((length, state), whole),
            pl.BlockSpec((length, state), whole),
        ],
        out_shape=[
            jax.ShapeDtypeStruct(x.shape, bf16),
            jax.ShapeDtypeStruct(x.shape, bf16),
            jax.ShapeDtypeStruct((length, state), f32),
            jax.ShapeDtypeStruct((length, state), f32),
        ],
        scratch_shapes=[
            pltpu.VMEM((length, length // 2), f32),
            pltpu.VMEM((block, length), bf16),
            pltpu.VMEM((length, length // 2), bf16),
            pltpu.VMEM((length, length // 2), bf16),
            pltpu.VMEM((length, length // 2), bf16),
        ],
        input_output_aliases=aliases,
        name="node_inner",
        cost_estimate=pl.CostEstimate(
            flops=24 * length * length * count * block,
            bytes_accessed=12 * length * count * block,
            transcendentals=length * length * heads // parts,
        ),
    )(*operands)


def rank_nodes(parents_ref, rank_ref, half):
    nodes = rank_ref.shape[0]

    def clear(n, carry):
        rank_ref[n] = 0
        return carry

    def mark(n, carry):
        up = parents_ref[n]

        @pl.when(jnp.logical_and(up >= 0, (up >= half) != (n >= half)))
        def _():
            rank_ref[up] = 1

        return carry

    def place(n, count):
        crosses = rank_ref[n]
        rank_ref[n] = jnp.where(crosses > 0, count, -1)
        return count + crosses

    lax.fori_loop(0, nodes, clear, 0)
    lax.fori_loop(0, nodes, mark, 0)
    lax.fori_loop(0, nodes, place, 0)


def widen(narrow, heads, head_width):
    count = narrow.shape[0]
    flat = jnp.concatenate([narrow[n, :1].astype(f32) for n in range(count)], axis=0)
    return mm(flat.astype(bf16), spread_matrix(LANES, heads * head_width, head_width))


def pack_kernel(
    heads, head_width, parents_ref, recv_ref, main_ref, more_ref, decay_ref, slot_ref, chain_ref, rank_ref
):
    half = recv_ref.shape[0]
    width = heads * head_width
    base = lax.axis_index("node") // half * half
    rank_nodes(parents_ref, rank_ref, half)
    decay_ref[...] = widen(recv_ref[:, :, 2 * width :], heads, head_width)
    slot_ref[...] = jnp.zeros_like(slot_ref)
    chain_ref[...] = jnp.zeros_like(chain_ref)

    def inside(n):
        return jnp.logical_and(n >= base, n < base + half)

    def spot(n):
        return jnp.clip(n - base, 0, half - 1)

    def visit(m, carry):
        node = base + m
        flow = recv_ref[m, :, width : 2 * width].astype(f32)
        at = node
        live = jnp.bool_(True)
        for level in range(LEVELS):
            up = parents_ref[at]
            exists = jnp.logical_and(live, up >= 0)
            live = jnp.logical_and(exists, inside(up))
            away = jnp.logical_and(exists, jnp.logical_not(live))

            @pl.when(away)
            def _(flow=flow, up=up):
                slot = rank_ref[up]
                slot_ref[slot] = slot_ref[slot] + flow

            if level < LEVELS - 1:
                flow = flow * jnp.where(live, decay_ref[pl.ds(spot(up), 1)], 1.0)
            at = jnp.where(live, up, at)

        @pl.when(rank_ref[node] >= 0)
        def _():
            total = recv_ref[m, :, :width].astype(f32)
            factor = decay_ref[pl.ds(m, 1)]
            chain = recv_ref[m, :, 2 * width :].astype(f32)
            at = node
            live = jnp.bool_(True)
            for _ in range(LEVELS - 1):
                up = parents_ref[at]
                live = jnp.logical_and(jnp.logical_and(live, up >= 0), inside(up))
                where = spot(up)
                total = total + jnp.where(live, factor * recv_ref[where, :, :width].astype(f32), 0.0)
                factor = factor * jnp.where(live, decay_ref[pl.ds(where, 1)], 1.0)
                chain = chain * jnp.where(live, recv_ref[where, :, 2 * width :].astype(f32), 1.0)
                at = jnp.where(live, up, at)
            slot_ref[rank_ref[node]] = total
            chain_ref[rank_ref[node]] = chain

        return carry

    lax.fori_loop(0, half, visit, 0)
    main = main_ref.shape[0]
    main_ref[:, :, :width] = slot_ref[:main].astype(bf16)
    main_ref[:, :, width:] = chain_ref[:main].astype(bf16)
    more_ref[:, :, :width] = slot_ref[main:].astype(bf16)
    more_ref[:, :, width:] = chain_ref[main:].astype(bf16)


def slot_counts(nodes):
    most = nodes * LEVELS // (LEVELS + 1)
    return most // 2, most - most // 2


def pack_slots(parents, recv, nodes, heads, head_width):
    half, rows, _ = recv.shape
    width = heads * head_width
    main, more = slot_counts(nodes)
    in_specs = [pl.BlockSpec(memory_space=pltpu.SMEM), pl.BlockSpec(memory_space=pltpu.VMEM)]
    kernel = functools.partial(pack_kernel, heads, head_width)
    operands = [parents, recv]
    return pl.pallas_call(
        kernel,
        in_specs=in_specs,
        out_specs=[pl.BlockSpec(memory_space=pltpu.VMEM)] * 2,
        out_shape=[
            jax.ShapeDtypeStruct((main, rows, width + LANES), bf16),
            jax.ShapeDtypeStruct((more, rows, width + LANES), bf16),
        ],
        scratch_shapes=[
            pltpu.VMEM((half, width), f32),
            pltpu.VMEM((main + more, rows, width), f32),
            pltpu.VMEM((main + more, rows, LANES), f32),
            pltpu.SMEM((nodes,), jnp.int32),
        ],
        compiler_params=pltpu.CompilerParams(vmem_limit_bytes=VMEM_BYTES),
        name="pack_slots",
        cost_estimate=pl.CostEstimate(
            flops=20 * half * rows * width,
            bytes_accessed=8 * half * rows * width,
            transcendentals=0,
        ),
    )(*operands)


def join_kernel(
    heads,
    head_width,
    parents_ref,
    recv_ref,
    main_ref,
    more_ref,
    out_ref,
    decay_ref,
    slot_ref,
    chain_ref,
    back_ref,
    rank_ref,
):
    half = recv_ref.shape[0]
    width = heads * head_width
    main = main_ref.shape[0]
    base = lax.axis_index("node") // half * half
    rank_nodes(parents_ref, rank_ref, half)
    decay_ref[...] = widen(recv_ref[:, :, 2 * width :], heads, head_width)
    slot_ref[:main] = main_ref[:, :, :width].astype(f32)
    slot_ref[main:] = more_ref[:, :, :width].astype(f32)
    chain_ref[:main] = widen(main_ref[:, :, width:], heads, head_width)
    chain_ref[main:] = widen(more_ref[:, :, width:], heads, head_width)
    back_ref[...] = jnp.zeros_like(back_ref)

    def inside(n):
        return jnp.logical_and(n >= base, n < base + half)

    def climb(at, flow, start):
        factor = None
        live = jnp.bool_(True)
        for level in range(LEVELS):
            up = parents_ref[at]
            live = jnp.logical_and(live, up >= 0)
            near = jnp.logical_and(live, inside(up))
            far = jnp.logical_and(live, jnp.logical_not(near))
            where = jnp.clip(up - base, 0, half - 1)
            slot = jnp.where(far, rank_ref[jnp.maximum(up, 0)], 0)

            @pl.when(near)
            def _(flow=flow, where=where):
                back_ref[where] = back_ref[where] + flow

            if start is not None:
                value = jnp.where(near, recv_ref[where, :, :width].astype(f32), slot_ref[slot])
                value = jnp.where(live, value, 0.0)
                start = start + (value if factor is None else factor * value)
            if level < LEVELS - 1:
                step = jnp.where(near, decay_ref[pl.ds(where, 1)], chain_ref[pl.ds(slot, 1)])
                flow = flow * step
                factor = step if factor is None else factor * step
                top = jnp.maximum(up, 0)
                for _ in range(LEVELS - 1):
                    above = parents_ref[top]
                    more = jnp.logical_and(far, above >= 0)
                    more = jnp.logical_and(more, jnp.logical_not(inside(above)))
                    top = jnp.where(more, above, top)
                at = top
        return start

    def visit(m, carry):
        node = base + m
        seed = recv_ref[m, :, width : 2 * width].astype(f32)
        start = climb(node, seed, jnp.zeros(seed.shape, f32))
        out_ref[m, :, :width] = start.astype(bf16)

        @pl.when(rank_ref[node] >= 0)
        def _():
            extra = slot_ref[rank_ref[node]]
            back_ref[m] = back_ref[m] + extra
            climb(node, extra * decay_ref[pl.ds(m, 1)], None)

        return carry

    lax.fori_loop(0, half, visit, 0)
    out_ref[:, :, width:] = back_ref[...].astype(bf16)


def join_slots(parents, recv, main, more, nodes, heads, head_width):
    half, rows, _ = recv.shape
    width = heads * head_width
    in_specs = [pl.BlockSpec(memory_space=pltpu.SMEM)] + [pl.BlockSpec(memory_space=pltpu.VMEM)] * 3
    kernel = functools.partial(join_kernel, heads, head_width)
    operands = [parents, recv, main, more]
    slots = main.shape[0] + more.shape[0]
    return pl.pallas_call(
        kernel,
        in_specs=in_specs,
        out_specs=pl.BlockSpec(memory_space=pltpu.VMEM),
        out_shape=jax.ShapeDtypeStruct((half, rows, 2 * width), bf16),
        scratch_shapes=[
            pltpu.VMEM((half, width), f32),
            pltpu.VMEM((slots, rows, width), f32),
            pltpu.VMEM((slots, width), f32),
            pltpu.VMEM((half, rows, width), f32),
            pltpu.SMEM((nodes,), jnp.int32),
        ],
        compiler_params=pltpu.CompilerParams(vmem_limit_bytes=VMEM_BYTES),
        name="join_slots",
        cost_estimate=pl.CostEstimate(
            flops=20 * half * rows * width,
            bytes_accessed=8 * half * rows * width,
            transcendentals=0,
        ),
    )(*operands)


def outer_kernel(
    head_width,
    extras,
    final,
    x_ref,
    cot_ref,
    b_ref,
    c_ref,
    grow_ref,
    tail_ref,
    start_ref,
    back_ref,
    early_ref,
    late_ref,
    step_ref,
    inner_ref,
    grad_ref,
    *refs,
):
    added = refs[: 2 * extras]
    refs = refs[2 * extras :]
    if not final:
        out_ref, gx_ref, gc_ref, gb_ref = refs
    else:
        out_ref, gx_ref = refs[2:4]
        owns = refs[4:6]
        pieces = refs[6:-2]
        gc_ref, gb_ref = refs[-2:]
    block = x_ref.shape[1]
    index = pl.program_id(0)

    @pl.when(index == 0)
    def _():
        gc_ref[...] = sum(ref[...] for ref in added[:extras])
        gb_ref[...] = sum(ref[...] for ref in added[extras:])

    spread = spread_matrix(LANES, block, head_width, index * block)
    grow_wide = mm(grow_ref[...], spread)
    tail_wide = mm(tail_ref[...], spread)
    early_step, late_step = half_steps(step_ref, spread)
    start = start_ref[...]
    back = back_ref[...]
    starts = (start, (early_step * start.astype(f32) + early_ref[...].astype(f32)).astype(bf16))
    backs = ((late_step * back.astype(f32) + late_ref[...].astype(f32)).astype(bf16), back)
    middle = x_ref.shape[0] // 2
    for n, part in enumerate((slice(0, middle), slice(middle, 2 * middle))):
        grow = grow_wide[part]
        tail = tail_wide[part]
        carried = grow * mm(c_ref[part], starts[n])
        out_ref[part] = (inner_ref[part].astype(f32) + carried).astype(bf16)
        carried = tail * mm(b_ref[part], backs[n])
        gx_ref[part] = (grad_ref[part].astype(f32) + carried).astype(bf16)
        gc_ref[part] += mm(grow.astype(bf16) * cot_ref[part], starts[n], NT)
        gb_ref[part] += mm(tail.astype(bf16) * x_ref[part], backs[n], NT)

    if final:

        @pl.when(index == pl.num_programs(0) - 1)
        def _():
            size = len(pieces) + 1
            me = lax.axis_index("head")
            rows = owns[0].shape[0]
            for shift in range(size):
                at = pl.multiple_of(lax.rem(me + shift, size) * rows, rows)
                for n, ref in enumerate((gb_ref, gc_ref)):
                    if shift == 0:
                        owns[n][...] = ref[pl.ds(at, rows)]
                    else:
                        pieces[shift - 1][n] = ref[pl.ds(at, rows)].astype(bf16)


def node_outer(
    x, cot, b, c, grow, tail, states, keep, steps, inner, grad, found, prior, chunk, heads, head_width
):
    length, state = b.shape
    width = heads * head_width
    block = min(width, 4 * LANES)
    count = width // block
    whole = lambda i: (0, 0)
    spot = lambda i: (0, i)
    place = lambda i: (0, chunk * count + i)
    final = prior is not None
    operands = [x, cot, b, c, grow, tail, states, states, keep, keep, steps, inner, grad]
    in_specs = [
        pl.BlockSpec((length, block), place),
        pl.BlockSpec((length, block), place),
        pl.BlockSpec((length, state), whole),
        pl.BlockSpec((length, state), whole),
        pl.BlockSpec((length, LANES), whole),
        pl.BlockSpec((length, LANES), whole),
        pl.BlockSpec((state, block), spot),
        pl.BlockSpec((state, block), lambda i: (0, count + i)),
        pl.BlockSpec((state, block), spot),
        pl.BlockSpec((state, block), lambda i: (0, count + i)),
        pl.BlockSpec((2 * SUBLANES, LANES), whole),
        pl.BlockSpec((length, block), place),
        pl.BlockSpec((length, block), place),
    ]
    operands += [v[1] for v in found] + [v[0] for v in found]
    in_specs += [pl.BlockSpec((length, state), whole)] * (2 * len(found))
    out_specs = [pl.BlockSpec((length, block), place)] * 2
    out_shape = [jax.ShapeDtypeStruct(x.shape, bf16)] * 2
    grads = jax.ShapeDtypeStruct((length, state), f32)
    scratch = []
    aliases = {}
    if final:
        aliases = {len(operands): 0, len(operands) + 1: 1}
        operands += list(prior)
        in_specs += [pl.BlockSpec(memory_space=pl.ANY)] * 2
        size = lax.axis_size("head")
        kept = (2, length // size, state)
        cube = lambda i: (0, 0, 0)
        out_specs += [pl.BlockSpec(kept[1:], whole)] * 2
        out_specs += [pl.BlockSpec(kept, cube)] * (size - 1)
        out_shape += [jax.ShapeDtypeStruct(kept[1:], f32)] * 2
        out_shape += [jax.ShapeDtypeStruct(kept, bf16)] * (size - 1)
        scratch = [pltpu.VMEM((length, state), f32)] * 2
    else:
        out_specs += [pl.BlockSpec((length, state), whole)] * 2
        out_shape += [grads] * 2
    kernel = functools.partial(outer_kernel, head_width, len(found), final)
    return pl.pallas_call(
        kernel,
        grid=(count,),
        in_specs=in_specs,
        out_specs=out_specs,
        out_shape=out_shape,
        scratch_shapes=scratch,
        input_output_aliases=aliases,
        name="node_outer",
        cost_estimate=pl.CostEstimate(
            flops=8 * length * state * width,
            bytes_accessed=12 * length * width,
            transcendentals=0,
        ),
    )(*operands)


def scatter_sum(owns, pieces):
    size = lax.axis_size("head")
    for shift, piece in enumerate(pieces, 1):
        pairs = [(i, (i + shift) % size) for i in range(size)]
        moved = lax.ppermute(piece, "head", pairs).astype(f32)
        owns = [own + moved[n] for n, own in enumerate(owns)]
    return owns


def one_device(inputs, b_matrix, c_matrix, step_size, decay_rate, parents, cotangent):
    state = b_matrix.shape[1]
    head_count = step_size.shape[0]
    head_width = inputs.shape[1] // head_count
    nodes = lax.axis_size("node")
    heads = head_count // CHUNKS
    half = nodes // 2
    rate = decay_rate[None, :]
    groups = [list(range(half)), list(range(half, nodes))]
    across = [(n, (n + half) % nodes) for n in range(nodes)]

    def swap(v):
        return lax.all_to_all(
            v.reshape(half, state // half, v.shape[-1]),
            "node",
            split_axis=0,
            concat_axis=0,
            tiled=True,
            axis_index_groups=groups,
        )

    def cross(v):
        return lax.ppermute(v, "node", across)

    places = jnp.arange(nodes)
    child = jnp.logical_and(
        parents[:, None] == places[None, :],
        (places[:, None] < half) != (places[None, :] < half),
    )
    crossing = jnp.sum(jnp.any(child, axis=0).astype(jnp.int32))
    crowded = crossing > slot_counts(nodes)[0]

    shared = (inputs, cotangent, b_matrix, c_matrix)
    sizes = (heads, head_width)
    made = []
    for k in range(CHUNKS):
        made.append(node_states(*shared, step_size, rate, k, *sizes))
    received = [swap(made[k][0]) for k in range(CHUNKS)]
    found = []
    prior = None
    for k in range(CHUNKS):
        for part in range(PARTS):
            *prior, gc, gb = node_inner(
                *shared, made[0][5], made[k][1], made[k][2], prior, k, part, PARTS, *sizes
            )
            found.append((gb, gc))
    inner = prior
    packed = []
    for k in range(CHUNKS):
        main, more = pack_slots(parents, received[k], nodes, *sizes)
        packed.append((main, more, cross(main)))
    others = lax.cond(
        crowded,
        lambda vs: tuple(cross(v) for v in vs),
        lambda vs: vs,
        tuple(p[1] for p in packed),
    )
    states = []
    for k in range(CHUNKS):
        joined = join_slots(parents, received[k], packed[k][2], others[k], nodes, *sizes)
        states.append(swap(joined).reshape(state, -1))
    prior = None
    for k in range(CHUNKS):
        result = node_outer(
            *shared, *made[k][3:5], states[k], *made[k][6:8], *inner, found, prior, k, *sizes
        )
        prior = result[:2]
        if k == 0:
            found = [(result[3], result[2])]
    grads = scatter_sum(result[2:4], result[4:])
    return prior[0], prior[1], grads[0], grads[1]


def solution(mesh):
    return jax.shard_map(
        one_device,
        mesh=mesh,
        in_specs=(
            P("node", "head"),
            P("node", None),
            P("node", None),
            P("head", "node"),
            P("head"),
            P(),
            P("node", "head"),
        ),
        out_specs=(
            P("node", "head"),
            P("node", "head"),
            P(("node", "head"), None),
            P(("node", "head"), None),
        ),
        check_vma=False,
    )
```

```python
import functools
import math

import jax
import jax.numpy as jnp
from jax import lax
from jax.experimental import pallas as pl
from jax.experimental.pallas import tpu as pltpu
from jax.sharding import PartitionSpec as P


LEVELS = 3
VMEM_BYTES = 24 << 20
LANES = 128
SUBLANES = 8
CHUNKS = 2
PARTS = 2

LOG2E = 1.0 / math.log(2.0)

f32 = jnp.float32
bf16 = jnp.bfloat16
NN = (((1,), (0,)), ((), ()))
NT = (((1,), (1,)), ((), ()))


def mm(a, b, dims=NN):
    return lax.dot_general(a, b, dims, preferred_element_type=f32)


def split_two(v):
    high = v.astype(bf16)
    return high, (v - high.astype(f32)).astype(bf16)


def spread_matrix(rows, width, head_width, offset=0):
    row = lax.broadcasted_iota(jnp.int32, (rows, width), 0)
    lane = (lax.broadcasted_iota(jnp.int32, (rows, width), 1) + offset) // head_width
    return (row == lane).astype(bf16)


def head_lanes(columns, first, head_width):
    lane = lax.broadcasted_iota(jnp.int32, columns.shape, 1) // head_width + first
    return jnp.take_along_axis(columns, lane, axis=1)


def pad_lanes(v):
    gap = LANES - v.shape[0]
    if gap:
        v = jnp.concatenate([v, jnp.zeros((gap, v.shape[1]), v.dtype)], axis=0)
    return v.T


def half_steps(step_ref, spread):
    steps = mm(step_ref[...], spread)
    return steps[:1], steps[SUBLANES : SUBLANES + 1]


class Copies:
    def __init__(self, sems):
        self.sems = sems
        self.made = []

    def start(self, source, target):
        copy = pltpu.make_async_copy(source, target, self.sems.at[len(self.made)])
        copy.start()
        self.made.append(copy)
        return copy


def wait_all(copies):
    for copy in copies:
        copy.wait()


def states_kernel(heads, head_width, chunk, block, *refs):
    x_hbm, cot_hbm, b_hbm, c_hbm, step_hbm, rate_hbm = refs[:6]
    outs = refs[6:14]
    x_ref, cot_ref, b_ref, c_ref, step_ref, rate_ref = refs[14:20]
    send_ref, low_ref, src_ref, grow_ref, tail_ref, gram_ref, keep_ref, steps_ref = refs[20:28]
    sems = refs[28]
    length = step_ref.shape[1]
    middle = length // 2
    width = heads * head_width
    count = width // block
    copies = Copies(sems)
    first_in = [
        copies.start(step_hbm.at[pl.ds(chunk * heads, heads)], step_ref),
        copies.start(rate_hbm, rate_ref),
    ]
    later_in = [copies.start(b_hbm, b_ref), copies.start(c_hbm, c_ref)]
    loads = []
    for i in range(count):
        lanes = pl.ds(i * block, block)
        there = pl.ds(chunk * width + i * block, block)
        loads.append(
            [
                copies.start(x_hbm.at[:, there], x_ref.at[:, lanes]),
                copies.start(cot_hbm.at[:, there], cot_ref.at[:, lanes]),
            ]
        )
    wait_all(first_in)
    step = step_ref[...]
    rates = jnp.broadcast_to(rate_ref[...], (LANES, rate_ref.shape[1])).T
    terms = -step * rates[chunk * heads : (chunk + 1) * heads, :1]
    row = lax.broadcasted_iota(jnp.int32, (length, length), 0)
    col = lax.broadcasted_iota(jnp.int32, (length, length), 1)
    upper = (row <= col).astype(bf16)
    first = terms.astype(bf16)
    rest = terms - first.astype(f32)
    second, third = split_two(rest)
    cumulative = mm(third, upper) + mm(second, upper) + mm(first, upper)
    last = cumulative[:, length - 1 :]
    mid = cumulative[:, middle - 1 : middle]
    late = lax.broadcasted_iota(jnp.int32, cumulative.shape, 1) >= middle
    low_ref[...] = pad_lanes(cumulative * LOG2E)
    src_ref[...] = (cumulative - jnp.log(step)) * LOG2E
    grow_ref[...] = pad_lanes(jnp.exp(cumulative - jnp.where(late, mid, 0.0))).astype(bf16)
    tail = jnp.exp(jnp.where(late, last, mid) - cumulative) * step
    tail_ref[...] = pad_lanes(tail).astype(bf16)
    total = jnp.exp(jnp.broadcast_to(last, (heads, send_ref.shape[0])))
    send_ref[:, 2 * width :] = pad_lanes(total).astype(bf16)
    each = (heads, SUBLANES)
    steps = [jnp.broadcast_to(mid, each), jnp.broadcast_to(last - mid, each)]
    steps_ref[...] = pad_lanes(jnp.exp(jnp.concatenate(steps, axis=1))).astype(bf16)
    wait_all(later_in)
    b_turned = b_ref[...].T
    c_turned = c_ref[...].T
    for rows in (slice(0, middle), slice(middle, length)):
        gram_ref[rows] = mm(c_ref[rows], b_ref[rows], NT).astype(bf16)
    small = (1, 2, 3, 4, 5, 7)
    made = (send_ref, low_ref, src_ref, grow_ref, tail_ref, gram_ref, keep_ref, steps_ref)
    stores = []
    ready = [(made[n], outs[n]) for n in small]
    ready.append((send_ref.at[:, pl.ds(2 * width, LANES)], outs[0].at[:, pl.ds(2 * width, LANES)]))
    for i in range(count):
        here = pl.ds(i * block, block)
        there = pl.ds(i * block + width, block)
        wait_all(loads[i])
        spread = spread_matrix(LANES, block, head_width, i * block)
        tailed = mm(tail_ref[...], spread).astype(bf16) * x_ref[:, here]
        emitted = mm(grow_ref[...], spread).astype(bf16) * cot_ref[:, here]
        early_step, late_step = half_steps(steps_ref, spread)
        early_state = mm(b_turned[:, :middle], tailed[:middle])
        late_state = mm(b_turned[:, middle:], tailed[middle:])
        early_seed = mm(c_turned[:, :middle], emitted[:middle])
        late_seed = mm(c_turned[:, middle:], emitted[middle:])
        send_ref[:, here] = (late_step * early_state + late_state).astype(bf16)
        send_ref[:, there] = (early_seed + early_step * late_seed).astype(bf16)
        keep_ref[:, here] = early_state.astype(bf16)
        keep_ref[:, there] = late_seed.astype(bf16)
        stores += [copies.start(*pair) for pair in ready]
        ready = [
            (ref.at[:, lanes], out.at[:, lanes])
            for ref, out in ((send_ref, outs[0]), (keep_ref, outs[6]))
            for lanes in (here, there)
        ]
    stores += [copies.start(*pair) for pair in ready]
    wait_all(stores)


def node_states(x, cot, b, c, step, rate, chunk, heads, head_width):
    length, state = b.shape
    width = heads * head_width
    block = min(width, 4 * LANES)
    count = width // block
    out_shape = [
        jax.ShapeDtypeStruct((state, 2 * width + LANES), bf16),
        jax.ShapeDtypeStruct((length, LANES), f32),
        jax.ShapeDtypeStruct((heads, length), f32),
        jax.ShapeDtypeStruct((length, LANES), bf16),
        jax.ShapeDtypeStruct((length, LANES), bf16),
        jax.ShapeDtypeStruct((length, length // 2), bf16),
        jax.ShapeDtypeStruct((state, 2 * width), bf16),
        jax.ShapeDtypeStruct((2 * SUBLANES, LANES), bf16),
    ]
    held = [(length, width)] * 2 + [b.shape] * 2
    scratch = [pltpu.VMEM(shape, bf16) for shape in held]
    scratch += [pltpu.VMEM((heads, length), f32), pltpu.VMEM(rate.shape, f32)]
    scratch += [pltpu.VMEM(v.shape, v.dtype) for v in out_shape]
    scratch.append(pltpu.SemaphoreType.DMA((11 + 6 * count,)))
    anywhere = pl.BlockSpec(memory_space=pl.ANY)
    return pl.pallas_call(
        functools.partial(states_kernel, heads, head_width, chunk, block),
        in_specs=[anywhere] * 6,
        out_specs=[anywhere] * len(out_shape),
        out_shape=out_shape,
        scratch_shapes=scratch,
        name="node_states",
        cost_estimate=pl.CostEstimate(
            flops=4 * length * state * width,
            bytes_accessed=4 * length * width + 8 * state * width,
            transcendentals=0,
        ),
    )(x, cot, b, c, step, rate)


def inner_kernel(
    head_width,
    first,
    aliased,
    x_ref,
    cot_ref,
    b_ref,
    c_ref,
    given_ref,
    low_ref,
    src_ref,
    *refs,
):
    if aliased:
        refs = refs[2:]
    out_ref, grad_ref, gc_ref, gb_ref, mixed_ref, turned_ref, wa_ref, wb_ref, gram_ref = refs
    length = x_ref.shape[0]
    index = pl.program_id(0)
    pack = LANES // head_width
    pairs = x_ref.shape[1] // LANES
    wide = length // 2
    blocks = wide // LANES
    weights = (wa_ref, wb_ref)

    @pl.when(index == 0)
    def _():
        gram_ref[...] = given_ref[...]
        mixed_ref[...] = jnp.zeros_like(mixed_ref)
        for ref in weights:
            ref[...] = jnp.zeros_like(ref)

    lane = lax.broadcasted_iota(jnp.int32, (1, LANES), 1) // head_width
    causal = lax.broadcasted_iota(jnp.int32, (LANES, LANES), 0) >= lax.broadcasted_iota(
        jnp.int32, (LANES, LANES), 1
    )
    halves = (slice(0, wide), slice(wide, length))
    xs = [x_ref[:, q * LANES : (q + 1) * LANES] for q in range(pairs)]
    turned_cots = [cot_ref[:, q * LANES : (q + 1) * LANES].T for q in range(pairs)]
    low = low_ref[...]

    def decays(h):
        q, a = h // pack, h % pack
        w = weights[h % 2]
        cot = cot_ref[:, q * LANES : (q + 1) * LANES]
        cot = jnp.where(lane == a, cot, jnp.zeros_like(cot))
        place = (first + index * pairs + q) * pack + a
        column = head_lanes(low, place, LANES)
        source = src_ref[pl.ds(place, 1), :]
        for part in halves:
            scores = mm(cot[part], xs[q][part], NT)
            for i in range(blocks):
                here = slice(i * LANES, (i + 1) * LANES)
                rows = slice(part.start + here.start, part.start + here.stop)
                for j in range(i + 1):
                    cols = slice(j * LANES, (j + 1) * LANES)
                    differ = column[rows] - source[:, part.start + cols.start : part.start + cols.stop]
                    if i == j:
                        differ = jnp.where(causal, differ, -jnp.inf)
                    decay = jnp.exp2(differ)
                    w[rows, cols] = decay.astype(bf16) * gram_ref[rows, cols]
                    mixed_ref[rows, cols] += decay * scores[here, cols]
                yield

    def products(h):
        q, a = h // pack, h % pack
        w = weights[h % 2]
        turned = turned_cots[q][a * head_width : (a + 1) * head_width]
        mine = slice(q * LANES + a * head_width, q * LANES + (a + 1) * head_width)
        own = slice(a * head_width, (a + 1) * head_width)
        for part in halves:
            out_ref[part, mine] = mm(w[part], xs[q][part])[:, own].astype(bf16)
            yield
            turned_ref[mine, part] = mm(turned[:, part], w[part]).astype(bf16)
            yield

    def finish(q):
        lanes = slice(q * LANES, (q + 1) * LANES)
        grad_ref[:, lanes] = turned_ref[lanes, :].T

    before = None
    for h in range(pairs * pack):
        for _ in decays(h):
            if before is not None:
                next(before, None)
        if before is not None:
            for _ in before:
                pass
            if h % pack == 0:
                finish(h // pack - 1)
        before = products(h)
    for _ in before:
        pass
    finish(pairs - 1)

    @pl.when(index == pl.num_programs(0) - 1)
    def _():
        for part in halves:
            mixed = mixed_ref[part].astype(bf16)
            gc_ref[part] = mm(mixed, b_ref[part])
            gb_ref[part] = mm(mixed.T, c_ref[part])


def node_inner(x, cot, b, c, gram, low, src, prior, chunk, part, parts, heads, head_width):
    length, state = b.shape
    width = heads * head_width
    block = min(width // parts, 2 * LANES)
    count = width // block // parts
    offset = (chunk * parts + part) * count
    whole = lambda i: (0, 0)
    place = lambda i: (0, offset + i)
    aliased = prior is not None
    operands = [x, cot, b, c, gram, low, src]
    in_specs = [
        pl.BlockSpec((length, block), place),
        pl.BlockSpec((length, block), place),
        pl.BlockSpec((length, state), whole),
        pl.BlockSpec((length, state), whole),
        pl.BlockSpec((length, length // 2), whole),
        pl.BlockSpec((length, LANES), whole),
        pl.BlockSpec((heads, length), whole),
    ]
    aliases = {}
    if aliased:
        aliases = {len(operands): 0, len(operands) + 1: 1}
        operands += list(prior)
        in_specs += [pl.BlockSpec(memory_space=pl.ANY)] * 2
    kernel = functools.partial(inner_kernel, head_width, part * count * block // LANES, aliased)
    return pl.pallas_call(
        kernel,
        grid=(count,),
        in_specs=in_specs,
        out_specs=[
            pl.BlockSpec((length, block), place),
            pl.BlockSpec((length, block), place),
            pl.BlockSpec((length, state), whole),
            pl.BlockSpec((length, state), whole),
        ],
        out_shape=[
            jax.ShapeDtypeStruct(x.shape, bf16),
            jax.ShapeDtypeStruct(x.shape, bf16),
            jax.ShapeDtypeStruct((length, state), f32),
            jax.ShapeDtypeStruct((length, state), f32),
        ],
        scratch_shapes=[
            pltpu.VMEM((length, length // 2), f32),
            pltpu.VMEM((block, length), bf16),
            pltpu.VMEM((length, length // 2), bf16),
            pltpu.VMEM((length, length // 2), bf16),
            pltpu.VMEM((length, length // 2), bf16),
        ],
        input_output_aliases=aliases,
        name="node_inner",
        cost_estimate=pl.CostEstimate(
            flops=24 * length * length * count * block,
            bytes_accessed=12 * length * count * block,
            transcendentals=length * length * heads // parts,
        ),
    )(*operands)


def rank_nodes(parents_ref, rank_ref, half):
    nodes = rank_ref.shape[0]

    def clear(n, carry):
        rank_ref[n] = 0
        return carry

    def mark(n, carry):
        up = parents_ref[n]

        @pl.when(jnp.logical_and(up >= 0, (up >= half) != (n >= half)))
        def _():
            rank_ref[up] = 1

        return carry

    def place(n, count):
        crosses = rank_ref[n]
        rank_ref[n] = jnp.where(crosses > 0, count, -1)
        return count + crosses

    lax.fori_loop(0, nodes, clear, 0)
    lax.fori_loop(0, nodes, mark, 0)
    lax.fori_loop(0, nodes, place, 0)


def widen(narrow, heads, head_width):
    count = narrow.shape[0]
    flat = jnp.concatenate([narrow[n, :1].astype(f32) for n in range(count)], axis=0)
    return mm(flat.astype(bf16), spread_matrix(LANES, heads * head_width, head_width))


def pack_kernel(
    heads, head_width, parents_ref, recv_ref, main_ref, more_ref, decay_ref, slot_ref, chain_ref, rank_ref
):
    half = recv_ref.shape[0]
    width = heads * head_width
    base = lax.axis_index("node") // half * half
    rank_nodes(parents_ref, rank_ref, half)
    decay_ref[...] = widen(recv_ref[:, :, 2 * width :], heads, head_width)
    slot_ref[...] = jnp.zeros_like(slot_ref)
    chain_ref[...] = jnp.zeros_like(chain_ref)

    def inside(n):
        return jnp.logical_and(n >= base, n < base + half)

    def spot(n):
        return jnp.clip(n - base, 0, half - 1)

    def visit(m, carry):
        node = base + m
        flow = recv_ref[m, :, width : 2 * width].astype(f32)
        at = node
        live = jnp.bool_(True)
        for level in range(LEVELS):
            up = parents_ref[at]
            exists = jnp.logical_and(live, up >= 0)
            live = jnp.logical_and(exists, inside(up))
            away = jnp.logical_and(exists, jnp.logical_not(live))

            @pl.when(away)
            def _(flow=flow, up=up):
                slot = rank_ref[up]
                slot_ref[slot] = slot_ref[slot] + flow

            if level < LEVELS - 1:
                flow = flow * jnp.where(live, decay_ref[pl.ds(spot(up), 1)], 1.0)
            at = jnp.where(live, up, at)

        @pl.when(rank_ref[node] >= 0)
        def _():
            total = recv_ref[m, :, :width].astype(f32)
            factor = decay_ref[pl.ds(m, 1)]
            chain = recv_ref[m, :, 2 * width :].astype(f32)
            at = node
            live = jnp.bool_(True)
            for _ in range(LEVELS - 1):
                up = parents_ref[at]
                live = jnp.logical_and(jnp.logical_and(live, up >= 0), inside(up))
                where = spot(up)
                total = total + jnp.where(live, factor * recv_ref[where, :, :width].astype(f32), 0.0)
                factor = factor * jnp.where(live, decay_ref[pl.ds(where, 1)], 1.0)
                chain = chain * jnp.where(live, recv_ref[where, :, 2 * width :].astype(f32), 1.0)
                at = jnp.where(live, up, at)
            slot_ref[rank_ref[node]] = total
            chain_ref[rank_ref[node]] = chain

        return carry

    lax.fori_loop(0, half, visit, 0)
    main = main_ref.shape[0]
    main_ref[:, :, :width] = slot_ref[:main].astype(bf16)
    main_ref[:, :, width:] = chain_ref[:main].astype(bf16)
    more_ref[:, :, :width] = slot_ref[main:].astype(bf16)
    more_ref[:, :, width:] = chain_ref[main:].astype(bf16)


def slot_counts(nodes):
    most = nodes * LEVELS // (LEVELS + 1)
    return most // 2, most - most // 2


def pack_slots(parents, recv, nodes, heads, head_width):
    half, rows, _ = recv.shape
    width = heads * head_width
    main, more = slot_counts(nodes)
    in_specs = [pl.BlockSpec(memory_space=pltpu.SMEM), pl.BlockSpec(memory_space=pltpu.VMEM)]
    kernel = functools.partial(pack_kernel, heads, head_width)
    operands = [parents, recv]
    return pl.pallas_call(
        kernel,
        in_specs=in_specs,
        out_specs=[pl.BlockSpec(memory_space=pltpu.VMEM)] * 2,
        out_shape=[
            jax.ShapeDtypeStruct((main, rows, width + LANES), bf16),
            jax.ShapeDtypeStruct((more, rows, width + LANES), bf16),
        ],
        scratch_shapes=[
            pltpu.VMEM((half, width), f32),
            pltpu.VMEM((main + more, rows, width), f32),
            pltpu.VMEM((main + more, rows, LANES), f32),
            pltpu.SMEM((nodes,), jnp.int32),
        ],
        compiler_params=pltpu.CompilerParams(vmem_limit_bytes=VMEM_BYTES),
        name="pack_slots",
        cost_estimate=pl.CostEstimate(
            flops=20 * half * rows * width,
            bytes_accessed=8 * half * rows * width,
            transcendentals=0,
        ),
    )(*operands)


def join_kernel(
    heads,
    head_width,
    parents_ref,
    recv_ref,
    main_ref,
    more_ref,
    out_ref,
    decay_ref,
    slot_ref,
    chain_ref,
    back_ref,
    rank_ref,
):
    half = recv_ref.shape[0]
    width = heads * head_width
    main = main_ref.shape[0]
    base = lax.axis_index("node") // half * half
    rank_nodes(parents_ref, rank_ref, half)
    decay_ref[...] = widen(recv_ref[:, :, 2 * width :], heads, head_width)
    slot_ref[:main] = main_ref[:, :, :width].astype(f32)
    slot_ref[main:] = more_ref[:, :, :width].astype(f32)
    chain_ref[:main] = widen(main_ref[:, :, width:], heads, head_width)
    chain_ref[main:] = widen(more_ref[:, :, width:], heads, head_width)
    back_ref[...] = jnp.zeros_like(back_ref)

    def inside(n):
        return jnp.logical_and(n >= base, n < base + half)

    def climb(at, flow, start):
        factor = None
        live = jnp.bool_(True)
        for level in range(LEVELS):
            up = parents_ref[at]
            live = jnp.logical_and(live, up >= 0)
            near = jnp.logical_and(live, inside(up))
            far = jnp.logical_and(live, jnp.logical_not(near))
            where = jnp.clip(up - base, 0, half - 1)
            slot = jnp.where(far, rank_ref[jnp.maximum(up, 0)], 0)

            @pl.when(near)
            def _(flow=flow, where=where):
                back_ref[where] = back_ref[where] + flow

            if start is not None:
                value = jnp.where(near, recv_ref[where, :, :width].astype(f32), slot_ref[slot])
                value = jnp.where(live, value, 0.0)
                start = start + (value if factor is None else factor * value)
            if level < LEVELS - 1:
                step = jnp.where(near, decay_ref[pl.ds(where, 1)], chain_ref[pl.ds(slot, 1)])
                flow = flow * step
                factor = step if factor is None else factor * step
                top = jnp.maximum(up, 0)
                for _ in range(LEVELS - 1):
                    above = parents_ref[top]
                    more = jnp.logical_and(far, above >= 0)
                    more = jnp.logical_and(more, jnp.logical_not(inside(above)))
                    top = jnp.where(more, above, top)
                at = top
        return start

    def visit(m, carry):
        node = base + m
        seed = recv_ref[m, :, width : 2 * width].astype(f32)
        start = climb(node, seed, jnp.zeros(seed.shape, f32))
        out_ref[m, :, :width] = start.astype(bf16)

        @pl.when(rank_ref[node] >= 0)
        def _():
            extra = slot_ref[rank_ref[node]]
            back_ref[m] = back_ref[m] + extra
            climb(node, extra * decay_ref[pl.ds(m, 1)], None)

        return carry

    lax.fori_loop(0, half, visit, 0)
    out_ref[:, :, width:] = back_ref[...].astype(bf16)


def join_slots(parents, recv, main, more, nodes, heads, head_width):
    half, rows, _ = recv.shape
    width = heads * head_width
    in_specs = [pl.BlockSpec(memory_space=pltpu.SMEM)] + [pl.BlockSpec(memory_space=pltpu.VMEM)] * 3
    kernel = functools.partial(join_kernel, heads, head_width)
    operands = [parents, recv, main, more]
    slots = main.shape[0] + more.shape[0]
    return pl.pallas_call(
        kernel,
        in_specs=in_specs,
        out_specs=pl.BlockSpec(memory_space=pltpu.VMEM),
        out_shape=jax.ShapeDtypeStruct((half, rows, 2 * width), bf16),
        scratch_shapes=[
            pltpu.VMEM((half, width), f32),
            pltpu.VMEM((slots, rows, width), f32),
            pltpu.VMEM((slots, width), f32),
            pltpu.VMEM((half, rows, width), f32),
            pltpu.SMEM((nodes,), jnp.int32),
        ],
        compiler_params=pltpu.CompilerParams(vmem_limit_bytes=VMEM_BYTES),
        name="join_slots",
        cost_estimate=pl.CostEstimate(
            flops=20 * half * rows * width,
            bytes_accessed=8 * half * rows * width,
            transcendentals=0,
        ),
    )(*operands)


def outer_kernel(heads, head_width, chunk, block, extras, final, *refs):
    given = 13 + 2 * extras
    sources = refs[:given]
    refs = refs[given:]
    if final:
        outs, owns, pieces = refs[2:4], refs[4:6], refs[6 : -(given + 5)]
        gc_ref, gb_ref = refs[-2:]
        refs = refs[-(given + 5) : -2]
    else:
        outs, (gc_ref, gb_ref) = refs[:2], refs[2:4]
        refs = refs[4:]
    held, results, sems = refs[:given], refs[given : given + 2], refs[-1]
    b_ref, c_ref, grow_ref, tail_ref, step_ref = held[:5]
    added = held[5 : 5 + 2 * extras]
    x_ref, cot_ref, inner_ref, grad_ref, start_ref, back_ref, early_ref, late_ref = held[-8:]
    width = heads * head_width
    count = width // block
    middle = x_ref.shape[0] // 2
    copies = Copies(sems)
    small = [copies.start(sources[n], held[n]) for n in range(5)]
    loads = []
    for i in range(count):
        lanes = pl.ds(i * block, block)
        over = pl.ds(width + i * block, block)
        column = pl.ds(chunk * width + i * block, block)
        spots = (column,) * 4 + (lanes, over) * 2
        loads.append(
            [
                copies.start(source.at[:, spot], ref.at[:, lanes])
                for source, spot, ref in zip(sources[-8:], spots, held[-8:])
            ]
        )
    sums = [copies.start(sources[5 + n], ref) for n, ref in enumerate(added)]
    wait_all(small)
    stores = []
    ready = []
    for i in range(count):
        here = pl.ds(i * block, block)
        column = pl.ds(chunk * width + i * block, block)
        wait_all(loads[i])
        spread = spread_matrix(LANES, block, head_width, i * block)
        grow_wide = mm(grow_ref[...], spread)
        tail_wide = mm(tail_ref[...], spread)
        early_step, late_step = half_steps(step_ref, spread)
        start = start_ref[:, here]
        back = back_ref[:, here]
        after = (early_step * start.astype(f32) + early_ref[:, here].astype(f32)).astype(bf16)
        before = (late_step * back.astype(f32) + late_ref[:, here].astype(f32)).astype(bf16)
        for n, part in enumerate((slice(0, middle), slice(middle, 2 * middle))):
            grow = grow_wide[part]
            tail = tail_wide[part]
            begin = (start, after)[n]
            end = (before, back)[n]
            carried = grow * mm(c_ref[part], begin)
            results[0][part, here] = (inner_ref[part, here].astype(f32) + carried).astype(bf16)
            carried = tail * mm(b_ref[part], end)
            results[1][part, here] = (grad_ref[part, here].astype(f32) + carried).astype(bf16)
            gc = mm(grow.astype(bf16) * cot_ref[part, here], begin, NT)
            gb = mm(tail.astype(bf16) * x_ref[part, here], end, NT)
            if i == 0:
                gc_ref[part] = gc
                gb_ref[part] = gb
            else:
                gc_ref[part] += gc
                gb_ref[part] += gb
        stores += [copies.start(*pair) for pair in ready]
        ready = [
            (result.at[:, here], out.at[:, column]) for result, out in zip(results, outs)
        ]
    wait_all(sums)
    gc_ref[...] += sum(ref[...] for ref in added[:extras])
    gb_ref[...] += sum(ref[...] for ref in added[extras:])
    stores += [copies.start(*pair) for pair in ready]
    if final:
        size = len(pieces) + 1
        me = lax.axis_index("head")
        rows = owns[0].shape[0]
        for shift in range(size):
            at = pl.multiple_of(lax.rem(me + shift, size) * rows, rows)
            for n, ref in enumerate((gb_ref, gc_ref)):
                if shift == 0:
                    owns[n][...] = ref[pl.ds(at, rows)]
                else:
                    pieces[shift - 1][n] = ref[pl.ds(at, rows)].astype(bf16)
    wait_all(stores)


def node_outer(
    x, cot, b, c, grow, tail, states, keep, steps, inner, grad, found, prior, chunk, heads, head_width
):
    length, state = b.shape
    width = heads * head_width
    block = min(width, 4 * LANES)
    count = width // block
    final = prior is not None
    small = [b, c, grow, tail, steps] + [v[1] for v in found] + [v[0] for v in found]
    operands = small + [x, cot, inner, grad, states, states, keep, keep]
    given = len(operands)
    anywhere = pl.BlockSpec(memory_space=pl.ANY)
    local = pl.BlockSpec(memory_space=pltpu.VMEM)
    out_specs = [anywhere] * 2
    out_shape = [jax.ShapeDtypeStruct(x.shape, bf16)] * 2
    scratch = [pltpu.VMEM(v.shape, v.dtype) for v in small]
    scratch += [pltpu.VMEM((length, width), bf16)] * 4 + [pltpu.VMEM((state, width), bf16)] * 4
    scratch += [pltpu.VMEM((length, width), bf16)] * 2
    scratch.append(pltpu.SemaphoreType.DMA((len(small) + 10 * count,)))
    aliases = {}
    if final:
        aliases = {given: 0, given + 1: 1}
        operands += list(prior)
        size = lax.axis_size("head")
        kept = (2, length // size, state)
        out_specs += [local] * (size + 1)
        out_shape += [jax.ShapeDtypeStruct(kept[1:], f32)] * 2
        out_shape += [jax.ShapeDtypeStruct(kept, bf16)] * (size - 1)
        scratch += [pltpu.VMEM((length, state), f32)] * 2
    else:
        out_specs += [local] * 2
        out_shape += [jax.ShapeDtypeStruct((length, state), f32)] * 2
    return pl.pallas_call(
        functools.partial(outer_kernel, heads, head_width, chunk, block, len(found), final),
        in_specs=[anywhere] * len(operands),
        out_specs=out_specs,
        out_shape=out_shape,
        scratch_shapes=scratch,
        input_output_aliases=aliases,
        name="node_outer",
        cost_estimate=pl.CostEstimate(
            flops=8 * length * state * width,
            bytes_accessed=14 * length * width,
            transcendentals=0,
        ),
    )(*operands)


def scatter_sum(owns, pieces):
    size = lax.axis_size("head")
    for shift, piece in enumerate(pieces, 1):
        pairs = [(i, (i + shift) % size) for i in range(size)]
        moved = lax.ppermute(piece, "head", pairs).astype(f32)
        owns = [own + moved[n] for n, own in enumerate(owns)]
    return owns


def one_device(inputs, b_matrix, c_matrix, step_size, decay_rate, parents, cotangent):
    state = b_matrix.shape[1]
    head_count = step_size.shape[0]
    head_width = inputs.shape[1] // head_count
    nodes = lax.axis_size("node")
    heads = head_count // CHUNKS
    half = nodes // 2
    rate = decay_rate[None, :]
    groups = [list(range(half)), list(range(half, nodes))]
    across = [(n, (n + half) % nodes) for n in range(nodes)]

    def swap(v):
        return lax.all_to_all(
            v.reshape(half, state // half, v.shape[-1]),
            "node",
            split_axis=0,
            concat_axis=0,
            tiled=True,
            axis_index_groups=groups,
        )

    def cross(v):
        return lax.ppermute(v, "node", across)

    places = jnp.arange(nodes)
    child = jnp.logical_and(
        parents[:, None] == places[None, :],
        (places[:, None] < half) != (places[None, :] < half),
    )
    crossing = jnp.sum(jnp.any(child, axis=0).astype(jnp.int32))
    main_count, more_count = slot_counts(nodes)
    few = more_count // 3
    crowded = (crossing > main_count).astype(jnp.int32) + (crossing > main_count + few)

    shared = (inputs, cotangent, b_matrix, c_matrix)
    sizes = (heads, head_width)
    made = []
    for k in range(CHUNKS):
        made.append(node_states(*shared, step_size, rate, k, *sizes))
    received = [swap(made[k][0]) for k in range(CHUNKS)]
    found = []
    prior = None
    for k in range(CHUNKS):
        for part in range(PARTS):
            *prior, gc, gb = node_inner(
                *shared, made[0][5], made[k][1], made[k][2], prior, k, part, PARTS, *sizes
            )
            found.append((gb, gc))
    inner = prior
    packed = []
    for k in range(CHUNKS):
        main, more = pack_slots(parents, received[k], nodes, *sizes)
        packed.append((main, more, cross(main)))
    others = lax.switch(
        crowded,
        (
            lambda vs: vs,
            lambda vs: tuple(jnp.concatenate([cross(v[:few]), v[few:]]) for v in vs),
            lambda vs: tuple(cross(v) for v in vs),
        ),
        tuple(p[1] for p in packed),
    )
    states = []
    for k in range(CHUNKS):
        joined = join_slots(parents, received[k], packed[k][2], others[k], nodes, *sizes)
        states.append(swap(joined).reshape(state, -1))
    prior = None
    for k in range(CHUNKS):
        result = node_outer(
            *shared, *made[k][3:5], states[k], *made[k][6:8], *inner, found, prior, k, *sizes
        )
        prior = result[:2]
        if k == 0:
            found = [(result[3], result[2])]
    grads = scatter_sum(result[2:4], result[4:])
    return prior[0], prior[1], grads[0], grads[1]


def solution(mesh):
    return jax.shard_map(
        one_device,
        mesh=mesh,
        in_specs=(
            P("node", "head"),
            P("node", None),
            P("node", None),
            P("head", "node"),
            P("head"),
            P(),
            P("node", "head"),
        ),
        out_specs=(
            P("node", "head"),
            P("node", "head"),
            P(("node", "head"), None),
            P(("node", "head"), None),
        ),
        check_vma=False,
    )
```

```python
import functools
import math

import jax
import jax.numpy as jnp
from jax import lax
from jax.experimental import pallas as pl
from jax.experimental.pallas import tpu as pltpu
from jax.sharding import PartitionSpec as P


LEVELS = 3
VMEM_BYTES = 24 << 20
LANES = 128
SUBLANES = 8
CHUNKS = 2
PARTS = 2

LOG2E = 1.0 / math.log(2.0)

f32 = jnp.float32
bf16 = jnp.bfloat16
NN = (((1,), (0,)), ((), ()))
NT = (((1,), (1,)), ((), ()))


def mm(a, b, dims=NN):
    return lax.dot_general(a, b, dims, preferred_element_type=f32)


def split_two(v):
    high = v.astype(bf16)
    return high, (v - high.astype(f32)).astype(bf16)


def spread_matrix(rows, width, head_width, offset=0):
    row = lax.broadcasted_iota(jnp.int32, (rows, width), 0)
    lane = (lax.broadcasted_iota(jnp.int32, (rows, width), 1) + offset) // head_width
    return (row == lane).astype(bf16)


def head_lanes(columns, first, head_width):
    lane = lax.broadcasted_iota(jnp.int32, columns.shape, 1) // head_width + first
    return jnp.take_along_axis(columns, lane, axis=1)


def pad_lanes(v):
    gap = LANES - v.shape[0]
    if gap:
        v = jnp.concatenate([v, jnp.zeros((gap, v.shape[1]), v.dtype)], axis=0)
    return v.T


def half_steps(step_ref, spread):
    steps = mm(step_ref[...], spread)
    return steps[:1], steps[SUBLANES : SUBLANES + 1]


class Copies:
    def __init__(self, sems):
        self.sems = sems
        self.made = []

    def start(self, source, target):
        copy = pltpu.make_async_copy(source, target, self.sems.at[len(self.made)])
        copy.start()
        self.made.append(copy)
        return copy


def wait_all(copies):
    for copy in copies:
        copy.wait()


def states_kernel(heads, head_width, chunk, block, *refs):
    x_hbm, cot_hbm, b_hbm, c_hbm, step_hbm, rate_hbm = refs[:6]
    outs = refs[6:14]
    x_ref, cot_ref, b_ref, c_ref, step_ref, rate_ref = refs[14:20]
    send_ref, low_ref, src_ref, grow_ref, tail_ref, gram_ref, keep_ref, steps_ref = refs[20:28]
    sems = refs[28]
    length = step_ref.shape[1]
    middle = length // 2
    width = heads * head_width
    count = width // block
    copies = Copies(sems)
    first_in = [
        copies.start(step_hbm.at[pl.ds(chunk * heads, heads)], step_ref),
        copies.start(rate_hbm, rate_ref),
    ]
    later_in = [copies.start(b_hbm, b_ref), copies.start(c_hbm, c_ref)]
    loads = []
    for i in range(count):
        lanes = pl.ds(i * block, block)
        there = pl.ds(chunk * width + i * block, block)
        loads.append(
            [
                copies.start(x_hbm.at[:, there], x_ref.at[:, lanes]),
                copies.start(cot_hbm.at[:, there], cot_ref.at[:, lanes]),
            ]
        )
    wait_all(first_in)
    step = step_ref[...]
    rates = jnp.broadcast_to(rate_ref[...], (LANES, rate_ref.shape[1])).T
    terms = -step * rates[chunk * heads : (chunk + 1) * heads, :1]
    row = lax.broadcasted_iota(jnp.int32, (length, length), 0)
    col = lax.broadcasted_iota(jnp.int32, (length, length), 1)
    upper = (row <= col).astype(bf16)
    first = terms.astype(bf16)
    rest = terms - first.astype(f32)
    second, third = split_two(rest)
    cumulative = mm(third, upper) + mm(second, upper) + mm(first, upper)
    last = cumulative[:, length - 1 :]
    mid = cumulative[:, middle - 1 : middle]
    late = lax.broadcasted_iota(jnp.int32, cumulative.shape, 1) >= middle
    low_ref[...] = pad_lanes(cumulative * LOG2E)
    src_ref[...] = (cumulative - jnp.log(step)) * LOG2E
    grow_ref[...] = pad_lanes(jnp.exp(cumulative - jnp.where(late, mid, 0.0))).astype(bf16)
    tail = jnp.exp(jnp.where(late, last, mid) - cumulative) * step
    tail_ref[...] = pad_lanes(tail).astype(bf16)
    total = jnp.exp(jnp.broadcast_to(last, (heads, send_ref.shape[0])))
    send_ref[:, 2 * width :] = pad_lanes(total).astype(bf16)
    each = (heads, SUBLANES)
    steps = [jnp.broadcast_to(mid, each), jnp.broadcast_to(last - mid, each)]
    steps_ref[...] = pad_lanes(jnp.exp(jnp.concatenate(steps, axis=1))).astype(bf16)
    wait_all(later_in)
    b_turned = b_ref[...].T
    c_turned = c_ref[...].T
    for rows in (slice(0, middle), slice(middle, length)):
        gram_ref[rows] = mm(c_ref[rows], b_ref[rows], NT).astype(bf16)
    small = (1, 2, 3, 4, 5, 7)
    made = (send_ref, low_ref, src_ref, grow_ref, tail_ref, gram_ref, keep_ref, steps_ref)
    stores = []
    ready = [(made[n], outs[n]) for n in small]
    ready.append((send_ref.at[:, pl.ds(2 * width, LANES)], outs[0].at[:, pl.ds(2 * width, LANES)]))
    for i in range(count):
        here = pl.ds(i * block, block)
        there = pl.ds(i * block + width, block)
        wait_all(loads[i])
        spread = spread_matrix(LANES, block, head_width, i * block)
        tailed = mm(tail_ref[...], spread).astype(bf16) * x_ref[:, here]
        emitted = mm(grow_ref[...], spread).astype(bf16) * cot_ref[:, here]
        early_step, late_step = half_steps(steps_ref, spread)
        early_state = mm(b_turned[:, :middle], tailed[:middle])
        late_state = mm(b_turned[:, middle:], tailed[middle:])
        early_seed = mm(c_turned[:, :middle], emitted[:middle])
        late_seed = mm(c_turned[:, middle:], emitted[middle:])
        send_ref[:, here] = (late_step * early_state + late_state).astype(bf16)
        send_ref[:, there] = (early_seed + early_step * late_seed).astype(bf16)
        keep_ref[:, here] = early_state.astype(bf16)
        keep_ref[:, there] = late_seed.astype(bf16)
        stores += [copies.start(*pair) for pair in ready]
        ready = [
            (ref.at[:, lanes], out.at[:, lanes])
            for ref, out in ((send_ref, outs[0]), (keep_ref, outs[6]))
            for lanes in (here, there)
        ]
    stores += [copies.start(*pair) for pair in ready]
    wait_all(stores)


def node_states(x, cot, b, c, step, rate, chunk, heads, head_width):
    length, state = b.shape
    width = heads * head_width
    block = min(width, 4 * LANES)
    count = width // block
    out_shape = [
        jax.ShapeDtypeStruct((state, 2 * width + LANES), bf16),
        jax.ShapeDtypeStruct((length, LANES), f32),
        jax.ShapeDtypeStruct((heads, length), f32),
        jax.ShapeDtypeStruct((length, LANES), bf16),
        jax.ShapeDtypeStruct((length, LANES), bf16),
        jax.ShapeDtypeStruct((length, length // 2), bf16),
        jax.ShapeDtypeStruct((state, 2 * width), bf16),
        jax.ShapeDtypeStruct((2 * SUBLANES, LANES), bf16),
    ]
    held = [(length, width)] * 2 + [b.shape] * 2
    scratch = [pltpu.VMEM(shape, bf16) for shape in held]
    scratch += [pltpu.VMEM((heads, length), f32), pltpu.VMEM(rate.shape, f32)]
    scratch += [pltpu.VMEM(v.shape, v.dtype) for v in out_shape]
    scratch.append(pltpu.SemaphoreType.DMA((11 + 6 * count,)))
    anywhere = pl.BlockSpec(memory_space=pl.ANY)
    return pl.pallas_call(
        functools.partial(states_kernel, heads, head_width, chunk, block),
        in_specs=[anywhere] * 6,
        out_specs=[anywhere] * len(out_shape),
        out_shape=out_shape,
        scratch_shapes=scratch,
        name="node_states",
        cost_estimate=pl.CostEstimate(
            flops=4 * length * state * width,
            bytes_accessed=4 * length * width + 8 * state * width,
            transcendentals=0,
        ),
    )(x, cot, b, c, step, rate)


def inner_kernel(
    head_width,
    first,
    aliased,
    x_ref,
    cot_ref,
    b_ref,
    c_ref,
    given_ref,
    low_ref,
    src_ref,
    *refs,
):
    if aliased:
        refs = refs[2:]
    out_ref, grad_ref, gc_ref, gb_ref, mixed_ref, turned_ref, wa_ref, wb_ref, gram_ref = refs
    length = x_ref.shape[0]
    index = pl.program_id(0)
    pack = LANES // head_width
    pairs = x_ref.shape[1] // LANES
    wide = length // 2
    blocks = wide // LANES
    weights = (wa_ref, wb_ref)

    @pl.when(index == 0)
    def _():
        gram_ref[...] = given_ref[...]
        mixed_ref[...] = jnp.zeros_like(mixed_ref)
        for ref in weights:
            ref[...] = jnp.zeros_like(ref)

    lane = lax.broadcasted_iota(jnp.int32, (1, LANES), 1) // head_width
    causal = lax.broadcasted_iota(jnp.int32, (LANES, LANES), 0) >= lax.broadcasted_iota(
        jnp.int32, (LANES, LANES), 1
    )
    halves = (slice(0, wide), slice(wide, length))
    xs = [x_ref[:, q * LANES : (q + 1) * LANES] for q in range(pairs)]
    turned_cots = [cot_ref[:, q * LANES : (q + 1) * LANES].T for q in range(pairs)]
    low = low_ref[...]

    def decays(h):
        q, a = h // pack, h % pack
        w = weights[h % 2]
        cot = cot_ref[:, q * LANES : (q + 1) * LANES]
        cot = jnp.where(lane == a, cot, jnp.zeros_like(cot))
        place = (first + index * pairs + q) * pack + a
        column = head_lanes(low, place, LANES)
        source = src_ref[pl.ds(place, 1), :]
        for part in halves:
            scores = mm(cot[part], xs[q][part], NT)
            for i in range(blocks):
                here = slice(i * LANES, (i + 1) * LANES)
                rows = slice(part.start + here.start, part.start + here.stop)
                for j in range(i + 1):
                    cols = slice(j * LANES, (j + 1) * LANES)
                    differ = column[rows] - source[:, part.start + cols.start : part.start + cols.stop]
                    if i == j:
                        differ = jnp.where(causal, differ, -jnp.inf)
                    decay = jnp.exp2(differ)
                    w[rows, cols] = decay.astype(bf16) * gram_ref[rows, cols]
                    mixed_ref[rows, cols] += decay * scores[here, cols]
                yield

    def products(h):
        q, a = h // pack, h % pack
        w = weights[h % 2]
        turned = turned_cots[q][a * head_width : (a + 1) * head_width]
        mine = slice(q * LANES + a * head_width, q * LANES + (a + 1) * head_width)
        own = slice(a * head_width, (a + 1) * head_width)
        for part in halves:
            out_ref[part, mine] = mm(w[part], xs[q][part])[:, own].astype(bf16)
            yield
            turned_ref[mine, part] = mm(turned[:, part], w[part]).astype(bf16)
            yield

    def finish(q):
        lanes = slice(q * LANES, (q + 1) * LANES)
        grad_ref[:, lanes] = turned_ref[lanes, :].T

    before = None
    for h in range(pairs * pack):
        for _ in decays(h):
            if before is not None:
                next(before, None)
        if before is not None:
            for _ in before:
                pass
            if h % pack == 0:
                finish(h // pack - 1)
        before = products(h)
    for _ in before:
        pass
    finish(pairs - 1)

    @pl.when(index == pl.num_programs(0) - 1)
    def _():
        for part in halves:
            mixed = mixed_ref[part].astype(bf16)
            gc_ref[part] = mm(mixed, b_ref[part])
            gb_ref[part] = mm(mixed.T, c_ref[part])


def node_inner(x, cot, b, c, gram, low, src, prior, chunk, part, parts, heads, head_width):
    length, state = b.shape
    width = heads * head_width
    block = min(width // parts, 2 * LANES)
    count = width // block // parts
    offset = (chunk * parts + part) * count
    whole = lambda i: (0, 0)
    place = lambda i: (0, offset + i)
    aliased = prior is not None
    operands = [x, cot, b, c, gram, low, src]
    in_specs = [
        pl.BlockSpec((length, block), place),
        pl.BlockSpec((length, block), place),
        pl.BlockSpec((length, state), whole),
        pl.BlockSpec((length, state), whole),
        pl.BlockSpec((length, length // 2), whole),
        pl.BlockSpec((length, LANES), whole),
        pl.BlockSpec((heads, length), whole),
    ]
    aliases = {}
    if aliased:
        aliases = {len(operands): 0, len(operands) + 1: 1}
        operands += list(prior)
        in_specs += [pl.BlockSpec(memory_space=pl.ANY)] * 2
    kernel = functools.partial(inner_kernel, head_width, part * count * block // LANES, aliased)
    return pl.pallas_call(
        kernel,
        grid=(count,),
        in_specs=in_specs,
        out_specs=[
            pl.BlockSpec((length, block), place),
            pl.BlockSpec((length, block), place),
            pl.BlockSpec((length, state), whole),
            pl.BlockSpec((length, state), whole),
        ],
        out_shape=[
            jax.ShapeDtypeStruct(x.shape, bf16),
            jax.ShapeDtypeStruct(x.shape, bf16),
            jax.ShapeDtypeStruct((length, state), f32),
            jax.ShapeDtypeStruct((length, state), f32),
        ],
        scratch_shapes=[
            pltpu.VMEM((length, length // 2), f32),
            pltpu.VMEM((block, length), bf16),
            pltpu.VMEM((length, length // 2), bf16),
            pltpu.VMEM((length, length // 2), bf16),
            pltpu.VMEM((length, length // 2), bf16),
        ],
        input_output_aliases=aliases,
        name="node_inner",
        cost_estimate=pl.CostEstimate(
            flops=24 * length * length * count * block,
            bytes_accessed=12 * length * count * block,
            transcendentals=length * length * heads // parts,
        ),
    )(*operands)


def rank_nodes(parents_ref, rank_ref, half):
    nodes = rank_ref.shape[0]

    def clear(n, carry):
        rank_ref[n] = 0
        return carry

    def mark(n, carry):
        up = parents_ref[n]

        @pl.when(jnp.logical_and(up >= 0, (up >= half) != (n >= half)))
        def _():
            rank_ref[up] = 1

        return carry

    def place(n, count):
        crosses = rank_ref[n]
        rank_ref[n] = jnp.where(crosses > 0, count, -1)
        return count + crosses

    lax.fori_loop(0, nodes, clear, 0)
    lax.fori_loop(0, nodes, mark, 0)
    lax.fori_loop(0, nodes, place, 0)


def widen(narrow, heads, head_width):
    count = narrow.shape[0]
    flat = jnp.concatenate([narrow[n, :1].astype(f32) for n in range(count)], axis=0)
    return mm(flat.astype(bf16), spread_matrix(LANES, heads * head_width, head_width))


def pack_kernel(
    heads, head_width, parents_ref, recv_ref, main_ref, more_ref, decay_ref, slot_ref, chain_ref, rank_ref
):
    half = recv_ref.shape[0]
    width = heads * head_width
    base = lax.axis_index("node") // half * half
    rank_nodes(parents_ref, rank_ref, half)
    decay_ref[...] = widen(recv_ref[:, :, 2 * width :], heads, head_width)
    slot_ref[...] = jnp.zeros_like(slot_ref)
    chain_ref[...] = jnp.zeros_like(chain_ref)

    def inside(n):
        return jnp.logical_and(n >= base, n < base + half)

    def spot(n):
        return jnp.clip(n - base, 0, half - 1)

    def visit(m, carry):
        node = base + m
        flow = recv_ref[m, :, width : 2 * width].astype(f32)
        at = node
        live = jnp.bool_(True)
        for level in range(LEVELS):
            up = parents_ref[at]
            exists = jnp.logical_and(live, up >= 0)
            live = jnp.logical_and(exists, inside(up))
            away = jnp.logical_and(exists, jnp.logical_not(live))

            @pl.when(away)
            def _(flow=flow, up=up):
                slot = rank_ref[up]
                slot_ref[slot] = slot_ref[slot] + flow

            if level < LEVELS - 1:
                flow = flow * jnp.where(live, decay_ref[pl.ds(spot(up), 1)], 1.0)
            at = jnp.where(live, up, at)

        @pl.when(rank_ref[node] >= 0)
        def _():
            total = recv_ref[m, :, :width].astype(f32)
            factor = decay_ref[pl.ds(m, 1)]
            chain = recv_ref[m, :, 2 * width :].astype(f32)
            at = node
            live = jnp.bool_(True)
            for _ in range(LEVELS - 1):
                up = parents_ref[at]
                live = jnp.logical_and(jnp.logical_and(live, up >= 0), inside(up))
                where = spot(up)
                total = total + jnp.where(live, factor * recv_ref[where, :, :width].astype(f32), 0.0)
                factor = factor * jnp.where(live, decay_ref[pl.ds(where, 1)], 1.0)
                chain = chain * jnp.where(live, recv_ref[where, :, 2 * width :].astype(f32), 1.0)
                at = jnp.where(live, up, at)
            slot_ref[rank_ref[node]] = total
            chain_ref[rank_ref[node]] = chain

        return carry

    lax.fori_loop(0, half, visit, 0)
    main = main_ref.shape[0]
    main_ref[:, :, :width] = slot_ref[:main].astype(bf16)
    main_ref[:, :, width:] = chain_ref[:main].astype(bf16)
    more_ref[:, :, :width] = slot_ref[main:].astype(bf16)
    more_ref[:, :, width:] = chain_ref[main:].astype(bf16)


def slot_counts(nodes):
    most = nodes * LEVELS // (LEVELS + 1)
    main = nodes // 2 - nodes // 16
    return main, most - main


def pack_slots(parents, recv, nodes, heads, head_width):
    half, rows, _ = recv.shape
    width = heads * head_width
    main, more = slot_counts(nodes)
    in_specs = [pl.BlockSpec(memory_space=pltpu.SMEM), pl.BlockSpec(memory_space=pltpu.VMEM)]
    kernel = functools.partial(pack_kernel, heads, head_width)
    operands = [parents, recv]
    return pl.pallas_call(
        kernel,
        in_specs=in_specs,
        out_specs=[pl.BlockSpec(memory_space=pltpu.VMEM)] * 2,
        out_shape=[
            jax.ShapeDtypeStruct((main, rows, width + LANES), bf16),
            jax.ShapeDtypeStruct((more, rows, width + LANES), bf16),
        ],
        scratch_shapes=[
            pltpu.VMEM((half, width), f32),
            pltpu.VMEM((main + more, rows, width), f32),
            pltpu.VMEM((main + more, rows, LANES), f32),
            pltpu.SMEM((nodes,), jnp.int32),
        ],
        compiler_params=pltpu.CompilerParams(vmem_limit_bytes=VMEM_BYTES),
        name="pack_slots",
        cost_estimate=pl.CostEstimate(
            flops=20 * half * rows * width,
            bytes_accessed=8 * half * rows * width,
            transcendentals=0,
        ),
    )(*operands)


def join_kernel(
    heads,
    head_width,
    parents_ref,
    recv_ref,
    main_ref,
    more_ref,
    out_ref,
    decay_ref,
    slot_ref,
    chain_ref,
    back_ref,
    rank_ref,
):
    half = recv_ref.shape[0]
    width = heads * head_width
    main = main_ref.shape[0]
    base = lax.axis_index("node") // half * half
    rank_nodes(parents_ref, rank_ref, half)
    decay_ref[...] = widen(recv_ref[:, :, 2 * width :], heads, head_width)
    slot_ref[:main] = main_ref[:, :, :width].astype(f32)
    slot_ref[main:] = more_ref[:, :, :width].astype(f32)
    chain_ref[:main] = widen(main_ref[:, :, width:], heads, head_width)
    chain_ref[main:] = widen(more_ref[:, :, width:], heads, head_width)
    back_ref[...] = jnp.zeros_like(back_ref)

    def inside(n):
        return jnp.logical_and(n >= base, n < base + half)

    def climb(at, flow, start):
        factor = None
        live = jnp.bool_(True)
        for level in range(LEVELS):
            up = parents_ref[at]
            live = jnp.logical_and(live, up >= 0)
            near = jnp.logical_and(live, inside(up))
            far = jnp.logical_and(live, jnp.logical_not(near))
            where = jnp.clip(up - base, 0, half - 1)
            slot = jnp.where(far, rank_ref[jnp.maximum(up, 0)], 0)

            @pl.when(near)
            def _(flow=flow, where=where):
                back_ref[where] = back_ref[where] + flow

            if start is not None:
                value = jnp.where(near, recv_ref[where, :, :width].astype(f32), slot_ref[slot])
                value = jnp.where(live, value, 0.0)
                start = start + (value if factor is None else factor * value)
            if level < LEVELS - 1:
                step = jnp.where(near, decay_ref[pl.ds(where, 1)], chain_ref[pl.ds(slot, 1)])
                flow = flow * step
                factor = step if factor is None else factor * step
                top = jnp.maximum(up, 0)
                for _ in range(LEVELS - 1):
                    above = parents_ref[top]
                    more = jnp.logical_and(far, above >= 0)
                    more = jnp.logical_and(more, jnp.logical_not(inside(above)))
                    top = jnp.where(more, above, top)
                at = top
        return start

    def visit(m, carry):
        node = base + m
        seed = recv_ref[m, :, width : 2 * width].astype(f32)
        start = climb(node, seed, jnp.zeros(seed.shape, f32))
        out_ref[m, :, :width] = start.astype(bf16)

        @pl.when(rank_ref[node] >= 0)
        def _():
            extra = slot_ref[rank_ref[node]]
            back_ref[m] = back_ref[m] + extra
            climb(node, extra * decay_ref[pl.ds(m, 1)], None)

        return carry

    lax.fori_loop(0, half, visit, 0)
    out_ref[:, :, width:] = back_ref[...].astype(bf16)


def join_slots(parents, recv, main, more, nodes, heads, head_width):
    half, rows, _ = recv.shape
    width = heads * head_width
    in_specs = [pl.BlockSpec(memory_space=pltpu.SMEM)] + [pl.BlockSpec(memory_space=pltpu.VMEM)] * 3
    kernel = functools.partial(join_kernel, heads, head_width)
    operands = [parents, recv, main, more]
    slots = main.shape[0] + more.shape[0]
    return pl.pallas_call(
        kernel,
        in_specs=in_specs,
        out_specs=pl.BlockSpec(memory_space=pltpu.VMEM),
        out_shape=jax.ShapeDtypeStruct((half, rows, 2 * width), bf16),
        scratch_shapes=[
            pltpu.VMEM((half, width), f32),
            pltpu.VMEM((slots, rows, width), f32),
            pltpu.VMEM((slots, width), f32),
            pltpu.VMEM((half, rows, width), f32),
            pltpu.SMEM((nodes,), jnp.int32),
        ],
        compiler_params=pltpu.CompilerParams(vmem_limit_bytes=VMEM_BYTES),
        name="join_slots",
        cost_estimate=pl.CostEstimate(
            flops=20 * half * rows * width,
            bytes_accessed=8 * half * rows * width,
            transcendentals=0,
        ),
    )(*operands)


def outer_kernel(heads, head_width, chunk, block, extras, final, *refs):
    given = 13 + 2 * extras
    sources = refs[:given]
    refs = refs[given:]
    if final:
        outs, owns, pieces = refs[2:4], refs[4:6], refs[6 : -(given + 5)]
        gc_ref, gb_ref = refs[-2:]
        refs = refs[-(given + 5) : -2]
    else:
        outs, (gc_ref, gb_ref) = refs[:2], refs[2:4]
        refs = refs[4:]
    held, results, sems = refs[:given], refs[given : given + 2], refs[-1]
    b_ref, c_ref, grow_ref, tail_ref, step_ref = held[:5]
    added = held[5 : 5 + 2 * extras]
    x_ref, cot_ref, inner_ref, grad_ref, start_ref, back_ref, early_ref, late_ref = held[-8:]
    width = heads * head_width
    count = width // block
    middle = x_ref.shape[0] // 2
    copies = Copies(sems)
    small = [copies.start(sources[n], held[n]) for n in range(5)]
    loads = []
    for i in range(count):
        lanes = pl.ds(i * block, block)
        over = pl.ds(width + i * block, block)
        column = pl.ds(chunk * width + i * block, block)
        spots = (column,) * 4 + (lanes, over) * 2
        loads.append(
            [
                copies.start(source.at[:, spot], ref.at[:, lanes])
                for source, spot, ref in zip(sources[-8:], spots, held[-8:])
            ]
        )
    sums = [copies.start(sources[5 + n], ref) for n, ref in enumerate(added)]
    wait_all(small)
    stores = []
    ready = []
    for i in range(count):
        here = pl.ds(i * block, block)
        column = pl.ds(chunk * width + i * block, block)
        wait_all(loads[i])
        spread = spread_matrix(LANES, block, head_width, i * block)
        grow_wide = mm(grow_ref[...], spread)
        tail_wide = mm(tail_ref[...], spread)
        early_step, late_step = half_steps(step_ref, spread)
        start = start_ref[:, here]
        back = back_ref[:, here]
        after = (early_step * start.astype(f32) + early_ref[:, here].astype(f32)).astype(bf16)
        before = (late_step * back.astype(f32) + late_ref[:, here].astype(f32)).astype(bf16)
        for n, part in enumerate((slice(0, middle), slice(middle, 2 * middle))):
            grow = grow_wide[part]
            tail = tail_wide[part]
            begin = (start, after)[n]
            end = (before, back)[n]
            carried = grow * mm(c_ref[part], begin)
            results[0][part, here] = (inner_ref[part, here].astype(f32) + carried).astype(bf16)
            carried = tail * mm(b_ref[part], end)
            results[1][part, here] = (grad_ref[part, here].astype(f32) + carried).astype(bf16)
            gc = mm(grow.astype(bf16) * cot_ref[part, here], begin, NT)
            gb = mm(tail.astype(bf16) * x_ref[part, here], end, NT)
            if i == 0:
                gc_ref[part] = gc
                gb_ref[part] = gb
            else:
                gc_ref[part] += gc
                gb_ref[part] += gb
        stores += [copies.start(*pair) for pair in ready]
        ready = [
            (result.at[:, here], out.at[:, column]) for result, out in zip(results, outs)
        ]
    wait_all(sums)
    gc_ref[...] += sum(ref[...] for ref in added[:extras])
    gb_ref[...] += sum(ref[...] for ref in added[extras:])
    stores += [copies.start(*pair) for pair in ready]
    if final:
        size = len(pieces) + 1
        me = lax.axis_index("head")
        rows = owns[0].shape[0]
        for shift in range(size):
            at = pl.multiple_of(lax.rem(me + shift, size) * rows, rows)
            for n, ref in enumerate((gb_ref, gc_ref)):
                if shift == 0:
                    owns[n][...] = ref[pl.ds(at, rows)]
                else:
                    pieces[shift - 1][n] = ref[pl.ds(at, rows)].astype(bf16)
    wait_all(stores)


def node_outer(
    x, cot, b, c, grow, tail, states, keep, steps, inner, grad, found, prior, chunk, heads, head_width
):
    length, state = b.shape
    width = heads * head_width
    block = min(width, 4 * LANES)
    count = width // block
    final = prior is not None
    small = [b, c, grow, tail, steps] + [v[1] for v in found] + [v[0] for v in found]
    operands = small + [x, cot, inner, grad, states, states, keep, keep]
    given = len(operands)
    anywhere = pl.BlockSpec(memory_space=pl.ANY)
    local = pl.BlockSpec(memory_space=pltpu.VMEM)
    out_specs = [anywhere] * 2
    out_shape = [jax.ShapeDtypeStruct(x.shape, bf16)] * 2
    scratch = [pltpu.VMEM(v.shape, v.dtype) for v in small]
    scratch += [pltpu.VMEM((length, width), bf16)] * 4 + [pltpu.VMEM((state, width), bf16)] * 4
    scratch += [pltpu.VMEM((length, width), bf16)] * 2
    scratch.append(pltpu.SemaphoreType.DMA((len(small) + 10 * count,)))
    aliases = {}
    if final:
        aliases = {given: 0, given + 1: 1}
        operands += list(prior)
        size = lax.axis_size("head")
        kept = (2, length // size, state)
        out_specs += [local] * (size + 1)
        out_shape += [jax.ShapeDtypeStruct(kept[1:], f32)] * 2
        out_shape += [jax.ShapeDtypeStruct(kept, bf16)] * (size - 1)
        scratch += [pltpu.VMEM((length, state), f32)] * 2
    else:
        out_specs += [local] * 2
        out_shape += [jax.ShapeDtypeStruct((length, state), f32)] * 2
    return pl.pallas_call(
        functools.partial(outer_kernel, heads, head_width, chunk, block, len(found), final),
        in_specs=[anywhere] * len(operands),
        out_specs=out_specs,
        out_shape=out_shape,
        scratch_shapes=scratch,
        input_output_aliases=aliases,
        name="node_outer",
        cost_estimate=pl.CostEstimate(
            flops=8 * length * state * width,
            bytes_accessed=14 * length * width,
            transcendentals=0,
        ),
    )(*operands)


def scatter_sum(owns, pieces):
    size = lax.axis_size("head")
    for shift, piece in enumerate(pieces, 1):
        pairs = [(i, (i + shift) % size) for i in range(size)]
        moved = lax.ppermute(piece, "head", pairs).astype(f32)
        owns = [own + moved[n] for n, own in enumerate(owns)]
    return owns


def one_device(inputs, b_matrix, c_matrix, step_size, decay_rate, parents, cotangent):
    state = b_matrix.shape[1]
    head_count = step_size.shape[0]
    head_width = inputs.shape[1] // head_count
    nodes = lax.axis_size("node")
    heads = head_count // CHUNKS
    half = nodes // 2
    rate = decay_rate[None, :]
    groups = [list(range(half)), list(range(half, nodes))]
    across = [(n, (n + half) % nodes) for n in range(nodes)]

    def swap(v):
        return lax.all_to_all(
            v.reshape(half, state // half, v.shape[-1]),
            "node",
            split_axis=0,
            concat_axis=0,
            tiled=True,
            axis_index_groups=groups,
        )

    def cross(v):
        return lax.ppermute(v, "node", across)

    places = jnp.arange(nodes)
    child = jnp.logical_and(
        parents[:, None] == places[None, :],
        (places[:, None] < half) != (places[None, :] < half),
    )
    crossing = jnp.sum(jnp.any(child, axis=0).astype(jnp.int32))
    crowded = crossing > slot_counts(nodes)[0]

    shared = (inputs, cotangent, b_matrix, c_matrix)
    sizes = (heads, head_width)
    made = []
    for k in range(CHUNKS):
        made.append(node_states(*shared, step_size, rate, k, *sizes))
    received = [swap(made[k][0]) for k in range(CHUNKS)]
    found = []
    prior = None
    for k in range(CHUNKS):
        for part in range(PARTS):
            *prior, gc, gb = node_inner(
                *shared, made[0][5], made[k][1], made[k][2], prior, k, part, PARTS, *sizes
            )
            found.append((gb, gc))
    inner = prior
    packed = []
    for k in range(CHUNKS):
        main, more = pack_slots(parents, received[k], nodes, *sizes)
        packed.append((main, more, cross(main)))
    others = lax.cond(
        crowded,
        lambda vs: tuple(cross(v) for v in vs),
        lambda vs: vs,
        tuple(p[1] for p in packed),
    )
    states = []
    for k in range(CHUNKS):
        joined = join_slots(parents, received[k], packed[k][2], others[k], nodes, *sizes)
        states.append(swap(joined).reshape(state, -1))
    prior = None
    for k in range(CHUNKS):
        result = node_outer(
            *shared, *made[k][3:5], states[k], *made[k][6:8], *inner, found, prior, k, *sizes
        )
        prior = result[:2]
        if k == 0:
            found = [(result[3], result[2])]
    grads = scatter_sum(result[2:4], result[4:])
    return prior[0], prior[1], grads[0], grads[1]


def solution(mesh):
    return jax.shard_map(
        one_device,
        mesh=mesh,
        in_specs=(
            P("node", "head"),
            P("node", None),
            P("node", None),
            P("head", "node"),
            P("head"),
            P(),
            P("node", "head"),
        ),
        out_specs=(
            P("node", "head"),
            P("node", "head"),
            P(("node", "head"), None),
            P(("node", "head"), None),
        ),
        check_vma=False,
    )
```

```python
import functools
import math

import jax
import jax.numpy as jnp
from jax import lax
from jax.experimental import pallas as pl
from jax.experimental.pallas import tpu as pltpu
from jax.sharding import PartitionSpec as P


LEVELS = 3
VMEM_BYTES = 24 << 20
LANES = 128
SUBLANES = 8
CHUNKS = 2
PARTS = 2

LOG2E = 1.0 / math.log(2.0)

f32 = jnp.float32
bf16 = jnp.bfloat16
NN = (((1,), (0,)), ((), ()))
NT = (((1,), (1,)), ((), ()))


def mm(a, b, dims=NN):
    return lax.dot_general(a, b, dims, preferred_element_type=f32)


def split_two(v):
    high = v.astype(bf16)
    return high, (v - high.astype(f32)).astype(bf16)


def spread_matrix(rows, width, head_width, offset=0):
    row = lax.broadcasted_iota(jnp.int32, (rows, width), 0)
    lane = (lax.broadcasted_iota(jnp.int32, (rows, width), 1) + offset) // head_width
    return (row == lane).astype(bf16)


def head_lanes(columns, first, head_width):
    lane = lax.broadcasted_iota(jnp.int32, columns.shape, 1) // head_width + first
    return jnp.take_along_axis(columns, lane, axis=1)


def pad_lanes(v):
    gap = LANES - v.shape[0]
    if gap:
        v = jnp.concatenate([v, jnp.zeros((gap, v.shape[1]), v.dtype)], axis=0)
    return v.T


def half_steps(step_ref, spread):
    steps = mm(step_ref[...], spread)
    return steps[:1], steps[SUBLANES : SUBLANES + 1]


class Copies:
    def __init__(self, sems):
        self.sems = sems
        self.made = []

    def start(self, source, target):
        copy = pltpu.make_async_copy(source, target, self.sems.at[len(self.made)])
        copy.start()
        self.made.append(copy)
        return copy


def wait_all(copies):
    for copy in copies:
        copy.wait()


def states_kernel(heads, head_width, chunk, block, *refs):
    x_hbm, cot_hbm, b_hbm, c_hbm, step_hbm, rate_hbm = refs[:6]
    outs = refs[6:14]
    x_ref, cot_ref, b_ref, c_ref, step_ref, rate_ref = refs[14:20]
    send_ref, low_ref, src_ref, grow_ref, tail_ref, gram_ref, keep_ref, steps_ref = refs[20:28]
    sems = refs[28]
    length = step_ref.shape[1]
    middle = length // 2
    width = heads * head_width
    count = width // block
    copies = Copies(sems)
    first_in = [
        copies.start(step_hbm.at[pl.ds(chunk * heads, heads)], step_ref),
        copies.start(rate_hbm, rate_ref),
    ]
    later_in = [copies.start(b_hbm, b_ref), copies.start(c_hbm, c_ref)]
    loads = []
    for i in range(count):
        lanes = pl.ds(i * block, block)
        there = pl.ds(chunk * width + i * block, block)
        loads.append(
            [
                copies.start(x_hbm.at[:, there], x_ref.at[:, lanes]),
                copies.start(cot_hbm.at[:, there], cot_ref.at[:, lanes]),
            ]
        )
    wait_all(first_in)
    step = step_ref[...]
    rates = jnp.broadcast_to(rate_ref[...], (LANES, rate_ref.shape[1])).T
    terms = -step * rates[chunk * heads : (chunk + 1) * heads, :1]
    row = lax.broadcasted_iota(jnp.int32, (length, length), 0)
    col = lax.broadcasted_iota(jnp.int32, (length, length), 1)
    upper = (row <= col).astype(bf16)
    first = terms.astype(bf16)
    rest = terms - first.astype(f32)
    second, third = split_two(rest)
    cumulative = mm(third, upper) + mm(second, upper) + mm(first, upper)
    last = cumulative[:, length - 1 :]
    mid = cumulative[:, middle - 1 : middle]
    late = lax.broadcasted_iota(jnp.int32, cumulative.shape, 1) >= middle
    low_ref[...] = pad_lanes(cumulative * LOG2E)
    src_ref[...] = (cumulative - jnp.log(step)) * LOG2E
    grow_ref[...] = pad_lanes(jnp.exp(cumulative - jnp.where(late, mid, 0.0))).astype(bf16)
    tail = jnp.exp(jnp.where(late, last, mid) - cumulative) * step
    tail_ref[...] = pad_lanes(tail).astype(bf16)
    total = jnp.exp(jnp.broadcast_to(last, (heads, send_ref.shape[0])))
    send_ref[:, 2 * width :] = pad_lanes(total).astype(bf16)
    each = (heads, SUBLANES)
    steps = [jnp.broadcast_to(mid, each), jnp.broadcast_to(last - mid, each)]
    steps_ref[...] = pad_lanes(jnp.exp(jnp.concatenate(steps, axis=1))).astype(bf16)
    wait_all(later_in)
    b_turned = b_ref[...].T
    c_turned = c_ref[...].T
    small = (1, 2, 3, 4, 7)
    if chunk == CHUNKS - 1:
        small = (1, 2, 3, 4, 5, 7)
        for rows in (slice(0, middle), slice(middle, length)):
            gram_ref[rows] = mm(c_ref[rows], b_ref[rows], NT).astype(bf16)
    made = (send_ref, low_ref, src_ref, grow_ref, tail_ref, gram_ref, keep_ref, steps_ref)
    stores = []
    ready = [(made[n], outs[n]) for n in small]
    ready.append((send_ref.at[:, pl.ds(2 * width, LANES)], outs[0].at[:, pl.ds(2 * width, LANES)]))
    for i in range(count):
        here = pl.ds(i * block, block)
        there = pl.ds(i * block + width, block)
        wait_all(loads[i])
        spread = spread_matrix(LANES, block, head_width, i * block)
        tailed = mm(tail_ref[...], spread).astype(bf16) * x_ref[:, here]
        emitted = mm(grow_ref[...], spread).astype(bf16) * cot_ref[:, here]
        early_step, late_step = half_steps(steps_ref, spread)
        early_state = mm(b_turned[:, :middle], tailed[:middle])
        late_state = mm(b_turned[:, middle:], tailed[middle:])
        early_seed = mm(c_turned[:, :middle], emitted[:middle])
        late_seed = mm(c_turned[:, middle:], emitted[middle:])
        send_ref[:, here] = (late_step * early_state + late_state).astype(bf16)
        send_ref[:, there] = (early_seed + early_step * late_seed).astype(bf16)
        keep_ref[:, here] = early_state.astype(bf16)
        keep_ref[:, there] = late_seed.astype(bf16)
        stores += [copies.start(*pair) for pair in ready]
        ready = [
            (ref.at[:, lanes], out.at[:, lanes])
            for ref, out in ((send_ref, outs[0]), (keep_ref, outs[6]))
            for lanes in (here, there)
        ]
    stores += [copies.start(*pair) for pair in ready]
    wait_all(stores)


def node_states(x, cot, b, c, step, rate, chunk, heads, head_width):
    length, state = b.shape
    width = heads * head_width
    block = min(width, 4 * LANES)
    count = width // block
    out_shape = [
        jax.ShapeDtypeStruct((state, 2 * width + LANES), bf16),
        jax.ShapeDtypeStruct((length, LANES), f32),
        jax.ShapeDtypeStruct((heads, length), f32),
        jax.ShapeDtypeStruct((length, LANES), bf16),
        jax.ShapeDtypeStruct((length, LANES), bf16),
        jax.ShapeDtypeStruct((length, length // 2), bf16),
        jax.ShapeDtypeStruct((state, 2 * width), bf16),
        jax.ShapeDtypeStruct((2 * SUBLANES, LANES), bf16),
    ]
    held = [(length, width)] * 2 + [b.shape] * 2
    scratch = [pltpu.VMEM(shape, bf16) for shape in held]
    scratch += [pltpu.VMEM((heads, length), f32), pltpu.VMEM(rate.shape, f32)]
    scratch += [pltpu.VMEM(v.shape, v.dtype) for v in out_shape]
    scratch.append(pltpu.SemaphoreType.DMA((11 + 6 * count,)))
    anywhere = pl.BlockSpec(memory_space=pl.ANY)
    return pl.pallas_call(
        functools.partial(states_kernel, heads, head_width, chunk, block),
        in_specs=[anywhere] * 6,
        out_specs=[anywhere] * len(out_shape),
        out_shape=out_shape,
        scratch_shapes=scratch,
        name="node_states",
        cost_estimate=pl.CostEstimate(
            flops=4 * length * state * width,
            bytes_accessed=4 * length * width + 8 * state * width,
            transcendentals=0,
        ),
    )(x, cot, b, c, step, rate)


def inner_kernel(
    head_width,
    first,
    aliased,
    x_ref,
    cot_ref,
    b_ref,
    c_ref,
    given_ref,
    low_ref,
    src_ref,
    *refs,
):
    if aliased:
        refs = refs[2:]
    out_ref, grad_ref, gc_ref, gb_ref, mixed_ref, turned_ref, wa_ref, wb_ref, gram_ref = refs
    length = x_ref.shape[0]
    index = pl.program_id(0)
    pack = LANES // head_width
    pairs = x_ref.shape[1] // LANES
    wide = length // 2
    blocks = wide // LANES
    weights = (wa_ref, wb_ref)

    @pl.when(index == 0)
    def _():
        gram_ref[...] = given_ref[...]
        mixed_ref[...] = jnp.zeros_like(mixed_ref)
        for ref in weights:
            ref[...] = jnp.zeros_like(ref)

    lane = lax.broadcasted_iota(jnp.int32, (1, LANES), 1) // head_width
    causal = lax.broadcasted_iota(jnp.int32, (LANES, LANES), 0) >= lax.broadcasted_iota(
        jnp.int32, (LANES, LANES), 1
    )
    halves = (slice(0, wide), slice(wide, length))
    xs = [x_ref[:, q * LANES : (q + 1) * LANES] for q in range(pairs)]
    turned_cots = [cot_ref[:, q * LANES : (q + 1) * LANES].T for q in range(pairs)]
    low = low_ref[...]

    def decays(h):
        q, a = h // pack, h % pack
        w = weights[h % 2]
        cot = cot_ref[:, q * LANES : (q + 1) * LANES]
        cot = jnp.where(lane == a, cot, jnp.zeros_like(cot))
        place = (first + index * pairs + q) * pack + a
        column = head_lanes(low, place, LANES)
        source = src_ref[pl.ds(place, 1), :]
        for part in halves:
            scores = mm(cot[part], xs[q][part], NT)
            for i in range(blocks):
                here = slice(i * LANES, (i + 1) * LANES)
                rows = slice(part.start + here.start, part.start + here.stop)
                for j in range(i + 1):
                    cols = slice(j * LANES, (j + 1) * LANES)
                    differ = column[rows] - source[:, part.start + cols.start : part.start + cols.stop]
                    if i == j:
                        differ = jnp.where(causal, differ, -jnp.inf)
                    decay = jnp.exp2(differ)
                    w[rows, cols] = decay.astype(bf16) * gram_ref[rows, cols]
                    mixed_ref[rows, cols] += decay * scores[here, cols]
                yield

    def products(h):
        q, a = h // pack, h % pack
        w = weights[h % 2]
        turned = turned_cots[q][a * head_width : (a + 1) * head_width]
        mine = slice(q * LANES + a * head_width, q * LANES + (a + 1) * head_width)
        own = slice(a * head_width, (a + 1) * head_width)
        for part in halves:
            out_ref[part, mine] = mm(w[part], xs[q][part])[:, own].astype(bf16)
            yield
            turned_ref[mine, part] = mm(turned[:, part], w[part]).astype(bf16)
            yield

    def finish(q):
        lanes = slice(q * LANES, (q + 1) * LANES)
        grad_ref[:, lanes] = turned_ref[lanes, :].T

    before = None
    for h in range(pairs * pack):
        for _ in decays(h):
            if before is not None:
                next(before, None)
        if before is not None:
            for _ in before:
                pass
            if h % pack == 0:
                finish(h // pack - 1)
        before = products(h)
    for _ in before:
        pass
    finish(pairs - 1)

    @pl.when(index == pl.num_programs(0) - 1)
    def _():
        for part in halves:
            mixed = mixed_ref[part].astype(bf16)
            gc_ref[part] = mm(mixed, b_ref[part])
            gb_ref[part] = mm(mixed.T, c_ref[part])


def node_inner(x, cot, b, c, gram, low, src, prior, chunk, part, parts, heads, head_width):
    length, state = b.shape
    width = heads * head_width
    block = min(width // parts, 2 * LANES)
    count = width // block // parts
    offset = (chunk * parts + part) * count
    whole = lambda i: (0, 0)
    place = lambda i: (0, offset + i)
    aliased = prior is not None
    operands = [x, cot, b, c, gram, low, src]
    in_specs = [
        pl.BlockSpec((length, block), place),
        pl.BlockSpec((length, block), place),
        pl.BlockSpec((length, state), whole),
        pl.BlockSpec((length, state), whole),
        pl.BlockSpec((length, length // 2), whole),
        pl.BlockSpec((length, LANES), whole),
        pl.BlockSpec((heads, length), whole),
    ]
    aliases = {}
    if aliased:
        aliases = {len(operands): 0, len(operands) + 1: 1}
        operands += list(prior)
        in_specs += [pl.BlockSpec(memory_space=pl.ANY)] * 2
    kernel = functools.partial(inner_kernel, head_width, part * count * block // LANES, aliased)
    return pl.pallas_call(
        kernel,
        grid=(count,),
        in_specs=in_specs,
        out_specs=[
            pl.BlockSpec((length, block), place),
            pl.BlockSpec((length, block), place),
            pl.BlockSpec((length, state), whole),
            pl.BlockSpec((length, state), whole),
        ],
        out_shape=[
            jax.ShapeDtypeStruct(x.shape, bf16),
            jax.ShapeDtypeStruct(x.shape, bf16),
            jax.ShapeDtypeStruct((length, state), f32),
            jax.ShapeDtypeStruct((length, state), f32),
        ],
        scratch_shapes=[
            pltpu.VMEM((length, length // 2), f32),
            pltpu.VMEM((block, length), bf16),
            pltpu.VMEM((length, length // 2), bf16),
            pltpu.VMEM((length, length // 2), bf16),
            pltpu.VMEM((length, length // 2), bf16),
        ],
        input_output_aliases=aliases,
        name="node_inner",
        cost_estimate=pl.CostEstimate(
            flops=24 * length * length * count * block,
            bytes_accessed=12 * length * count * block,
            transcendentals=length * length * heads // parts,
        ),
    )(*operands)


def rank_nodes(parents_ref, rank_ref, half):
    nodes = rank_ref.shape[0]

    def clear(n, carry):
        rank_ref[n] = 0
        return carry

    def mark(n, carry):
        up = parents_ref[n]

        @pl.when(jnp.logical_and(up >= 0, (up >= half) != (n >= half)))
        def _():
            rank_ref[up] = 1

        return carry

    def place(n, count):
        crosses = rank_ref[n]
        rank_ref[n] = jnp.where(crosses > 0, count, -1)
        return count + crosses

    lax.fori_loop(0, nodes, clear, 0)
    lax.fori_loop(0, nodes, mark, 0)
    lax.fori_loop(0, nodes, place, 0)


def widen(narrow, heads, head_width):
    count = narrow.shape[0]
    flat = jnp.concatenate([narrow[n, :1].astype(f32) for n in range(count)], axis=0)
    return mm(flat.astype(bf16), spread_matrix(LANES, heads * head_width, head_width))


def pack_kernel(
    heads, head_width, parents_ref, recv_ref, main_ref, more_ref, decay_ref, slot_ref, chain_ref, rank_ref
):
    half = recv_ref.shape[0]
    width = heads * head_width
    base = lax.axis_index("node") // half * half
    rank_nodes(parents_ref, rank_ref, half)
    decay_ref[...] = widen(recv_ref[:, :, 2 * width :], heads, head_width)
    slot_ref[...] = jnp.zeros_like(slot_ref)
    chain_ref[...] = jnp.zeros_like(chain_ref)

    def inside(n):
        return jnp.logical_and(n >= base, n < base + half)

    def spot(n):
        return jnp.clip(n - base, 0, half - 1)

    def visit(m, carry):
        node = base + m
        flow = recv_ref[m, :, width : 2 * width].astype(f32)
        at = node
        live = jnp.bool_(True)
        for level in range(LEVELS):
            up = parents_ref[at]
            exists = jnp.logical_and(live, up >= 0)
            live = jnp.logical_and(exists, inside(up))
            away = jnp.logical_and(exists, jnp.logical_not(live))

            @pl.when(away)
            def _(flow=flow, up=up):
                slot = rank_ref[up]
                slot_ref[slot] = slot_ref[slot] + flow

            if level < LEVELS - 1:
                flow = flow * jnp.where(live, decay_ref[pl.ds(spot(up), 1)], 1.0)
            at = jnp.where(live, up, at)

        @pl.when(rank_ref[node] >= 0)
        def _():
            total = recv_ref[m, :, :width].astype(f32)
            factor = decay_ref[pl.ds(m, 1)]
            chain = recv_ref[m, :, 2 * width :].astype(f32)
            at = node
            live = jnp.bool_(True)
            for _ in range(LEVELS - 1):
                up = parents_ref[at]
                live = jnp.logical_and(jnp.logical_and(live, up >= 0), inside(up))
                where = spot(up)
                total = total + jnp.where(live, factor * recv_ref[where, :, :width].astype(f32), 0.0)
                factor = factor * jnp.where(live, decay_ref[pl.ds(where, 1)], 1.0)
                chain = chain * jnp.where(live, recv_ref[where, :, 2 * width :].astype(f32), 1.0)
                at = jnp.where(live, up, at)
            slot_ref[rank_ref[node]] = total
            chain_ref[rank_ref[node]] = chain

        return carry

    lax.fori_loop(0, half, visit, 0)
    main = main_ref.shape[0]
    main_ref[:, :, :width] = slot_ref[:main].astype(bf16)
    main_ref[:, :, width:] = chain_ref[:main].astype(bf16)
    more_ref[:, :, :width] = slot_ref[main:].astype(bf16)
    more_ref[:, :, width:] = chain_ref[main:].astype(bf16)


def slot_counts(nodes):
    most = nodes * LEVELS // (LEVELS + 1)
    main = nodes // 2 - nodes // 16
    return main, most - main


def pack_slots(parents, recv, nodes, heads, head_width):
    half, rows, _ = recv.shape
    width = heads * head_width
    main, more = slot_counts(nodes)
    in_specs = [pl.BlockSpec(memory_space=pltpu.SMEM), pl.BlockSpec(memory_space=pltpu.VMEM)]
    kernel = functools.partial(pack_kernel, heads, head_width)
    operands = [parents, recv]
    return pl.pallas_call(
        kernel,
        in_specs=in_specs,
        out_specs=[pl.BlockSpec(memory_space=pltpu.VMEM)] * 2,
        out_shape=[
            jax.ShapeDtypeStruct((main, rows, width + LANES), bf16),
            jax.ShapeDtypeStruct((more, rows, width + LANES), bf16),
        ],
        scratch_shapes=[
            pltpu.VMEM((half, width), f32),
            pltpu.VMEM((main + more, rows, width), f32),
            pltpu.VMEM((main + more, rows, LANES), f32),
            pltpu.SMEM((nodes,), jnp.int32),
        ],
        compiler_params=pltpu.CompilerParams(vmem_limit_bytes=VMEM_BYTES),
        name="pack_slots",
        cost_estimate=pl.CostEstimate(
            flops=20 * half * rows * width,
            bytes_accessed=8 * half * rows * width,
            transcendentals=0,
        ),
    )(*operands)


def join_kernel(
    heads,
    head_width,
    parents_ref,
    recv_ref,
    main_ref,
    more_ref,
    out_ref,
    decay_ref,
    slot_ref,
    chain_ref,
    back_ref,
    rank_ref,
):
    half = recv_ref.shape[0]
    width = heads * head_width
    main = main_ref.shape[0]
    base = lax.axis_index("node") // half * half
    rank_nodes(parents_ref, rank_ref, half)
    decay_ref[...] = widen(recv_ref[:, :, 2 * width :], heads, head_width)
    slot_ref[:main] = main_ref[:, :, :width]
    slot_ref[main:] = more_ref[:, :, :width]
    chain_ref[:main] = widen(main_ref[:, :, width:], heads, head_width)
    chain_ref[main:] = widen(more_ref[:, :, width:], heads, head_width)
    back_ref[...] = jnp.zeros_like(back_ref)

    def inside(n):
        return jnp.logical_and(n >= base, n < base + half)

    def climb(at, flow, start):
        factor = None
        live = jnp.bool_(True)
        for level in range(LEVELS):
            up = parents_ref[at]
            live = jnp.logical_and(live, up >= 0)
            near = jnp.logical_and(live, inside(up))
            far = jnp.logical_and(live, jnp.logical_not(near))
            where = jnp.clip(up - base, 0, half - 1)
            slot = jnp.where(far, rank_ref[jnp.maximum(up, 0)], 0)

            @pl.when(near)
            def _(flow=flow, where=where):
                back_ref[where] = back_ref[where] + flow

            if start is not None:
                value = jnp.where(near, recv_ref[where, :, :width], slot_ref[slot])
                value = jnp.where(live, value.astype(f32), 0.0)
                start = start + (value if factor is None else factor * value)
            if level < LEVELS - 1:
                step = jnp.where(near, decay_ref[pl.ds(where, 1)], chain_ref[pl.ds(slot, 1)])
                flow = flow * step
                factor = step if factor is None else factor * step
                top = jnp.maximum(up, 0)
                for _ in range(LEVELS - 1):
                    above = parents_ref[top]
                    more = jnp.logical_and(far, above >= 0)
                    more = jnp.logical_and(more, jnp.logical_not(inside(above)))
                    top = jnp.where(more, above, top)
                at = top
        return start

    def visit(m, carry):
        node = base + m
        seed = recv_ref[m, :, width : 2 * width].astype(f32)
        start = climb(node, seed, jnp.zeros(seed.shape, f32))
        out_ref[m, :, :width] = start.astype(bf16)

        @pl.when(rank_ref[node] >= 0)
        def _():
            extra = slot_ref[rank_ref[node]].astype(f32)
            back_ref[m] = back_ref[m] + extra
            climb(node, extra * decay_ref[pl.ds(m, 1)], None)

        return carry

    lax.fori_loop(0, half, visit, 0)
    out_ref[:, :, width:] = back_ref[...].astype(bf16)


def join_slots(parents, recv, main, more, nodes, heads, head_width):
    half, rows, _ = recv.shape
    width = heads * head_width
    in_specs = [pl.BlockSpec(memory_space=pltpu.SMEM)] + [pl.BlockSpec(memory_space=pltpu.VMEM)] * 3
    kernel = functools.partial(join_kernel, heads, head_width)
    operands = [parents, recv, main, more]
    slots = main.shape[0] + more.shape[0]
    return pl.pallas_call(
        kernel,
        in_specs=in_specs,
        out_specs=pl.BlockSpec(memory_space=pltpu.VMEM),
        out_shape=jax.ShapeDtypeStruct((half, rows, 2 * width), bf16),
        scratch_shapes=[
            pltpu.VMEM((half, width), f32),
            pltpu.VMEM((slots, rows, width), bf16),
            pltpu.VMEM((slots, width), f32),
            pltpu.VMEM((half, rows, width), f32),
            pltpu.SMEM((nodes,), jnp.int32),
        ],
        compiler_params=pltpu.CompilerParams(vmem_limit_bytes=VMEM_BYTES),
        name="join_slots",
        cost_estimate=pl.CostEstimate(
            flops=20 * half * rows * width,
            bytes_accessed=8 * half * rows * width,
            transcendentals=0,
        ),
    )(*operands)


def outer_kernel(heads, head_width, chunk, block, extras, final, *refs):
    given = 13 + 2 * extras
    sources = refs[:given]
    refs = refs[given:]
    if final:
        outs, owns, pieces = refs[2:4], refs[4:6], refs[6 : -(given + 5)]
        gc_ref, gb_ref = refs[-2:]
        refs = refs[-(given + 5) : -2]
    else:
        outs, (gc_ref, gb_ref) = refs[:2], refs[2:4]
        refs = refs[4:]
    held, results, sems = refs[:given], refs[given : given + 2], refs[-1]
    b_ref, c_ref, grow_ref, tail_ref, step_ref = held[:5]
    added = held[5 : 5 + 2 * extras]
    x_ref, cot_ref, inner_ref, grad_ref, start_ref, back_ref, early_ref, late_ref = held[-8:]
    width = heads * head_width
    count = width // block
    middle = x_ref.shape[0] // 2
    copies = Copies(sems)
    small = [copies.start(sources[n], held[n]) for n in range(5)]
    loads = []
    for i in range(count):
        lanes = pl.ds(i * block, block)
        over = pl.ds(width + i * block, block)
        column = pl.ds(chunk * width + i * block, block)
        spots = (column,) * 4 + (lanes, over) * 2
        loads.append(
            [
                copies.start(source.at[:, spot], ref.at[:, lanes])
                for source, spot, ref in zip(sources[-8:], spots, held[-8:])
            ]
        )
    sums = [copies.start(sources[5 + n], ref) for n, ref in enumerate(added)]
    wait_all(small)
    stores = []
    ready = []
    for i in range(count):
        here = pl.ds(i * block, block)
        column = pl.ds(chunk * width + i * block, block)
        wait_all(loads[i])
        spread = spread_matrix(LANES, block, head_width, i * block)
        grow_wide = mm(grow_ref[...], spread)
        tail_wide = mm(tail_ref[...], spread)
        early_step, late_step = half_steps(step_ref, spread)
        start = start_ref[:, here]
        back = back_ref[:, here]
        after = (early_step * start.astype(f32) + early_ref[:, here].astype(f32)).astype(bf16)
        before = (late_step * back.astype(f32) + late_ref[:, here].astype(f32)).astype(bf16)
        for n, part in enumerate((slice(0, middle), slice(middle, 2 * middle))):
            grow = grow_wide[part]
            tail = tail_wide[part]
            begin = (start, after)[n]
            end = (before, back)[n]
            carried = grow * mm(c_ref[part], begin)
            results[0][part, here] = (inner_ref[part, here].astype(f32) + carried).astype(bf16)
            carried = tail * mm(b_ref[part], end)
            results[1][part, here] = (grad_ref[part, here].astype(f32) + carried).astype(bf16)
            gc = mm(grow.astype(bf16) * cot_ref[part, here], begin, NT)
            gb = mm(tail.astype(bf16) * x_ref[part, here], end, NT)
            if i == 0:
                gc_ref[part] = gc
                gb_ref[part] = gb
            else:
                gc_ref[part] += gc
                gb_ref[part] += gb
        stores += [copies.start(*pair) for pair in ready]
        ready = [
            (result.at[:, here], out.at[:, column]) for result, out in zip(results, outs)
        ]
    wait_all(sums)
    gc_ref[...] += sum(ref[...] for ref in added[:extras])
    gb_ref[...] += sum(ref[...] for ref in added[extras:])
    stores += [copies.start(*pair) for pair in ready]
    if final:
        size = len(pieces) + 1
        me = lax.axis_index("head")
        rows = owns[0].shape[0]
        for shift in range(size):
            at = pl.multiple_of(lax.rem(me + shift, size) * rows, rows)
            for n, ref in enumerate((gb_ref, gc_ref)):
                if shift == 0:
                    owns[n][...] = ref[pl.ds(at, rows)]
                else:
                    pieces[shift - 1][n] = ref[pl.ds(at, rows)].astype(bf16)
    wait_all(stores)


def node_outer(
    x, cot, b, c, grow, tail, states, keep, steps, inner, grad, found, prior, chunk, heads, head_width
):
    length, state = b.shape
    width = heads * head_width
    block = min(width, 4 * LANES)
    count = width // block
    final = prior is not None
    small = [b, c, grow, tail, steps] + [v[1] for v in found] + [v[0] for v in found]
    operands = small + [x, cot, inner, grad, states, states, keep, keep]
    given = len(operands)
    anywhere = pl.BlockSpec(memory_space=pl.ANY)
    local = pl.BlockSpec(memory_space=pltpu.VMEM)
    out_specs = [anywhere] * 2
    out_shape = [jax.ShapeDtypeStruct(x.shape, bf16)] * 2
    scratch = [pltpu.VMEM(v.shape, v.dtype) for v in small]
    scratch += [pltpu.VMEM((length, width), bf16)] * 4 + [pltpu.VMEM((state, width), bf16)] * 4
    scratch += [pltpu.VMEM((length, width), bf16)] * 2
    scratch.append(pltpu.SemaphoreType.DMA((len(small) + 10 * count,)))
    aliases = {}
    if final:
        aliases = {given: 0, given + 1: 1}
        operands += list(prior)
        size = lax.axis_size("head")
        kept = (2, length // size, state)
        out_specs += [local] * (size + 1)
        out_shape += [jax.ShapeDtypeStruct(kept[1:], f32)] * 2
        out_shape += [jax.ShapeDtypeStruct(kept, bf16)] * (size - 1)
        scratch += [pltpu.VMEM((length, state), f32)] * 2
    else:
        out_specs += [local] * 2
        out_shape += [jax.ShapeDtypeStruct((length, state), f32)] * 2
    return pl.pallas_call(
        functools.partial(outer_kernel, heads, head_width, chunk, block, len(found), final),
        in_specs=[anywhere] * len(operands),
        out_specs=out_specs,
        out_shape=out_shape,
        scratch_shapes=scratch,
        input_output_aliases=aliases,
        name="node_outer",
        cost_estimate=pl.CostEstimate(
            flops=8 * length * state * width,
            bytes_accessed=14 * length * width,
            transcendentals=0,
        ),
    )(*operands)


def scatter_sum(owns, pieces):
    size = lax.axis_size("head")
    for shift, piece in enumerate(pieces, 1):
        pairs = [(i, (i + shift) % size) for i in range(size)]
        moved = lax.ppermute(piece, "head", pairs).astype(f32)
        owns = [own + moved[n] for n, own in enumerate(owns)]
    return owns


def one_device(inputs, b_matrix, c_matrix, step_size, decay_rate, parents, cotangent):
    state = b_matrix.shape[1]
    head_count = step_size.shape[0]
    head_width = inputs.shape[1] // head_count
    nodes = lax.axis_size("node")
    heads = head_count // CHUNKS
    half = nodes // 2
    rate = decay_rate[None, :]
    groups = [list(range(half)), list(range(half, nodes))]
    across = [(n, (n + half) % nodes) for n in range(nodes)]

    def swap(v):
        return lax.all_to_all(
            v.reshape(half, state // half, v.shape[-1]),
            "node",
            split_axis=0,
            concat_axis=0,
            tiled=True,
            axis_index_groups=groups,
        )

    def cross(v):
        return lax.ppermute(v, "node", across)

    places = jnp.arange(nodes)
    child = jnp.logical_and(
        parents[:, None] == places[None, :],
        (places[:, None] < half) != (places[None, :] < half),
    )
    crossing = jnp.sum(jnp.any(child, axis=0).astype(jnp.int32))
    crowded = crossing > slot_counts(nodes)[0]

    shared = (inputs, cotangent, b_matrix, c_matrix)
    sizes = (heads, head_width)
    made = []
    for k in range(CHUNKS):
        made.append(node_states(*shared, step_size, rate, k, *sizes))
    received = [swap(made[k][0]) for k in range(CHUNKS)]
    found = []
    prior = None
    for k in range(CHUNKS):
        for part in range(PARTS):
            *prior, gc, gb = node_inner(
                *shared, made[-1][5], made[k][1], made[k][2], prior, k, part, PARTS, *sizes
            )
            found.append((gb, gc))
    inner = prior
    packed = []
    for k in range(CHUNKS):
        main, more = pack_slots(parents, received[k], nodes, *sizes)
        held = pltpu.with_memory_space_constraint(main, pltpu.HBM)
        packed.append((main, more, cross(held)))
    others = lax.cond(
        crowded,
        lambda vs: tuple(cross(v) for v in vs),
        lambda vs: vs,
        tuple(p[1] for p in packed),
    )
    states = []
    for k in range(CHUNKS):
        joined = join_slots(parents, received[k], packed[k][2], others[k], nodes, *sizes)
        states.append(swap(joined).reshape(state, -1))
    prior = None
    for k in range(CHUNKS):
        result = node_outer(
            *shared, *made[k][3:5], states[k], *made[k][6:8], *inner, found, prior, k, *sizes
        )
        prior = result[:2]
        if k == 0:
            found = [(result[3], result[2])]
    grads = scatter_sum(result[2:4], result[4:])
    return prior[0], prior[1], grads[0], grads[1]


def solution(mesh):
    return jax.shard_map(
        one_device,
        mesh=mesh,
        in_specs=(
            P("node", "head"),
            P("node", None),
            P("node", None),
            P("head", "node"),
            P("head"),
            P(),
            P("node", "head"),
        ),
        out_specs=(
            P("node", "head"),
            P("node", "head"),
            P(("node", "head"), None),
            P(("node", "head"), None),
        ),
        check_vma=False,
    )
```

```python
import functools
import math

import jax
import jax.numpy as jnp
from jax import lax
from jax.experimental import pallas as pl
from jax.experimental.pallas import tpu as pltpu
from jax.sharding import PartitionSpec as P


LEVELS = 3
VMEM_BYTES = 24 << 20
LANES = 128
SUBLANES = 8
CHUNKS = 2
PARTS = 2

LOG2E = 1.0 / math.log(2.0)

f32 = jnp.float32
bf16 = jnp.bfloat16
NN = (((1,), (0,)), ((), ()))
NT = (((1,), (1,)), ((), ()))


def mm(a, b, dims=NN):
    return lax.dot_general(a, b, dims, preferred_element_type=f32)


def split_two(v):
    high = v.astype(bf16)
    return high, (v - high.astype(f32)).astype(bf16)


def spread_matrix(rows, width, head_width, offset=0):
    row = lax.broadcasted_iota(jnp.int32, (rows, width), 0)
    lane = (lax.broadcasted_iota(jnp.int32, (rows, width), 1) + offset) // head_width
    return (row == lane).astype(bf16)


def head_lanes(columns, first, head_width):
    lane = lax.broadcasted_iota(jnp.int32, columns.shape, 1) // head_width + first
    return jnp.take_along_axis(columns, lane, axis=1)


def pad_lanes(v):
    gap = LANES - v.shape[0]
    if gap:
        v = jnp.concatenate([v, jnp.zeros((gap, v.shape[1]), v.dtype)], axis=0)
    return v.T


def half_steps(step_ref, spread):
    steps = mm(step_ref[...], spread)
    return steps[:1], steps[SUBLANES : SUBLANES + 1]


class Copies:
    def __init__(self, sems):
        self.sems = sems
        self.made = []

    def start(self, source, target):
        copy = pltpu.make_async_copy(source, target, self.sems.at[len(self.made)])
        copy.start()
        self.made.append(copy)
        return copy


def wait_all(copies):
    for copy in copies:
        copy.wait()


def states_kernel(heads, head_width, chunk, block, *refs):
    x_hbm, cot_hbm, b_hbm, c_hbm, step_hbm, rate_hbm = refs[:6]
    outs = refs[6:14]
    x_ref, cot_ref, b_ref, c_ref, step_ref, rate_ref = refs[14:20]
    send_ref, low_ref, src_ref, grow_ref, tail_ref, gram_ref, keep_ref, steps_ref = refs[20:28]
    sems = refs[28]
    length = step_ref.shape[1]
    middle = length // 2
    width = heads * head_width
    count = width // block
    copies = Copies(sems)
    first_in = [
        copies.start(step_hbm.at[pl.ds(chunk * heads, heads)], step_ref),
        copies.start(rate_hbm, rate_ref),
    ]
    later_in = [copies.start(b_hbm, b_ref), copies.start(c_hbm, c_ref)]
    loads = []
    for i in range(count):
        lanes = pl.ds(i * block, block)
        there = pl.ds(chunk * width + i * block, block)
        loads.append(
            [
                copies.start(x_hbm.at[:, there], x_ref.at[:, lanes]),
                copies.start(cot_hbm.at[:, there], cot_ref.at[:, lanes]),
            ]
        )
    wait_all(first_in)
    step = step_ref[...]
    rates = jnp.broadcast_to(rate_ref[...], (LANES, rate_ref.shape[1])).T
    terms = -step * rates[chunk * heads : (chunk + 1) * heads, :1]
    row = lax.broadcasted_iota(jnp.int32, (length, length), 0)
    col = lax.broadcasted_iota(jnp.int32, (length, length), 1)
    upper = (row <= col).astype(bf16)
    first = terms.astype(bf16)
    rest = terms - first.astype(f32)
    second, third = split_two(rest)
    cumulative = mm(third, upper) + mm(second, upper) + mm(first, upper)
    last = cumulative[:, length - 1 :]
    mid = cumulative[:, middle - 1 : middle]
    late = lax.broadcasted_iota(jnp.int32, cumulative.shape, 1) >= middle
    low_ref[...] = pad_lanes(cumulative * LOG2E)
    src_ref[...] = (cumulative - jnp.log(step)) * LOG2E
    grow_ref[...] = pad_lanes(jnp.exp(cumulative - jnp.where(late, mid, 0.0))).astype(bf16)
    tail = jnp.exp(jnp.where(late, last, mid) - cumulative) * step
    tail_ref[...] = pad_lanes(tail).astype(bf16)
    total = jnp.exp(jnp.broadcast_to(last, (heads, send_ref.shape[0])))
    send_ref[:, 2 * width :] = pad_lanes(total).astype(bf16)
    each = (heads, SUBLANES)
    steps = [jnp.broadcast_to(mid, each), jnp.broadcast_to(last - mid, each)]
    steps_ref[...] = pad_lanes(jnp.exp(jnp.concatenate(steps, axis=1))).astype(bf16)
    wait_all(later_in)
    b_turned = b_ref[...].T
    c_turned = c_ref[...].T
    small = (1, 2, 3, 4, 7)
    if chunk == CHUNKS - 1:
        small = (1, 2, 3, 4, 5, 7)
        for rows in (slice(0, middle), slice(middle, length)):
            gram_ref[rows] = mm(c_ref[rows], b_ref[rows], NT).astype(bf16)
    made = (send_ref, low_ref, src_ref, grow_ref, tail_ref, gram_ref, keep_ref, steps_ref)
    stores = []
    ready = [(made[n], outs[n]) for n in small]
    ready.append((send_ref.at[:, pl.ds(2 * width, LANES)], outs[0].at[:, pl.ds(2 * width, LANES)]))
    for i in range(count):
        here = pl.ds(i * block, block)
        there = pl.ds(i * block + width, block)
        wait_all(loads[i])
        spread = spread_matrix(LANES, block, head_width, i * block)
        tailed = mm(tail_ref[...], spread).astype(bf16) * x_ref[:, here]
        emitted = mm(grow_ref[...], spread).astype(bf16) * cot_ref[:, here]
        early_step, late_step = half_steps(steps_ref, spread)
        early_state = mm(b_turned[:, :middle], tailed[:middle])
        late_state = mm(b_turned[:, middle:], tailed[middle:])
        early_seed = mm(c_turned[:, :middle], emitted[:middle])
        late_seed = mm(c_turned[:, middle:], emitted[middle:])
        send_ref[:, here] = (late_step * early_state + late_state).astype(bf16)
        send_ref[:, there] = (early_seed + early_step * late_seed).astype(bf16)
        keep_ref[:, here] = early_state.astype(bf16)
        keep_ref[:, there] = late_seed.astype(bf16)
        stores += [copies.start(*pair) for pair in ready]
        ready = [
            (ref.at[:, lanes], out.at[:, lanes])
            for ref, out in ((send_ref, outs[0]), (keep_ref, outs[6]))
            for lanes in (here, there)
        ]
    stores += [copies.start(*pair) for pair in ready]
    wait_all(stores)


def node_states(x, cot, b, c, step, rate, chunk, heads, head_width):
    length, state = b.shape
    width = heads * head_width
    block = min(width, 4 * LANES)
    count = width // block
    out_shape = [
        jax.ShapeDtypeStruct((state, 2 * width + LANES), bf16),
        jax.ShapeDtypeStruct((length, LANES), f32),
        jax.ShapeDtypeStruct((heads, length), f32),
        jax.ShapeDtypeStruct((length, LANES), bf16),
        jax.ShapeDtypeStruct((length, LANES), bf16),
        jax.ShapeDtypeStruct((length, length // 2), bf16),
        jax.ShapeDtypeStruct((state, 2 * width), bf16),
        jax.ShapeDtypeStruct((2 * SUBLANES, LANES), bf16),
    ]
    held = [(length, width)] * 2 + [b.shape] * 2
    scratch = [pltpu.VMEM(shape, bf16) for shape in held]
    scratch += [pltpu.VMEM((heads, length), f32), pltpu.VMEM(rate.shape, f32)]
    scratch += [pltpu.VMEM(v.shape, v.dtype) for v in out_shape]
    scratch.append(pltpu.SemaphoreType.DMA((11 + 6 * count,)))
    anywhere = pl.BlockSpec(memory_space=pl.ANY)
    return pl.pallas_call(
        functools.partial(states_kernel, heads, head_width, chunk, block),
        in_specs=[anywhere] * 6,
        out_specs=[anywhere] * len(out_shape),
        out_shape=out_shape,
        scratch_shapes=scratch,
        name="node_states",
        cost_estimate=pl.CostEstimate(
            flops=4 * length * state * width,
            bytes_accessed=4 * length * width + 8 * state * width,
            transcendentals=0,
        ),
    )(x, cot, b, c, step, rate)


def inner_kernel(
    head_width,
    first,
    aliased,
    x_ref,
    cot_ref,
    b_ref,
    c_ref,
    given_ref,
    low_ref,
    src_ref,
    *refs,
):
    if aliased:
        refs = refs[2:]
    out_ref, grad_ref, gc_ref, gb_ref, mixed_ref, turned_ref, wa_ref, wb_ref, gram_ref = refs
    length = x_ref.shape[0]
    index = pl.program_id(0)
    pack = LANES // head_width
    pairs = x_ref.shape[1] // LANES
    wide = length // 2
    blocks = wide // LANES
    weights = (wa_ref, wb_ref)

    @pl.when(index == 0)
    def _():
        gram_ref[...] = given_ref[...]
        mixed_ref[...] = jnp.zeros_like(mixed_ref)
        for ref in weights:
            ref[...] = jnp.zeros_like(ref)

    lane = lax.broadcasted_iota(jnp.int32, (1, LANES), 1) // head_width
    causal = lax.broadcasted_iota(jnp.int32, (LANES, LANES), 0) >= lax.broadcasted_iota(
        jnp.int32, (LANES, LANES), 1
    )
    halves = (slice(0, wide), slice(wide, length))
    xs = [x_ref[:, q * LANES : (q + 1) * LANES] for q in range(pairs)]
    turned_cots = [cot_ref[:, q * LANES : (q + 1) * LANES].T for q in range(pairs)]
    low = low_ref[...]

    def decays(h):
        q, a = h // pack, h % pack
        w = weights[h % 2]
        cot = cot_ref[:, q * LANES : (q + 1) * LANES]
        cot = jnp.where(lane == a, cot, jnp.zeros_like(cot))
        place = (first + index * pairs + q) * pack + a
        column = head_lanes(low, place, LANES)
        source = src_ref[pl.ds(place, 1), :]
        for part in halves:
            scores = mm(cot[part], xs[q][part], NT)
            for i in range(blocks):
                here = slice(i * LANES, (i + 1) * LANES)
                rows = slice(part.start + here.start, part.start + here.stop)
                for j in range(i + 1):
                    cols = slice(j * LANES, (j + 1) * LANES)
                    differ = column[rows] - source[:, part.start + cols.start : part.start + cols.stop]
                    if i == j:
                        differ = jnp.where(causal, differ, -jnp.inf)
                    decay = jnp.exp2(differ)
                    w[rows, cols] = decay.astype(bf16) * gram_ref[rows, cols]
                    mixed_ref[rows, cols] += decay * scores[here, cols]
                yield

    def products(h):
        q, a = h // pack, h % pack
        w = weights[h % 2]
        turned = turned_cots[q][a * head_width : (a + 1) * head_width]
        mine = slice(q * LANES + a * head_width, q * LANES + (a + 1) * head_width)
        own = slice(a * head_width, (a + 1) * head_width)
        for part in halves:
            out_ref[part, mine] = mm(w[part], xs[q][part])[:, own].astype(bf16)
            yield
            turned_ref[mine, part] = mm(turned[:, part], w[part]).astype(bf16)
            yield

    def finish(q):
        lanes = slice(q * LANES, (q + 1) * LANES)
        grad_ref[:, lanes] = turned_ref[lanes, :].T

    before = None
    for h in range(pairs * pack):
        for _ in decays(h):
            if before is not None:
                next(before, None)
        if before is not None:
            for _ in before:
                pass
            if h % pack == 0:
                finish(h // pack - 1)
        before = products(h)
    for _ in before:
        pass
    finish(pairs - 1)

    @pl.when(index == pl.num_programs(0) - 1)
    def _():
        for part in halves:
            mixed = mixed_ref[part].astype(bf16)
            gc_ref[part] = mm(mixed, b_ref[part])
            gb_ref[part] = mm(mixed.T, c_ref[part])


def node_inner(x, cot, b, c, gram, low, src, prior, chunk, part, parts, heads, head_width):
    length, state = b.shape
    width = heads * head_width
    block = min(width // parts, 2 * LANES)
    count = width // block // parts
    offset = (chunk * parts + part) * count
    whole = lambda i: (0, 0)
    place = lambda i: (0, offset + i)
    aliased = prior is not None
    operands = [x, cot, b, c, gram, low, src]
    in_specs = [
        pl.BlockSpec((length, block), place),
        pl.BlockSpec((length, block), place),
        pl.BlockSpec((length, state), whole),
        pl.BlockSpec((length, state), whole),
        pl.BlockSpec((length, length // 2), whole),
        pl.BlockSpec((length, LANES), whole),
        pl.BlockSpec((heads, length), whole),
    ]
    aliases = {}
    if aliased:
        aliases = {len(operands): 0, len(operands) + 1: 1}
        operands += list(prior)
        in_specs += [pl.BlockSpec(memory_space=pl.ANY)] * 2
    kernel = functools.partial(inner_kernel, head_width, part * count * block // LANES, aliased)
    return pl.pallas_call(
        kernel,
        grid=(count,),
        in_specs=in_specs,
        out_specs=[
            pl.BlockSpec((length, block), place),
            pl.BlockSpec((length, block), place),
            pl.BlockSpec((length, state), whole),
            pl.BlockSpec((length, state), whole),
        ],
        out_shape=[
            jax.ShapeDtypeStruct(x.shape, bf16),
            jax.ShapeDtypeStruct(x.shape, bf16),
            jax.ShapeDtypeStruct((length, state), f32),
            jax.ShapeDtypeStruct((length, state), f32),
        ],
        scratch_shapes=[
            pltpu.VMEM((length, length // 2), f32),
            pltpu.VMEM((block, length), bf16),
            pltpu.VMEM((length, length // 2), bf16),
            pltpu.VMEM((length, length // 2), bf16),
            pltpu.VMEM((length, length // 2), bf16),
        ],
        input_output_aliases=aliases,
        name="node_inner",
        cost_estimate=pl.CostEstimate(
            flops=24 * length * length * count * block,
            bytes_accessed=12 * length * count * block,
            transcendentals=length * length * heads // parts,
        ),
    )(*operands)


def rank_nodes(parents_ref, rank_ref, half):
    nodes = rank_ref.shape[0]

    def clear(n, carry):
        rank_ref[n] = 0
        return carry

    def mark(n, carry):
        up = parents_ref[n]

        @pl.when(jnp.logical_and(up >= 0, (up >= half) != (n >= half)))
        def _():
            rank_ref[up] = 1

        return carry

    def place(n, count):
        crosses = rank_ref[n]
        rank_ref[n] = jnp.where(crosses > 0, count, -1)
        return count + crosses

    lax.fori_loop(0, nodes, clear, 0)
    lax.fori_loop(0, nodes, mark, 0)
    lax.fori_loop(0, nodes, place, 0)


def widen(narrow, heads, head_width):
    count = narrow.shape[0]
    flat = jnp.concatenate([narrow[n, :1].astype(f32) for n in range(count)], axis=0)
    return mm(flat.astype(bf16), spread_matrix(LANES, heads * head_width, head_width))


def pack_kernel(heads, head_width, parents_ref, recv_ref, *refs):
    tiers, (decay_ref, slot_ref, chain_ref, rank_ref) = refs[:-4], refs[-4:]
    half = recv_ref.shape[0]
    width = heads * head_width
    base = lax.axis_index("node") // half * half
    rank_nodes(parents_ref, rank_ref, half)
    decay_ref[...] = widen(recv_ref[:, :, 2 * width :], heads, head_width)
    slot_ref[...] = jnp.zeros_like(slot_ref)
    chain_ref[...] = jnp.zeros_like(chain_ref)

    def inside(n):
        return jnp.logical_and(n >= base, n < base + half)

    def spot(n):
        return jnp.clip(n - base, 0, half - 1)

    def visit(m, carry):
        node = base + m
        flow = recv_ref[m, :, width : 2 * width].astype(f32)
        at = node
        live = jnp.bool_(True)
        for level in range(LEVELS):
            up = parents_ref[at]
            exists = jnp.logical_and(live, up >= 0)
            live = jnp.logical_and(exists, inside(up))
            away = jnp.logical_and(exists, jnp.logical_not(live))

            @pl.when(away)
            def _(flow=flow, up=up):
                slot = rank_ref[up]
                slot_ref[slot] = slot_ref[slot] + flow

            if level < LEVELS - 1:
                flow = flow * jnp.where(live, decay_ref[pl.ds(spot(up), 1)], 1.0)
            at = jnp.where(live, up, at)

        @pl.when(rank_ref[node] >= 0)
        def _():
            total = recv_ref[m, :, :width].astype(f32)
            factor = decay_ref[pl.ds(m, 1)]
            chain = recv_ref[m, :, 2 * width :].astype(f32)
            at = node
            live = jnp.bool_(True)
            for _ in range(LEVELS - 1):
                up = parents_ref[at]
                live = jnp.logical_and(jnp.logical_and(live, up >= 0), inside(up))
                where = spot(up)
                total = total + jnp.where(live, factor * recv_ref[where, :, :width].astype(f32), 0.0)
                factor = factor * jnp.where(live, decay_ref[pl.ds(where, 1)], 1.0)
                chain = chain * jnp.where(live, recv_ref[where, :, 2 * width :].astype(f32), 1.0)
                at = jnp.where(live, up, at)
            slot_ref[rank_ref[node]] = total
            chain_ref[rank_ref[node]] = chain

        return carry

    lax.fori_loop(0, half, visit, 0)
    at = 0
    for ref in tiers:
        spots = slice(at, at + ref.shape[0])
        ref[:, :, :width] = slot_ref[spots].astype(bf16)
        ref[:, :, width:] = chain_ref[spots].astype(bf16)
        at += ref.shape[0]


def slot_counts(nodes):
    most = nodes * LEVELS // (LEVELS + 1)
    spare = nodes // 8
    return nodes // 2 - spare, spare, most - nodes // 2


def pack_slots(parents, recv, nodes, heads, head_width):
    half, rows, _ = recv.shape
    width = heads * head_width
    counts = slot_counts(nodes)
    in_specs = [pl.BlockSpec(memory_space=pltpu.SMEM), pl.BlockSpec(memory_space=pltpu.VMEM)]
    kernel = functools.partial(pack_kernel, heads, head_width)
    operands = [parents, recv]
    return pl.pallas_call(
        kernel,
        in_specs=in_specs,
        out_specs=[pl.BlockSpec(memory_space=pltpu.VMEM)] * len(counts),
        out_shape=[
            jax.ShapeDtypeStruct((count, rows, width + LANES), bf16) for count in counts
        ],
        scratch_shapes=[
            pltpu.VMEM((half, width), f32),
            pltpu.VMEM((sum(counts), rows, width), f32),
            pltpu.VMEM((sum(counts), rows, LANES), f32),
            pltpu.SMEM((nodes,), jnp.int32),
        ],
        compiler_params=pltpu.CompilerParams(vmem_limit_bytes=VMEM_BYTES),
        name="pack_slots",
        cost_estimate=pl.CostEstimate(
            flops=20 * half * rows * width,
            bytes_accessed=8 * half * rows * width,
            transcendentals=0,
        ),
    )(*operands)


def join_kernel(heads, head_width, parents_ref, recv_ref, *refs):
    tiers = refs[:-6]
    out_ref, decay_ref, slot_ref, chain_ref, back_ref, rank_ref = refs[-6:]
    half = recv_ref.shape[0]
    width = heads * head_width
    base = lax.axis_index("node") // half * half
    rank_nodes(parents_ref, rank_ref, half)
    decay_ref[...] = widen(recv_ref[:, :, 2 * width :], heads, head_width)
    at = 0
    for ref in tiers:
        spots = slice(at, at + ref.shape[0])
        slot_ref[spots] = ref[:, :, :width]
        chain_ref[spots] = widen(ref[:, :, width:], heads, head_width)
        at += ref.shape[0]
    back_ref[...] = jnp.zeros_like(back_ref)

    def inside(n):
        return jnp.logical_and(n >= base, n < base + half)

    def climb(at, flow, start):
        factor = None
        live = jnp.bool_(True)
        for level in range(LEVELS):
            up = parents_ref[at]
            live = jnp.logical_and(live, up >= 0)
            near = jnp.logical_and(live, inside(up))
            far = jnp.logical_and(live, jnp.logical_not(near))
            where = jnp.clip(up - base, 0, half - 1)
            slot = jnp.where(far, rank_ref[jnp.maximum(up, 0)], 0)

            @pl.when(near)
            def _(flow=flow, where=where):
                back_ref[where] = back_ref[where] + flow

            if start is not None:
                value = jnp.where(near, recv_ref[where, :, :width], slot_ref[slot])
                value = jnp.where(live, value.astype(f32), 0.0)
                start = start + (value if factor is None else factor * value)
            if level < LEVELS - 1:
                step = jnp.where(near, decay_ref[pl.ds(where, 1)], chain_ref[pl.ds(slot, 1)])
                flow = flow * step
                factor = step if factor is None else factor * step
                top = jnp.maximum(up, 0)
                for _ in range(LEVELS - 1):
                    above = parents_ref[top]
                    more = jnp.logical_and(far, above >= 0)
                    more = jnp.logical_and(more, jnp.logical_not(inside(above)))
                    top = jnp.where(more, above, top)
                at = top
        return start

    def visit(m, carry):
        node = base + m
        seed = recv_ref[m, :, width : 2 * width].astype(f32)
        start = climb(node, seed, jnp.zeros(seed.shape, f32))
        out_ref[m, :, :width] = start.astype(bf16)

        @pl.when(rank_ref[node] >= 0)
        def _():
            extra = slot_ref[rank_ref[node]].astype(f32)
            back_ref[m] = back_ref[m] + extra
            climb(node, extra * decay_ref[pl.ds(m, 1)], None)

        return carry

    lax.fori_loop(0, half, visit, 0)
    out_ref[:, :, width:] = back_ref[...].astype(bf16)


def join_slots(parents, recv, tiers, nodes, heads, head_width):
    half, rows, _ = recv.shape
    width = heads * head_width
    in_specs = [pl.BlockSpec(memory_space=pltpu.SMEM)] + [
        pl.BlockSpec(memory_space=pltpu.VMEM)
    ] * (1 + len(tiers))
    kernel = functools.partial(join_kernel, heads, head_width)
    operands = [parents, recv, *tiers]
    slots = sum(v.shape[0] for v in tiers)
    return pl.pallas_call(
        kernel,
        in_specs=in_specs,
        out_specs=pl.BlockSpec(memory_space=pltpu.VMEM),
        out_shape=jax.ShapeDtypeStruct((half, rows, 2 * width), bf16),
        scratch_shapes=[
            pltpu.VMEM((half, width), f32),
            pltpu.VMEM((slots, rows, width), bf16),
            pltpu.VMEM((slots, width), f32),
            pltpu.VMEM((half, rows, width), f32),
            pltpu.SMEM((nodes,), jnp.int32),
        ],
        compiler_params=pltpu.CompilerParams(vmem_limit_bytes=VMEM_BYTES),
        name="join_slots",
        cost_estimate=pl.CostEstimate(
            flops=20 * half * rows * width,
            bytes_accessed=8 * half * rows * width,
            transcendentals=0,
        ),
    )(*operands)


def outer_kernel(heads, head_width, chunk, block, extras, final, *refs):
    given = 13 + 2 * extras
    sources = refs[:given]
    refs = refs[given:]
    if final:
        outs, owns, pieces = refs[2:4], refs[4:6], refs[6 : -(given + 5)]
        gc_ref, gb_ref = refs[-2:]
        refs = refs[-(given + 5) : -2]
    else:
        outs, (gc_ref, gb_ref) = refs[:2], refs[2:4]
        refs = refs[4:]
    held, results, sems = refs[:given], refs[given : given + 2], refs[-1]
    b_ref, c_ref, grow_ref, tail_ref, step_ref = held[:5]
    added = held[5 : 5 + 2 * extras]
    x_ref, cot_ref, inner_ref, grad_ref, start_ref, back_ref, early_ref, late_ref = held[-8:]
    width = heads * head_width
    count = width // block
    middle = x_ref.shape[0] // 2
    copies = Copies(sems)
    small = [copies.start(sources[n], held[n]) for n in range(5)]
    loads = []
    for i in range(count):
        lanes = pl.ds(i * block, block)
        over = pl.ds(width + i * block, block)
        column = pl.ds(chunk * width + i * block, block)
        spots = (column,) * 4 + (lanes, over) * 2
        loads.append(
            [
                copies.start(source.at[:, spot], ref.at[:, lanes])
                for source, spot, ref in zip(sources[-8:], spots, held[-8:])
            ]
        )
    sums = [copies.start(sources[5 + n], ref) for n, ref in enumerate(added)]
    wait_all(small)
    stores = []
    ready = []
    for i in range(count):
        here = pl.ds(i * block, block)
        column = pl.ds(chunk * width + i * block, block)
        wait_all(loads[i])
        spread = spread_matrix(LANES, block, head_width, i * block)
        grow_wide = mm(grow_ref[...], spread)
        tail_wide = mm(tail_ref[...], spread)
        early_step, late_step = half_steps(step_ref, spread)
        start = start_ref[:, here]
        back = back_ref[:, here]
        after = (early_step * start.astype(f32) + early_ref[:, here].astype(f32)).astype(bf16)
        before = (late_step * back.astype(f32) + late_ref[:, here].astype(f32)).astype(bf16)
        for n, part in enumerate((slice(0, middle), slice(middle, 2 * middle))):
            grow = grow_wide[part]
            tail = tail_wide[part]
            begin = (start, after)[n]
            end = (before, back)[n]
            carried = grow * mm(c_ref[part], begin)
            results[0][part, here] = (inner_ref[part, here].astype(f32) + carried).astype(bf16)
            carried = tail * mm(b_ref[part], end)
            results[1][part, here] = (grad_ref[part, here].astype(f32) + carried).astype(bf16)
            gc = mm(grow.astype(bf16) * cot_ref[part, here], begin, NT)
            gb = mm(tail.astype(bf16) * x_ref[part, here], end, NT)
            if i == 0:
                gc_ref[part] = gc
                gb_ref[part] = gb
            else:
                gc_ref[part] += gc
                gb_ref[part] += gb
        stores += [copies.start(*pair) for pair in ready]
        ready = [
            (result.at[:, here], out.at[:, column]) for result, out in zip(results, outs)
        ]
    wait_all(sums)
    gc_ref[...] += sum(ref[...] for ref in added[:extras])
    gb_ref[...] += sum(ref[...] for ref in added[extras:])
    stores += [copies.start(*pair) for pair in ready]
    if final:
        size = len(pieces) + 1
        me = lax.axis_index("head")
        rows = owns[0].shape[0]
        for shift in range(size):
            at = pl.multiple_of(lax.rem(me + shift, size) * rows, rows)
            for n, ref in enumerate((gb_ref, gc_ref)):
                if shift == 0:
                    owns[n][...] = ref[pl.ds(at, rows)]
                else:
                    pieces[shift - 1][n] = ref[pl.ds(at, rows)].astype(bf16)
    wait_all(stores)


def node_outer(
    x, cot, b, c, grow, tail, states, keep, steps, inner, grad, found, prior, chunk, heads, head_width
):
    length, state = b.shape
    width = heads * head_width
    block = min(width, 4 * LANES)
    count = width // block
    final = prior is not None
    small = [b, c, grow, tail, steps] + [v[1] for v in found] + [v[0] for v in found]
    operands = small + [x, cot, inner, grad, states, states, keep, keep]
    given = len(operands)
    anywhere = pl.BlockSpec(memory_space=pl.ANY)
    local = pl.BlockSpec(memory_space=pltpu.VMEM)
    out_specs = [anywhere] * 2
    out_shape = [jax.ShapeDtypeStruct(x.shape, bf16)] * 2
    scratch = [pltpu.VMEM(v.shape, v.dtype) for v in small]
    scratch += [pltpu.VMEM((length, width), bf16)] * 4 + [pltpu.VMEM((state, width), bf16)] * 4
    scratch += [pltpu.VMEM((length, width), bf16)] * 2
    scratch.append(pltpu.SemaphoreType.DMA((len(small) + 10 * count,)))
    aliases = {}
    if final:
        aliases = {given: 0, given + 1: 1}
        operands += list(prior)
        size = lax.axis_size("head")
        kept = (2, length // size, state)
        out_specs += [local] * (size + 1)
        out_shape += [jax.ShapeDtypeStruct(kept[1:], f32)] * 2
        out_shape += [jax.ShapeDtypeStruct(kept, bf16)] * (size - 1)
        scratch += [pltpu.VMEM((length, state), f32)] * 2
    else:
        out_specs += [local] * 2
        out_shape += [jax.ShapeDtypeStruct((length, state), f32)] * 2
    return pl.pallas_call(
        functools.partial(outer_kernel, heads, head_width, chunk, block, len(found), final),
        in_specs=[anywhere] * len(operands),
        out_specs=out_specs,
        out_shape=out_shape,
        scratch_shapes=scratch,
        input_output_aliases=aliases,
        name="node_outer",
        cost_estimate=pl.CostEstimate(
            flops=8 * length * state * width,
            bytes_accessed=14 * length * width,
            transcendentals=0,
        ),
    )(*operands)


def scatter_sum(owns, pieces):
    size = lax.axis_size("head")
    for shift, piece in enumerate(pieces, 1):
        pairs = [(i, (i + shift) % size) for i in range(size)]
        moved = lax.ppermute(piece, "head", pairs).astype(f32)
        owns = [own + moved[n] for n, own in enumerate(owns)]
    return owns


def one_device(inputs, b_matrix, c_matrix, step_size, decay_rate, parents, cotangent):
    state = b_matrix.shape[1]
    head_count = step_size.shape[0]
    head_width = inputs.shape[1] // head_count
    nodes = lax.axis_size("node")
    heads = head_count // CHUNKS
    half = nodes // 2
    rate = decay_rate[None, :]
    groups = [list(range(half)), list(range(half, nodes))]
    across = [(n, (n + half) % nodes) for n in range(nodes)]

    def swap(v):
        return lax.all_to_all(
            v.reshape(half, state // half, v.shape[-1]),
            "node",
            split_axis=0,
            concat_axis=0,
            tiled=True,
            axis_index_groups=groups,
        )

    def cross(v):
        return lax.ppermute(v, "node", across)

    places = jnp.arange(nodes)
    child = jnp.logical_and(
        parents[:, None] == places[None, :],
        (places[:, None] < half) != (places[None, :] < half),
    )
    crossing = jnp.sum(jnp.any(child, axis=0).astype(jnp.int32))
    always, spare, _ = slot_counts(nodes)
    crowded = (crossing > always).astype(jnp.int32) + (crossing > always + spare)

    shared = (inputs, cotangent, b_matrix, c_matrix)
    sizes = (heads, head_width)
    made = []
    for k in range(CHUNKS):
        made.append(node_states(*shared, step_size, rate, k, *sizes))
    received = [swap(made[k][0]) for k in range(CHUNKS)]
    found = []
    prior = None
    for k in range(CHUNKS):
        for part in range(PARTS):
            *prior, gc, gb = node_inner(
                *shared, made[-1][5], made[k][1], made[k][2], prior, k, part, PARTS, *sizes
            )
            found.append((gb, gc))
    inner = prior
    packed = []
    for k in range(CHUNKS):
        main, *more = pack_slots(parents, received[k], nodes, *sizes)
        held = pltpu.with_memory_space_constraint(main, pltpu.HBM)
        packed.append((cross(held), more))
    others = lax.switch(
        crowded,
        (
            lambda vs: vs,
            lambda vs: [(cross(v[0]), v[1]) for v in vs],
            lambda vs: [(cross(v[0]), cross(v[1])) for v in vs],
        ),
        [tuple(p[1]) for p in packed],
    )
    states = []
    for k in range(CHUNKS):
        tiers = (packed[k][0], *others[k])
        joined = join_slots(parents, received[k], tiers, nodes, *sizes)
        states.append(swap(joined).reshape(state, -1))
    prior = None
    for k in range(CHUNKS):
        result = node_outer(
            *shared, *made[k][3:5], states[k], *made[k][6:8], *inner, found, prior, k, *sizes
        )
        prior = result[:2]
        if k == 0:
            found = [(result[3], result[2])]
    grads = scatter_sum(result[2:4], result[4:])
    return prior[0], prior[1], grads[0], grads[1]


def solution(mesh):
    return jax.shard_map(
        one_device,
        mesh=mesh,
        in_specs=(
            P("node", "head"),
            P("node", None),
            P("node", None),
            P("head", "node"),
            P("head"),
            P(),
            P("node", "head"),
        ),
        out_specs=(
            P("node", "head"),
            P("node", "head"),
            P(("node", "head"), None),
            P(("node", "head"), None),
        ),
        check_vma=False,
    )
```

```python
import functools
import math

import jax
import jax.numpy as jnp
from jax import lax
from jax.experimental import pallas as pl
from jax.experimental.pallas import tpu as pltpu
from jax.sharding import PartitionSpec as P


LEVELS = 3
VMEM_BYTES = 24 << 20
LANES = 128
SUBLANES = 8
CHUNKS = 2
PARTS = 2

LOG2E = 1.0 / math.log(2.0)

f32 = jnp.float32
bf16 = jnp.bfloat16
NN = (((1,), (0,)), ((), ()))
NT = (((1,), (1,)), ((), ()))


def mm(a, b, dims=NN):
    return lax.dot_general(a, b, dims, preferred_element_type=f32)


def split_two(v):
    high = v.astype(bf16)
    return high, (v - high.astype(f32)).astype(bf16)


def spread_matrix(rows, width, head_width, offset=0):
    row = lax.broadcasted_iota(jnp.int32, (rows, width), 0)
    lane = (lax.broadcasted_iota(jnp.int32, (rows, width), 1) + offset) // head_width
    return (row == lane).astype(bf16)


def head_lanes(columns, first, head_width):
    lane = lax.broadcasted_iota(jnp.int32, columns.shape, 1) // head_width + first
    return jnp.take_along_axis(columns, lane, axis=1)


def pad_lanes(v):
    gap = LANES - v.shape[0]
    if gap:
        v = jnp.concatenate([v, jnp.zeros((gap, v.shape[1]), v.dtype)], axis=0)
    return v.T


def half_steps(step_ref, spread):
    steps = mm(step_ref[...], spread)
    return steps[:1], steps[SUBLANES : SUBLANES + 1]


class Copies:
    def __init__(self, sems):
        self.sems = sems
        self.made = []

    def start(self, source, target):
        copy = pltpu.make_async_copy(source, target, self.sems.at[len(self.made)])
        copy.start()
        self.made.append(copy)
        return copy


def wait_all(copies):
    for copy in copies:
        copy.wait()


def states_kernel(heads, head_width, chunk, block, *refs):
    x_hbm, cot_hbm, b_hbm, c_hbm, step_hbm, rate_hbm = refs[:6]
    outs = refs[6:14]
    x_ref, cot_ref, b_ref, c_ref, step_ref, rate_ref = refs[14:20]
    send_ref, low_ref, src_ref, grow_ref, tail_ref, gram_ref, keep_ref, steps_ref = refs[20:28]
    sems = refs[28]
    length = step_ref.shape[1]
    middle = length // 2
    width = heads * head_width
    count = width // block
    copies = Copies(sems)
    first_in = [
        copies.start(step_hbm.at[pl.ds(chunk * heads, heads)], step_ref),
        copies.start(rate_hbm, rate_ref),
    ]
    later_in = [copies.start(b_hbm, b_ref), copies.start(c_hbm, c_ref)]
    loads = []
    for i in range(count):
        lanes = pl.ds(i * block, block)
        there = pl.ds(chunk * width + i * block, block)
        loads.append(
            [
                copies.start(x_hbm.at[:, there], x_ref.at[:, lanes]),
                copies.start(cot_hbm.at[:, there], cot_ref.at[:, lanes]),
            ]
        )
    wait_all(first_in)
    step = step_ref[...]
    rates = jnp.broadcast_to(rate_ref[...], (LANES, rate_ref.shape[1])).T
    terms = -step * rates[chunk * heads : (chunk + 1) * heads, :1]
    row = lax.broadcasted_iota(jnp.int32, (length, length), 0)
    col = lax.broadcasted_iota(jnp.int32, (length, length), 1)
    upper = (row <= col).astype(bf16)
    first = terms.astype(bf16)
    rest = terms - first.astype(f32)
    second, third = split_two(rest)
    cumulative = mm(third, upper) + mm(second, upper) + mm(first, upper)
    last = cumulative[:, length - 1 :]
    mid = cumulative[:, middle - 1 : middle]
    late = lax.broadcasted_iota(jnp.int32, cumulative.shape, 1) >= middle
    low_ref[...] = pad_lanes(cumulative * LOG2E)
    src_ref[...] = (cumulative - jnp.log(step)) * LOG2E
    grow_ref[...] = pad_lanes(jnp.exp(cumulative - jnp.where(late, mid, 0.0))).astype(bf16)
    tail = jnp.exp(jnp.where(late, last, mid) - cumulative) * step
    tail_ref[...] = pad_lanes(tail).astype(bf16)
    total = jnp.exp(jnp.broadcast_to(last, (heads, send_ref.shape[0])))
    send_ref[:, 2 * width :] = pad_lanes(total).astype(bf16)
    each = (heads, SUBLANES)
    steps = [jnp.broadcast_to(mid, each), jnp.broadcast_to(last - mid, each)]
    steps_ref[...] = pad_lanes(jnp.exp(jnp.concatenate(steps, axis=1))).astype(bf16)
    wait_all(later_in)
    b_turned = b_ref[...].T
    c_turned = c_ref[...].T
    small = (1, 2, 3, 4, 7)
    if chunk == CHUNKS - 1:
        small = (1, 2, 3, 4, 5, 7)
        for rows in (slice(0, middle), slice(middle, length)):
            gram_ref[rows] = mm(c_ref[rows], b_ref[rows], NT).astype(bf16)
    made = (send_ref, low_ref, src_ref, grow_ref, tail_ref, gram_ref, keep_ref, steps_ref)
    stores = []
    ready = [(made[n], outs[n]) for n in small]
    ready.append((send_ref.at[:, pl.ds(2 * width, LANES)], outs[0].at[:, pl.ds(2 * width, LANES)]))
    for i in range(count):
        here = pl.ds(i * block, block)
        there = pl.ds(i * block + width, block)
        wait_all(loads[i])
        spread = spread_matrix(LANES, block, head_width, i * block)
        tailed = mm(tail_ref[...], spread).astype(bf16) * x_ref[:, here]
        emitted = mm(grow_ref[...], spread).astype(bf16) * cot_ref[:, here]
        early_step, late_step = half_steps(steps_ref, spread)
        early_state = mm(b_turned[:, :middle], tailed[:middle])
        late_state = mm(b_turned[:, middle:], tailed[middle:])
        early_seed = mm(c_turned[:, :middle], emitted[:middle])
        late_seed = mm(c_turned[:, middle:], emitted[middle:])
        send_ref[:, here] = (late_step * early_state + late_state).astype(bf16)
        send_ref[:, there] = (early_seed + early_step * late_seed).astype(bf16)
        keep_ref[:, here] = early_state.astype(bf16)
        keep_ref[:, there] = late_seed.astype(bf16)
        stores += [copies.start(*pair) for pair in ready]
        ready = [
            (ref.at[:, lanes], out.at[:, lanes])
            for ref, out in ((send_ref, outs[0]), (keep_ref, outs[6]))
            for lanes in (here, there)
        ]
    stores += [copies.start(*pair) for pair in ready]
    wait_all(stores)


def node_states(x, cot, b, c, step, rate, chunk, heads, head_width):
    length, state = b.shape
    width = heads * head_width
    block = min(width, 4 * LANES)
    count = width // block
    out_shape = [
        jax.ShapeDtypeStruct((state, 2 * width + LANES), bf16),
        jax.ShapeDtypeStruct((length, LANES), f32),
        jax.ShapeDtypeStruct((heads, length), f32),
        jax.ShapeDtypeStruct((length, LANES), bf16),
        jax.ShapeDtypeStruct((length, LANES), bf16),
        jax.ShapeDtypeStruct((length, length // 2), bf16),
        jax.ShapeDtypeStruct((state, 2 * width), bf16),
        jax.ShapeDtypeStruct((2 * SUBLANES, LANES), bf16),
    ]
    held = [(length, width)] * 2 + [b.shape] * 2
    scratch = [pltpu.VMEM(shape, bf16) for shape in held]
    scratch += [pltpu.VMEM((heads, length), f32), pltpu.VMEM(rate.shape, f32)]
    scratch += [pltpu.VMEM(v.shape, v.dtype) for v in out_shape]
    scratch.append(pltpu.SemaphoreType.DMA((11 + 6 * count,)))
    anywhere = pl.BlockSpec(memory_space=pl.ANY)
    return pl.pallas_call(
        functools.partial(states_kernel, heads, head_width, chunk, block),
        in_specs=[anywhere] * 6,
        out_specs=[anywhere] * len(out_shape),
        out_shape=out_shape,
        scratch_shapes=scratch,
        name="node_states",
        cost_estimate=pl.CostEstimate(
            flops=4 * length * state * width,
            bytes_accessed=4 * length * width + 8 * state * width,
            transcendentals=0,
        ),
    )(x, cot, b, c, step, rate)


def inner_kernel(
    head_width,
    first,
    aliased,
    x_ref,
    cot_ref,
    b_ref,
    c_ref,
    given_ref,
    low_ref,
    src_ref,
    *refs,
):
    if aliased:
        refs = refs[2:]
    out_ref, grad_ref, gc_ref, gb_ref, mixed_ref, turned_ref, wa_ref, wb_ref, gram_ref = refs
    length = x_ref.shape[0]
    index = pl.program_id(0)
    pack = LANES // head_width
    pairs = x_ref.shape[1] // LANES
    wide = length // 2
    blocks = wide // LANES
    weights = (wa_ref, wb_ref)

    @pl.when(index == 0)
    def _():
        gram_ref[...] = given_ref[...]
        mixed_ref[...] = jnp.zeros_like(mixed_ref)
        for ref in weights:
            ref[...] = jnp.zeros_like(ref)

    lane = lax.broadcasted_iota(jnp.int32, (1, LANES), 1) // head_width
    causal = lax.broadcasted_iota(jnp.int32, (LANES, LANES), 0) >= lax.broadcasted_iota(
        jnp.int32, (LANES, LANES), 1
    )
    halves = (slice(0, wide), slice(wide, length))
    xs = [x_ref[:, q * LANES : (q + 1) * LANES] for q in range(pairs)]
    turned_cots = [cot_ref[:, q * LANES : (q + 1) * LANES].T for q in range(pairs)]
    low = low_ref[...]

    def decays(h):
        q, a = h // pack, h % pack
        w = weights[h % 2]
        cot = cot_ref[:, q * LANES : (q + 1) * LANES]
        cot = jnp.where(lane == a, cot, jnp.zeros_like(cot))
        place = (first + index * pairs + q) * pack + a
        column = head_lanes(low, place, LANES)
        source = src_ref[pl.ds(place, 1), :]
        for part in halves:
            scores = mm(cot[part], xs[q][part], NT)
            for i in range(blocks):
                here = slice(i * LANES, (i + 1) * LANES)
                rows = slice(part.start + here.start, part.start + here.stop)
                for j in range(i + 1):
                    cols = slice(j * LANES, (j + 1) * LANES)
                    differ = column[rows] - source[:, part.start + cols.start : part.start + cols.stop]
                    if i == j:
                        differ = jnp.where(causal, differ, -jnp.inf)
                    decay = jnp.exp2(differ)
                    w[rows, cols] = decay.astype(bf16) * gram_ref[rows, cols]
                    mixed_ref[rows, cols] += decay * scores[here, cols]
                yield

    def products(h):
        q, a = h // pack, h % pack
        w = weights[h % 2]
        turned = turned_cots[q][a * head_width : (a + 1) * head_width]
        mine = slice(q * LANES + a * head_width, q * LANES + (a + 1) * head_width)
        own = slice(a * head_width, (a + 1) * head_width)
        for part in halves:
            out_ref[part, mine] = mm(w[part], xs[q][part])[:, own].astype(bf16)
            yield
            turned_ref[mine, part] = mm(turned[:, part], w[part]).astype(bf16)
            yield

    def finish(q):
        lanes = slice(q * LANES, (q + 1) * LANES)
        grad_ref[:, lanes] = turned_ref[lanes, :].T

    before = None
    for h in range(pairs * pack):
        for _ in decays(h):
            if before is not None:
                next(before, None)
        if before is not None:
            for _ in before:
                pass
            if h % pack == 0:
                finish(h // pack - 1)
        before = products(h)
    for _ in before:
        pass
    finish(pairs - 1)

    @pl.when(index == pl.num_programs(0) - 1)
    def _():
        for part in halves:
            mixed = mixed_ref[part].astype(bf16)
            gc_ref[part] = mm(mixed, b_ref[part])
            gb_ref[part] = mm(mixed.T, c_ref[part])


def node_inner(x, cot, b, c, gram, low, src, prior, chunk, part, parts, heads, head_width):
    length, state = b.shape
    width = heads * head_width
    block = min(width // parts, 4 * LANES)
    count = width // block // parts
    offset = (chunk * parts + part) * count
    whole = lambda i: (0, 0)
    place = lambda i: (0, offset + i)
    aliased = prior is not None
    operands = [x, cot, b, c, gram, low, src]
    in_specs = [
        pl.BlockSpec((length, block), place),
        pl.BlockSpec((length, block), place),
        pl.BlockSpec((length, state), whole),
        pl.BlockSpec((length, state), whole),
        pl.BlockSpec((length, length // 2), whole),
        pl.BlockSpec((length, LANES), whole),
        pl.BlockSpec((heads, length), whole),
    ]
    aliases = {}
    if aliased:
        aliases = {len(operands): 0, len(operands) + 1: 1}
        operands += list(prior)
        in_specs += [pl.BlockSpec(memory_space=pl.ANY)] * 2
    kernel = functools.partial(inner_kernel, head_width, part * count * block // LANES, aliased)
    return pl.pallas_call(
        kernel,
        grid=(count,),
        in_specs=in_specs,
        out_specs=[
            pl.BlockSpec((length, block), place),
            pl.BlockSpec((length, block), place),
            pl.BlockSpec((length, state), whole),
            pl.BlockSpec((length, state), whole),
        ],
        out_shape=[
            jax.ShapeDtypeStruct(x.shape, bf16),
            jax.ShapeDtypeStruct(x.shape, bf16),
            jax.ShapeDtypeStruct((length, state), f32),
            jax.ShapeDtypeStruct((length, state), f32),
        ],
        scratch_shapes=[
            pltpu.VMEM((length, length // 2), f32),
            pltpu.VMEM((block, length), bf16),
            pltpu.VMEM((length, length // 2), bf16),
            pltpu.VMEM((length, length // 2), bf16),
            pltpu.VMEM((length, length // 2), bf16),
        ],
        input_output_aliases=aliases,
        name="node_inner",
        cost_estimate=pl.CostEstimate(
            flops=24 * length * length * count * block,
            bytes_accessed=12 * length * count * block,
            transcendentals=length * length * heads // parts,
        ),
    )(*operands)


def rank_nodes(parents_ref, rank_ref, half):
    nodes = rank_ref.shape[0]

    def clear(n, carry):
        rank_ref[n] = 0
        return carry

    def mark(n, carry):
        up = parents_ref[n]

        @pl.when(jnp.logical_and(up >= 0, (up >= half) != (n >= half)))
        def _():
            rank_ref[up] = 1

        return carry

    def place(n, count):
        crosses = rank_ref[n]
        rank_ref[n] = jnp.where(crosses > 0, count, -1)
        return count + crosses

    lax.fori_loop(0, nodes, clear, 0)
    lax.fori_loop(0, nodes, mark, 0)
    lax.fori_loop(0, nodes, place, 0)


def widen(narrow, heads, head_width):
    count = narrow.shape[0]
    flat = jnp.concatenate([narrow[n, :1].astype(f32) for n in range(count)], axis=0)
    return mm(flat.astype(bf16), spread_matrix(LANES, heads * head_width, head_width))


def pack_kernel(heads, head_width, parents_ref, recv_ref, *refs):
    tiers, (decay_ref, slot_ref, chain_ref, rank_ref) = refs[:-4], refs[-4:]
    half = recv_ref.shape[0]
    width = heads * head_width
    base = lax.axis_index("node") // half * half
    rank_nodes(parents_ref, rank_ref, half)
    decay_ref[...] = widen(recv_ref[:, :, 2 * width :], heads, head_width)
    slot_ref[...] = jnp.zeros_like(slot_ref)
    chain_ref[...] = jnp.zeros_like(chain_ref)

    def inside(n):
        return jnp.logical_and(n >= base, n < base + half)

    def spot(n):
        return jnp.clip(n - base, 0, half - 1)

    def visit(m, carry):
        node = base + m
        flow = recv_ref[m, :, width : 2 * width].astype(f32)
        at = node
        live = jnp.bool_(True)
        for level in range(LEVELS):
            up = parents_ref[at]
            exists = jnp.logical_and(live, up >= 0)
            live = jnp.logical_and(exists, inside(up))
            away = jnp.logical_and(exists, jnp.logical_not(live))

            @pl.when(away)
            def _(flow=flow, up=up):
                slot = rank_ref[up]
                slot_ref[slot] = slot_ref[slot] + flow

            if level < LEVELS - 1:
                flow = flow * jnp.where(live, decay_ref[pl.ds(spot(up), 1)], 1.0)
            at = jnp.where(live, up, at)

        @pl.when(rank_ref[node] >= 0)
        def _():
            total = recv_ref[m, :, :width].astype(f32)
            factor = decay_ref[pl.ds(m, 1)]
            chain = recv_ref[m, :, 2 * width :].astype(f32)
            at = node
            live = jnp.bool_(True)
            for _ in range(LEVELS - 1):
                up = parents_ref[at]
                live = jnp.logical_and(jnp.logical_and(live, up >= 0), inside(up))
                where = spot(up)
                total = total + jnp.where(live, factor * recv_ref[where, :, :width].astype(f32), 0.0)
                factor = factor * jnp.where(live, decay_ref[pl.ds(where, 1)], 1.0)
                chain = chain * jnp.where(live, recv_ref[where, :, 2 * width :].astype(f32), 1.0)
                at = jnp.where(live, up, at)
            slot_ref[rank_ref[node]] = total
            chain_ref[rank_ref[node]] = chain

        return carry

    lax.fori_loop(0, half, visit, 0)
    at = 0
    for ref in tiers:
        spots = slice(at, at + ref.shape[0])
        ref[:, :, :width] = slot_ref[spots].astype(bf16)
        ref[:, :, width:] = chain_ref[spots].astype(bf16)
        at += ref.shape[0]


def slot_counts(nodes):
    most = nodes * LEVELS // (LEVELS + 1)
    spare = nodes // 8
    return nodes // 2 - spare, spare, most - nodes // 2


def pack_slots(parents, recv, nodes, heads, head_width):
    half, rows, _ = recv.shape
    width = heads * head_width
    counts = slot_counts(nodes)
    in_specs = [pl.BlockSpec(memory_space=pltpu.SMEM), pl.BlockSpec(memory_space=pltpu.VMEM)]
    kernel = functools.partial(pack_kernel, heads, head_width)
    operands = [parents, recv]
    return pl.pallas_call(
        kernel,
        in_specs=in_specs,
        out_specs=[pl.BlockSpec(memory_space=pltpu.VMEM)] * len(counts),
        out_shape=[
            jax.ShapeDtypeStruct((count, rows, width + LANES), bf16) for count in counts
        ],
        scratch_shapes=[
            pltpu.VMEM((half, width), f32),
            pltpu.VMEM((sum(counts), rows, width), f32),
            pltpu.VMEM((sum(counts), rows, LANES), f32),
            pltpu.SMEM((nodes,), jnp.int32),
        ],
        compiler_params=pltpu.CompilerParams(vmem_limit_bytes=VMEM_BYTES),
        name="pack_slots",
        cost_estimate=pl.CostEstimate(
            flops=20 * half * rows * width,
            bytes_accessed=8 * half * rows * width,
            transcendentals=0,
        ),
    )(*operands)


def join_kernel(heads, head_width, parents_ref, recv_ref, *refs):
    tiers = refs[:-6]
    out_ref, decay_ref, slot_ref, chain_ref, back_ref, rank_ref = refs[-6:]
    half = recv_ref.shape[0]
    width = heads * head_width
    base = lax.axis_index("node") // half * half
    rank_nodes(parents_ref, rank_ref, half)
    decay_ref[...] = widen(recv_ref[:, :, 2 * width :], heads, head_width)
    at = 0
    for ref in tiers:
        spots = slice(at, at + ref.shape[0])
        slot_ref[spots] = ref[:, :, :width]
        chain_ref[spots] = widen(ref[:, :, width:], heads, head_width)
        at += ref.shape[0]
    back_ref[...] = jnp.zeros_like(back_ref)

    def inside(n):
        return jnp.logical_and(n >= base, n < base + half)

    def climb(at, flow, start):
        factor = None
        live = jnp.bool_(True)
        for level in range(LEVELS):
            up = parents_ref[at]
            live = jnp.logical_and(live, up >= 0)
            near = jnp.logical_and(live, inside(up))
            far = jnp.logical_and(live, jnp.logical_not(near))
            where = jnp.clip(up - base, 0, half - 1)
            slot = jnp.where(far, rank_ref[jnp.maximum(up, 0)], 0)

            @pl.when(near)
            def _(flow=flow, where=where):
                back_ref[where] = back_ref[where] + flow

            if start is not None:
                value = jnp.where(near, recv_ref[where, :, :width], slot_ref[slot])
                value = jnp.where(live, value.astype(f32), 0.0)
                start = start + (value if factor is None else factor * value)
            if level < LEVELS - 1:
                step = jnp.where(near, decay_ref[pl.ds(where, 1)], chain_ref[pl.ds(slot, 1)])
                flow = flow * step
                factor = step if factor is None else factor * step
                top = jnp.maximum(up, 0)
                for _ in range(LEVELS - 1):
                    above = parents_ref[top]
                    more = jnp.logical_and(far, above >= 0)
                    more = jnp.logical_and(more, jnp.logical_not(inside(above)))
                    top = jnp.where(more, above, top)
                at = top
        return start

    def visit(m, carry):
        node = base + m
        seed = recv_ref[m, :, width : 2 * width].astype(f32)
        start = climb(node, seed, jnp.zeros(seed.shape, f32))
        out_ref[m, :, :width] = start.astype(bf16)

        @pl.when(rank_ref[node] >= 0)
        def _():
            extra = slot_ref[rank_ref[node]].astype(f32)
            back_ref[m] = back_ref[m] + extra
            climb(node, extra * decay_ref[pl.ds(m, 1)], None)

        return carry

    lax.fori_loop(0, half, visit, 0)
    out_ref[:, :, width:] = back_ref[...].astype(bf16)


def join_slots(parents, recv, tiers, nodes, heads, head_width):
    half, rows, _ = recv.shape
    width = heads * head_width
    in_specs = [pl.BlockSpec(memory_space=pltpu.SMEM)] + [
        pl.BlockSpec(memory_space=pltpu.VMEM)
    ] * (1 + len(tiers))
    kernel = functools.partial(join_kernel, heads, head_width)
    operands = [parents, recv, *tiers]
    slots = sum(v.shape[0] for v in tiers)
    return pl.pallas_call(
        kernel,
        in_specs=in_specs,
        out_specs=pl.BlockSpec(memory_space=pltpu.VMEM),
        out_shape=jax.ShapeDtypeStruct((half, rows, 2 * width), bf16),
        scratch_shapes=[
            pltpu.VMEM((half, width), f32),
            pltpu.VMEM((slots, rows, width), bf16),
            pltpu.VMEM((slots, width), f32),
            pltpu.VMEM((half, rows, width), f32),
            pltpu.SMEM((nodes,), jnp.int32),
        ],
        compiler_params=pltpu.CompilerParams(vmem_limit_bytes=VMEM_BYTES),
        name="join_slots",
        cost_estimate=pl.CostEstimate(
            flops=20 * half * rows * width,
            bytes_accessed=8 * half * rows * width,
            transcendentals=0,
        ),
    )(*operands)


def outer_kernel(heads, head_width, chunk, block, extras, final, *refs):
    given = 13 + 2 * extras
    sources = refs[:given]
    refs = refs[given:]
    if final:
        outs, owns, pieces = refs[2:4], refs[4:6], refs[6 : -(given + 5)]
        gc_ref, gb_ref = refs[-2:]
        refs = refs[-(given + 5) : -2]
    else:
        outs, (gc_ref, gb_ref) = refs[:2], refs[2:4]
        refs = refs[4:]
    held, results, sems = refs[:given], refs[given : given + 2], refs[-1]
    b_ref, c_ref, grow_ref, tail_ref, step_ref = held[:5]
    added = held[5 : 5 + 2 * extras]
    x_ref, cot_ref, inner_ref, grad_ref, start_ref, back_ref, early_ref, late_ref = held[-8:]
    width = heads * head_width
    count = width // block
    middle = x_ref.shape[0] // 2
    copies = Copies(sems)
    small = [copies.start(sources[n], held[n]) for n in range(5)]
    loads = []
    for i in range(count):
        lanes = pl.ds(i * block, block)
        over = pl.ds(width + i * block, block)
        column = pl.ds(chunk * width + i * block, block)
        spots = (column,) * 4 + (lanes, over) * 2
        loads.append(
            [
                copies.start(source.at[:, spot], ref.at[:, lanes])
                for source, spot, ref in zip(sources[-8:], spots, held[-8:])
            ]
        )
    sums = [copies.start(sources[5 + n], ref) for n, ref in enumerate(added)]
    wait_all(small)
    stores = []
    ready = []
    for i in range(count):
        here = pl.ds(i * block, block)
        column = pl.ds(chunk * width + i * block, block)
        wait_all(loads[i])
        spread = spread_matrix(LANES, block, head_width, i * block)
        grow_wide = mm(grow_ref[...], spread)
        tail_wide = mm(tail_ref[...], spread)
        early_step, late_step = half_steps(step_ref, spread)
        start = start_ref[:, here]
        back = back_ref[:, here]
        after = (early_step * start.astype(f32) + early_ref[:, here].astype(f32)).astype(bf16)
        before = (late_step * back.astype(f32) + late_ref[:, here].astype(f32)).astype(bf16)
        for n, part in enumerate((slice(0, middle), slice(middle, 2 * middle))):
            grow = grow_wide[part]
            tail = tail_wide[part]
            begin = (start, after)[n]
            end = (before, back)[n]
            carried = grow * mm(c_ref[part], begin)
            results[0][part, here] = (inner_ref[part, here].astype(f32) + carried).astype(bf16)
            carried = tail * mm(b_ref[part], end)
            results[1][part, here] = (grad_ref[part, here].astype(f32) + carried).astype(bf16)
            gc = mm(grow.astype(bf16) * cot_ref[part, here], begin, NT)
            gb = mm(tail.astype(bf16) * x_ref[part, here], end, NT)
            if i == 0:
                gc_ref[part] = gc
                gb_ref[part] = gb
            else:
                gc_ref[part] += gc
                gb_ref[part] += gb
        stores += [copies.start(*pair) for pair in ready]
        ready = [
            (result.at[:, here], out.at[:, column]) for result, out in zip(results, outs)
        ]
    wait_all(sums)
    gc_ref[...] += sum(ref[...] for ref in added[:extras])
    gb_ref[...] += sum(ref[...] for ref in added[extras:])
    stores += [copies.start(*pair) for pair in ready]
    if final:
        size = len(pieces) + 1
        me = lax.axis_index("head")
        rows = owns[0].shape[0]
        for shift in range(size):
            at = pl.multiple_of(lax.rem(me + shift, size) * rows, rows)
            for n, ref in enumerate((gb_ref, gc_ref)):
                if shift == 0:
                    owns[n][...] = ref[pl.ds(at, rows)]
                else:
                    pieces[shift - 1][n] = ref[pl.ds(at, rows)].astype(bf16)
    wait_all(stores)


def node_outer(
    x, cot, b, c, grow, tail, states, keep, steps, inner, grad, found, prior, chunk, heads, head_width
):
    length, state = b.shape
    width = heads * head_width
    block = min(width, 4 * LANES)
    count = width // block
    final = prior is not None
    small = [b, c, grow, tail, steps] + [v[1] for v in found] + [v[0] for v in found]
    operands = small + [x, cot, inner, grad, states, states, keep, keep]
    given = len(operands)
    anywhere = pl.BlockSpec(memory_space=pl.ANY)
    local = pl.BlockSpec(memory_space=pltpu.VMEM)
    out_specs = [anywhere] * 2
    out_shape = [jax.ShapeDtypeStruct(x.shape, bf16)] * 2
    scratch = [pltpu.VMEM(v.shape, v.dtype) for v in small]
    scratch += [pltpu.VMEM((length, width), bf16)] * 4 + [pltpu.VMEM((state, width), bf16)] * 4
    scratch += [pltpu.VMEM((length, width), bf16)] * 2
    scratch.append(pltpu.SemaphoreType.DMA((len(small) + 10 * count,)))
    aliases = {}
    if final:
        aliases = {given: 0, given + 1: 1}
        operands += list(prior)
        size = lax.axis_size("head")
        kept = (2, length // size, state)
        out_specs += [local] * (size + 1)
        out_shape += [jax.ShapeDtypeStruct(kept[1:], f32)] * 2
        out_shape += [jax.ShapeDtypeStruct(kept, bf16)] * (size - 1)
        scratch += [pltpu.VMEM((length, state), f32)] * 2
    else:
        out_specs += [local] * 2
        out_shape += [jax.ShapeDtypeStruct((length, state), f32)] * 2
    return pl.pallas_call(
        functools.partial(outer_kernel, heads, head_width, chunk, block, len(found), final),
        in_specs=[anywhere] * len(operands),
        out_specs=out_specs,
        out_shape=out_shape,
        scratch_shapes=scratch,
        input_output_aliases=aliases,
        name="node_outer",
        cost_estimate=pl.CostEstimate(
            flops=8 * length * state * width,
            bytes_accessed=14 * length * width,
            transcendentals=0,
        ),
    )(*operands)


def scatter_sum(owns, pieces):
    size = lax.axis_size("head")
    for shift, piece in enumerate(pieces, 1):
        pairs = [(i, (i + shift) % size) for i in range(size)]
        moved = lax.ppermute(piece, "head", pairs).astype(f32)
        owns = [own + moved[n] for n, own in enumerate(owns)]
    return owns


def one_device(inputs, b_matrix, c_matrix, step_size, decay_rate, parents, cotangent):
    state = b_matrix.shape[1]
    head_count = step_size.shape[0]
    head_width = inputs.shape[1] // head_count
    nodes = lax.axis_size("node")
    heads = head_count // CHUNKS
    half = nodes // 2
    rate = decay_rate[None, :]
    groups = [list(range(half)), list(range(half, nodes))]
    across = [(n, (n + half) % nodes) for n in range(nodes)]

    def swap(v):
        return lax.all_to_all(
            v.reshape(half, state // half, v.shape[-1]),
            "node",
            split_axis=0,
            concat_axis=0,
            tiled=True,
            axis_index_groups=groups,
        )

    def cross(v):
        return lax.ppermute(v, "node", across)

    places = jnp.arange(nodes)
    child = jnp.logical_and(
        parents[:, None] == places[None, :],
        (places[:, None] < half) != (places[None, :] < half),
    )
    crossing = jnp.sum(jnp.any(child, axis=0).astype(jnp.int32))
    always, spare, _ = slot_counts(nodes)
    crowded = (crossing > always).astype(jnp.int32) + (crossing > always + spare)

    shared = (inputs, cotangent, b_matrix, c_matrix)
    sizes = (heads, head_width)
    made = []
    for k in range(CHUNKS):
        made.append(node_states(*shared, step_size, rate, k, *sizes))
    received = [swap(made[k][0]) for k in range(CHUNKS)]
    found = []
    prior = None
    for k in range(CHUNKS):
        for part in range(PARTS):
            *prior, gc, gb = node_inner(
                *shared, made[-1][5], made[k][1], made[k][2], prior, k, part, PARTS, *sizes
            )
            found.append((gb, gc))
    inner = prior
    packed = []
    for k in range(CHUNKS):
        main, *more = pack_slots(parents, received[k], nodes, *sizes)
        packed.append((cross(main), more))
    others = lax.switch(
        crowded,
        (
            lambda vs: vs,
            lambda vs: [(cross(v[0]), v[1]) for v in vs],
            lambda vs: [(cross(v[0]), cross(v[1])) for v in vs],
        ),
        [tuple(p[1]) for p in packed],
    )
    states = []
    for k in range(CHUNKS):
        tiers = (packed[k][0], *others[k])
        joined = join_slots(parents, received[k], tiers, nodes, *sizes)
        states.append(swap(joined).reshape(state, -1))
    prior = None
    for k in range(CHUNKS):
        result = node_outer(
            *shared, *made[k][3:5], states[k], *made[k][6:8], *inner, found, prior, k, *sizes
        )
        prior = result[:2]
        if k == 0:
            found = [(result[3], result[2])]
    grads = scatter_sum(result[2:4], result[4:])
    return prior[0], prior[1], grads[0], grads[1]


def solution(mesh):
    return jax.shard_map(
        one_device,
        mesh=mesh,
        in_specs=(
            P("node", "head"),
            P("node", None),
            P("node", None),
            P("head", "node"),
            P("head"),
            P(),
            P("node", "head"),
        ),
        out_specs=(
            P("node", "head"),
            P("node", "head"),
            P(("node", "head"), None),
            P(("node", "head"), None),
        ),
        check_vma=False,
    )
```
